32 devices in a mesh: dp: 2 (over core), ctx: 4 (over z), tp: 4 (over y, x).
Axes of the slice: x: 2, y: 2, z: 4, core: 2. Of those that a mesh axis runs over, the one named last changes fastest.
Arguments:
- block_input: float32 [512, 2, 1024], P(('ctx', 'tp'), 'dp'), may hold values from -6 to 6
- input_gain: float32 [2, 1024], replicated, may hold values from 0.5 to 1.5
- query_weight: bfloat16 [2, 1024, 2048], P(None, None, 'tp'), may hold values from -0.1875 to 0.1875
- key_weight: bfloat16 [2, 1024, 1024], P(None, None, 'tp'), may hold values from -0.1875 to 0.1875
- value_weight: bfloat16 [2, 1024, 1024], P(None, None, 'tp'), may hold values from -0.1875 to 0.1875
- query_gain: float32 [2, 128], replicated, may hold values from 0.1 to 1.9
- key_gain: float32 [2, 128], replicated, may hold values from 0.1 to 1.9
- out_weight: bfloat16 [2, 2048, 1024], P(None, 'tp'), may hold values from -0.75 to 0.75
- post_gain: float32 [2, 1024], replicated, may hold values from 0.5 to 1.5
- gate_weight: bfloat16 [2, 1024, 3072], P(None, None, 'tp'), may hold values from -0.1875 to 0.1875
- up_weight: bfloat16 [2, 1024, 3072], P(None, None, 'tp'), may hold values from -0.1875 to 0.1875
- down_weight: bfloat16 [2, 3072, 1024], P(None, 'tp'), may hold values from -0.109375 to 0.109375
- grad_output: float32 [512, 2, 1024], P(('ctx', 'tp'), 'dp'), may hold values from -6 to 6
Outputs:
- output: float32 [512, 2, 1024], P(('ctx', 'tp'), 'dp')
- grad_input: float32 [512, 2, 1024], P(('ctx', 'tp'), 'dp')
- input_gain_grad: float32 [2, 1024], replicated
- query_weight_grad: float32 [2, 1024, 2048], P(None, ('dp', 'ctx'), 'tp')
- key_weight_grad: float32 [2, 1024, 1024], P(None, ('dp', 'ctx'), 'tp')
- value_weight_grad: float32 [2, 1024, 1024], P(None, ('dp', 'ctx'), 'tp')
- query_gain_grad: float32 [2, 128], replicated
- key_gain_grad: float32 [2, 128], replicated
- out_weight_grad: float32 [2, 2048, 1024], P(None, 'tp', ('dp', 'ctx'))
- post_gain_grad: float32 [2, 1024], replicated
- gate_weight_grad: float32 [2, 1024, 3072], P(None, ('dp', 'ctx'), 'tp')
- up_weight_grad: float32 [2, 1024, 3072], P(None, ('dp', 'ctx'), 'tp')
- down_weight_grad: float32 [2, 3072, 1024], P(None, 'tp', ('dp', 'ctx'))
The draws below stay inside these ranges and needn't reach their ends.
All inputs are finite; a program needn't handle non-finite values.
Results may differ from the reference program's by a relative error of at most 0.034.
Values may be sent and summed in bfloat16 or wider, within the bound.
A program may use at most 192 MiB of HBM per device.

```python
import jax
import jax.numpy as jnp
from jax import lax

D = 1024
HEADS = 16
KV_HEADS = 8
HEAD_DIM = 128
FF = 3072
LAYERS = 2
SEQS = 2
LEN = 512


def block_levels(own_key, extent, split, low, largest):
    def one(axis_at, shards_of):
        draws = jax.random.uniform(jax.random.fold_in(jax.random.fold_in(own_key, 6), axis_at), (shards_of,), jnp.float32, low / len(split), largest / len(split))
        return jnp.repeat(jnp.exp(draws), extent[axis_at] // shards_of).reshape((-1,) + (1,) * (len(extent) - axis_at - 1))

    level = one(*split[0])
    for cut in split[1:]:
        level = level * one(*cut)
    return level


def centred(key, dims, width, limit, cuts=(), held_as=jnp.bfloat16):
    loudness = block_levels(key, dims, cuts, -0.22, 0.18) if cuts else 1.0
    array = jax.random.normal(key, dims, jnp.float32) * width * loudness
    return jnp.minimum(jnp.maximum(array, -limit), limit).astype(held_as)


def setup_inputs(seed: int = 0) -> dict:
    streams_of = jax.random.split(jax.random.key(seed), 14)
    return {
        "block_input": centred(streams_of[0], (LEN, SEQS, D), 1.0, 6.0, ((0, 16), (1, 2)), jnp.float32),
        "input_gain": jnp.clip(1.0 + 0.1 * jax.random.normal(streams_of[1], (LAYERS, D), jnp.float32), 0.5, 1.5),
        "query_weight": centred(streams_of[2], (LAYERS, D, HEADS * HEAD_DIM), D ** -0.5, 0.1875, ((2, 4),)),
        "key_weight": centred(streams_of[3], (LAYERS, D, KV_HEADS * HEAD_DIM), D ** -0.5, 0.1875, ((2, 4),)),
        "value_weight": centred(streams_of[4], (LAYERS, D, KV_HEADS * HEAD_DIM), D ** -0.5, 0.1875, ((2, 4),)),
        "query_gain": jnp.clip(1.0 + 0.18 * jax.random.normal(streams_of[5], (LAYERS, HEAD_DIM), jnp.float32), 0.1, 1.9),
        "key_gain": jnp.clip(1.0 + 0.18 * jax.random.normal(streams_of[6], (LAYERS, HEAD_DIM), jnp.float32), 0.1, 1.9),
        "out_weight": centred(streams_of[7], (LAYERS, HEADS * HEAD_DIM, D), (HEADS * HEAD_DIM // 32) ** -0.5, 0.75, ((1, 4),)),
        "post_gain": jnp.clip(1.0 + 0.1 * jax.random.normal(streams_of[8], (LAYERS, D), jnp.float32), 0.5, 1.5),
        "gate_weight": centred(streams_of[9], (LAYERS, D, FF), D ** -0.5, 0.1875, ((2, 4),)),
        "up_weight": centred(streams_of[10], (LAYERS, D, FF), D ** -0.5, 0.1875, ((2, 4),)),
        "down_weight": centred(streams_of[11], (LAYERS, FF, D), FF ** -0.5, 0.109375, ((1, 4),)),
        "grad_output": centred(streams_of[12], (LEN, SEQS, D), 1.0, 6.0, ((0, 16), (1, 2)), jnp.float32),
    }


EPS = 1e-06
THETA = 1000000.0

def rounded(field):
    return lax.optimization_barrier(field.astype(jnp.bfloat16)).astype(jnp.float32)

def rms_forward(field, gain):
    inverse = lax.rsqrt(lax.optimization_barrier(jnp.mean(field * field, axis=-1, keepdims=True)) + EPS)
    normed = field * inverse
    return (normed * gain, normed, inverse)

def rms_backward(grad_out, normed, inverse, gain):
    leading = tuple(range(grad_out.ndim - 1))
    grad_gain = lax.optimization_barrier(jnp.sum(grad_out * normed, axis=leading))
    scaled = grad_out * gain
    grad_in = inverse * (scaled - normed * lax.optimization_barrier(jnp.mean(scaled * normed, axis=-1, keepdims=True)))
    return (grad_in, grad_gain)

def rope_tables(positions, head_dim):
    half = head_dim // 2
    frequency = THETA ** (-(2.0 * jnp.arange(half, dtype=jnp.float32)) / head_dim)
    angles = positions[:, None] * frequency[None, :]
    angles = jnp.concatenate([angles, angles], axis=-1)
    return (jnp.cos(angles)[:, None, None, :], jnp.sin(angles)[:, None, None, :])

def rotate(field, cosine, sine):
    half = field.shape[-1] // 2
    turned = jnp.concatenate([-field[..., half:], field[..., :half]], axis=-1)
    return field * cosine + turned * sine

def attend_forward(parts):
    query, keys, values = parts
    block = min(512, LEN)
    query_full = query.astype(jnp.float32)
    key_full = keys.astype(jnp.float32)
    value_full = values.astype(jnp.float32)
    key_rows = jnp.arange(LEN).astype(jnp.int32)
    score_scale = HEAD_DIM ** (-0.5)

    def one_block(index):
        start = (index * block).astype(jnp.int32)
        part = lax.dynamic_slice_in_dim(query_full, start, block, 0)
        scores = jnp.einsum('qkgd,tkd->kgqt', part, key_full) * score_scale
        rows = start + jnp.arange(block).astype(jnp.int32)
        scores = jnp.where(key_rows[None, :] <= rows[:, None], scores, -jnp.inf)
        highest = lax.optimization_barrier(jnp.max(scores, axis=-1))
        weights = jnp.exp(scores - highest[..., None])
        total = lax.optimization_barrier(jnp.sum(weights, axis=-1))
        mixed = jnp.einsum('kgqt,tkd->qkgd', rounded(weights), value_full)
        return (mixed / jnp.moveaxis(total, 2, 0)[..., None], highest + jnp.log(total))
    mixed, log_total = lax.map(one_block, jnp.arange(LEN // block).astype(jnp.int32))
    group_size = HEADS // KV_HEADS
    return (mixed.reshape(LEN, KV_HEADS, group_size, HEAD_DIM), jnp.moveaxis(log_total, 0, 2).reshape(KV_HEADS, group_size, LEN))

def attend_backward(parts):
    query, keys, values, heads, log_total, grad_heads = parts
    block = min(512, LEN)
    query_full = query.astype(jnp.float32)
    key_full = keys.astype(jnp.float32)
    value_full = values.astype(jnp.float32)
    grad_full = grad_heads.astype(jnp.float32)
    delta = lax.optimization_barrier(jnp.sum(grad_full * heads.astype(jnp.float32), axis=-1))
    key_rows = jnp.arange(LEN).astype(jnp.int32)
    score_scale = HEAD_DIM ** (-0.5)

    def one_block(carry, index):
        key_acc, value_acc = carry
        start = (index * block).astype(jnp.int32)
        part = lax.dynamic_slice_in_dim(query_full, start, block, 0)
        part_grad = lax.dynamic_slice_in_dim(grad_full, start, block, 0)
        part_lse = lax.dynamic_slice_in_dim(log_total, start, block, 2)
        part_delta = lax.dynamic_slice_in_dim(delta, start, block, 0)
        scores = jnp.einsum('qkgd,tkd->kgqt', part, key_full) * score_scale
        rows = start + jnp.arange(block).astype(jnp.int32)
        scores = jnp.where(key_rows[None, :] <= rows[:, None], scores, -jnp.inf)
        probs = jnp.exp(scores - part_lse[..., None])
        dprob = jnp.einsum('qkgd,tkd->kgqt', part_grad, value_full)
        dscore = rounded(probs * (dprob - jnp.moveaxis(part_delta, 0, 2)[..., None]))
        grad_query = jnp.einsum('kgqt,tkd->qkgd', dscore, key_full) * score_scale
        key_acc = key_acc + jnp.einsum('kgqt,qkgd->tkd', dscore, part) * score_scale
        value_acc = value_acc + jnp.einsum('kgqt,qkgd->tkd', rounded(probs), part_grad)
        return ((key_acc, value_acc), grad_query)
    zero_keys = jnp.zeros((LEN, KV_HEADS, HEAD_DIM), jnp.float32)
    (grad_keys, grad_values), grad_query = lax.scan(one_block, (zero_keys, zero_keys), jnp.arange(LEN // block).astype(jnp.int32))
    return (grad_query.reshape(LEN, KV_HEADS, HEADS // KV_HEADS, HEAD_DIM), grad_keys, grad_values)

def per_sequence(field):
    return jnp.moveaxis(field, 1, 0)

def reference(block_input, input_gain, query_weight, key_weight, value_weight, query_gain, key_gain, out_weight, post_gain, gate_weight, up_weight, down_weight, grad_output):
    group_size = HEADS // KV_HEADS
    rows_all = LEN * SEQS
    cosine, sine = rope_tables(jnp.arange(LEN).astype(jnp.float32), HEAD_DIM)
    hidden = block_input
    kept_all = []
    for index in range(LAYERS):
        normed_one, plain_one, inverse_one = rms_forward(hidden, input_gain[index])
        first_flat = normed_one.astype(jnp.bfloat16).reshape(rows_all, D)
        query = jnp.dot(first_flat, query_weight[index], preferred_element_type=jnp.float32).reshape(LEN, SEQS, HEADS, HEAD_DIM)
        keys = jnp.dot(first_flat, key_weight[index], preferred_element_type=jnp.float32).reshape(LEN, SEQS, KV_HEADS, HEAD_DIM)
        values = jnp.dot(first_flat, value_weight[index], preferred_element_type=jnp.float32).astype(jnp.bfloat16).reshape(LEN, SEQS, KV_HEADS, HEAD_DIM)
        query_normed, query_plain, query_inverse = rms_forward(query, query_gain[index])
        key_normed, key_plain, key_inverse = rms_forward(keys, key_gain[index])
        query_rot = rotate(query_normed, cosine, sine).astype(jnp.bfloat16).reshape(LEN, SEQS, KV_HEADS, group_size, HEAD_DIM)
        key_rot = rotate(key_normed, cosine, sine).astype(jnp.bfloat16)
        attended, log_total = lax.map(attend_forward, (per_sequence(query_rot), per_sequence(key_rot), per_sequence(values)))
        heads_bf = per_sequence(attended).reshape(LEN, SEQS, HEADS * HEAD_DIM).astype(jnp.bfloat16)
        heads_flat = heads_bf.reshape(rows_all, HEADS * HEAD_DIM)
        mixed = hidden + jnp.dot(heads_flat, out_weight[index], preferred_element_type=jnp.float32).reshape(LEN, SEQS, D)
        normed_two, plain_two, inverse_two = rms_forward(mixed, post_gain[index])
        second_flat = normed_two.astype(jnp.bfloat16).reshape(rows_all, D)
        gate = jnp.dot(second_flat, gate_weight[index], preferred_element_type=jnp.float32)
        upward = jnp.dot(second_flat, up_weight[index], preferred_element_type=jnp.float32)
        swish = (jax.nn.silu(gate) * upward).astype(jnp.bfloat16)
        hidden = mixed + jnp.dot(swish, down_weight[index], preferred_element_type=jnp.float32).reshape(LEN, SEQS, D)
        kept_all.append((plain_one, inverse_one, first_flat, query_plain, query_inverse, key_plain, key_inverse, query_rot, key_rot, values, log_total, heads_bf, plain_two, inverse_two, second_flat, gate, upward, swish))
    output = hidden
    grad_hidden = grad_output
    weight_parts = [None] * LAYERS
    gain_parts = [None] * LAYERS
    for index in reversed(range(LAYERS)):
        plain_one, inverse_one, first_flat, query_plain, query_inverse, key_plain, key_inverse, query_rot, key_rot, values, log_total, heads_bf, plain_two, inverse_two, second_flat, gate, upward, swish = kept_all[index]
        grad_rows = grad_hidden.astype(jnp.bfloat16).reshape(rows_all, D)
        grad_swish = jnp.dot(grad_rows, down_weight[index].T, preferred_element_type=jnp.float32)
        down_grad = jnp.dot(swish.T, grad_rows, preferred_element_type=jnp.float32)
        sigma = jax.nn.sigmoid(gate)
        grad_gate = (grad_swish * upward * (sigma * (1.0 + gate * (1.0 - sigma)))).astype(jnp.bfloat16)
        grad_up = (grad_swish * (gate * sigma)).astype(jnp.bfloat16)
        gate_grad = jnp.dot(second_flat.T, grad_gate, preferred_element_type=jnp.float32)
        up_grad = jnp.dot(second_flat.T, grad_up, preferred_element_type=jnp.float32)
        grad_second = jnp.dot(grad_gate, gate_weight[index].T, preferred_element_type=jnp.float32) + jnp.dot(grad_up, up_weight[index].T, preferred_element_type=jnp.float32)
        grad_norm_two, post_part = rms_backward(grad_second.reshape(LEN, SEQS, D), plain_two, inverse_two, post_gain[index])
        grad_mixed = grad_hidden + grad_norm_two
        mixed_rows = grad_mixed.astype(jnp.bfloat16).reshape(rows_all, D)
        grad_heads = jnp.dot(mixed_rows, out_weight[index].T, preferred_element_type=jnp.float32).astype(jnp.bfloat16)
        out_grad = jnp.dot(heads_bf.reshape(rows_all, HEADS * HEAD_DIM).T, mixed_rows, preferred_element_type=jnp.float32)
        grad_grouped = grad_heads.reshape(LEN, SEQS, KV_HEADS, group_size, HEAD_DIM)
        heads_grouped = heads_bf.reshape(LEN, SEQS, KV_HEADS, group_size, HEAD_DIM)
        grad_query, grad_keys, grad_values = lax.map(attend_backward, (per_sequence(query_rot), per_sequence(key_rot), per_sequence(values), per_sequence(heads_grouped), log_total, per_sequence(grad_grouped)))
        grad_query = rotate(per_sequence(grad_query).reshape(LEN, SEQS, HEADS, HEAD_DIM), cosine, -sine)
        grad_keys = rotate(per_sequence(grad_keys), cosine, -sine)
        grad_query, query_part = rms_backward(grad_query, query_plain, query_inverse, query_gain[index])
        grad_keys, key_part = rms_backward(grad_keys, key_plain, key_inverse, key_gain[index])
        query_bf = grad_query.astype(jnp.bfloat16).reshape(rows_all, HEADS * HEAD_DIM)
        key_bf = grad_keys.astype(jnp.bfloat16).reshape(rows_all, KV_HEADS * HEAD_DIM)
        value_bf = per_sequence(grad_values).astype(jnp.bfloat16).reshape(rows_all, KV_HEADS * HEAD_DIM)
        query_grad = jnp.dot(first_flat.T, query_bf, preferred_element_type=jnp.float32)
        key_grad = jnp.dot(first_flat.T, key_bf, preferred_element_type=jnp.float32)
        value_grad = jnp.dot(first_flat.T, value_bf, preferred_element_type=jnp.float32)
        grad_first = jnp.dot(query_bf, query_weight[index].T, preferred_element_type=jnp.float32) + jnp.dot(key_bf, key_weight[index].T, preferred_element_type=jnp.float32) + jnp.dot(value_bf, value_weight[index].T, preferred_element_type=jnp.float32)
        grad_norm_one, input_part = rms_backward(grad_first.reshape(LEN, SEQS, D), plain_one, inverse_one, input_gain[index])
        grad_hidden = grad_mixed + grad_norm_one
        weight_parts[index] = (query_grad, key_grad, value_grad, out_grad, gate_grad, up_grad, down_grad)
        gain_parts[index] = (input_part, query_part, key_part, post_part)
    weights_out = [jnp.stack([part[member] for part in weight_parts]) for member in range(7)]
    gains_out = [jnp.stack([part[member] for part in gain_parts]) for member in range(4)]
    return (output, grad_hidden, gains_out[0], weights_out[0], weights_out[1], weights_out[2], gains_out[1], gains_out[2], weights_out[3], gains_out[3], weights_out[4], weights_out[5], weights_out[6])
```

```python
import functools

import jax
import jax.numpy as jnp
import numpy as np
from jax import lax
from jax.experimental import pallas as pl
from jax.experimental.pallas import tpu as pltpu
from jax.sharding import PartitionSpec as P

EPS = 1e-06
THETA = 1000000.0
MESH = pl.DeviceIdType.MESH
F32 = jnp.float32
BF16 = jnp.bfloat16


def rms_forward(field, gain):
    inverse = lax.rsqrt(jnp.mean(field * field, axis=-1, keepdims=True) + EPS)
    normed = field * inverse
    return (normed * gain, normed, inverse)


def rms_backward(grad_out, normed, inverse, gain):
    scaled = grad_out * gain
    return inverse * (scaled - normed * jnp.mean(scaled * normed, axis=-1, keepdims=True))


def rope_tables(positions, head_dim):
    half = head_dim // 2
    frequency = THETA ** (-(2.0 * jnp.arange(half, dtype=F32)) / head_dim)
    angles = positions[:, None] * frequency[None, :]
    cosine, sine = jnp.cos(angles), jnp.sin(angles)
    return (jnp.concatenate([cosine, cosine], axis=-1), jnp.concatenate([-sine, sine], axis=-1))


def remote(src, dst, send, recv, **where):
    return pltpu.make_async_remote_copy(
        src_ref=src,
        dst_ref=dst,
        send_sem=send,
        recv_sem=recv,
        device_id=where,
        device_id_type=MESH,
    )


def boundary_kernel(mode, n_ctx, n_tp, *refs):
    refs = list(refs)
    has_sum = mode != "first"
    has_gather = mode in ("first", "fwd", "bwd")
    partial = refs.pop(0) if has_sum else None
    stream = refs.pop(0)
    gain = refs.pop(0) if mode not in ("fwd_last",) else None
    grad_res = refs.pop(0) if mode in ("bwd", "bwd_last") else None
    fresh = refs.pop(0) if mode != "first" else None
    gain_part = refs.pop(0) if mode in ("bwd", "bwd_last") else None
    out = refs.pop(0) if has_gather else None
    if has_sum:
        landed, rs_send, rs_recv = refs.pop(0), refs.pop(0), refs.pop(0)
    if has_gather:
        own, z_send, z_recv, t_send, t_recv = refs

    me_c = lax.axis_index("ctx")
    me_t = lax.axis_index("tp")
    tp_peers = [lax.rem(me_t + d, n_tp) for d in range(1, n_tp)]
    ctx_peers = [lax.rem(me_c + d, n_ctx) for d in range(1, n_ctx)] if has_gather else []
    barrier = pltpu.get_barrier_semaphore()
    for peer in tp_peers:
        pl.semaphore_signal(barrier, inc=1, device_id={"tp": peer}, device_id_type=MESH)
    for peer in ctx_peers:
        pl.semaphore_signal(barrier, inc=1, device_id={"ctx": peer}, device_id_type=MESH)
    pl.semaphore_wait(barrier, len(tp_peers) + len(ctx_peers))

    if has_sum:
        sums = [
            remote(partial.at[peer], landed.at[d], rs_send.at[d], rs_recv.at[d], tp=peer)
            for d, peer in enumerate(tp_peers)
        ]
        for copy in sums:
            copy.start()
        total = partial[me_t].astype(F32)
        for d, copy in enumerate(sums):
            copy.wait_recv()
            total = total + landed[d].astype(F32)
        for copy in sums:
            copy.wait_send()

    field = stream[...]
    if mode == "first":
        sent = rms_forward(field, gain[...])[0].astype(BF16)
    elif mode in ("fwd", "fwd_last"):
        field = field + total
        fresh[...] = field
        if mode == "fwd":
            sent = rms_forward(field, gain[...])[0].astype(BF16)
    else:
        _, normed, inverse = rms_forward(field, gain[...])
        gain_part[...] = jnp.sum(total * normed, axis=0, keepdims=True)
        field = grad_res[...] + rms_backward(total, normed, inverse, gain[...])
        fresh[...] = field
        sent = field.astype(BF16)

    if has_gather:
        own[...] = sent
        copies = []
        for d, peer in enumerate(ctx_peers):
            copies.append(
                remote(own, out.at[me_c, me_t], z_send.at[d], z_recv.at[d], ctx=peer)
            )
        for d, peer in enumerate(tp_peers):
            copies.append(
                remote(own, out.at[me_c, me_t], t_send.at[0, d], t_recv.at[0, d], tp=peer)
            )
        for copy in copies:
            copy.start()
        out[me_c, me_t] = sent
        for d in range(n_ctx - 1):
            source = lax.rem(me_c + n_ctx - (d + 1), n_ctx)
            slot = out.at[source, me_t]
            remote(own, slot, z_send.at[d], z_recv.at[d], ctx=source).wait_recv()
            for k, peer in enumerate(tp_peers):
                copy = remote(slot, slot, t_send.at[d + 1, k], t_recv.at[d + 1, k], tp=peer)
                copy.start()
                copies.append(copy)
        for d in range(n_ctx):
            source = lax.rem(me_c + n_ctx - d, n_ctx)
            for k in range(n_tp - 1):
                origin = lax.rem(me_t + n_tp - (k + 1), n_tp)
                remote(
                    own, out.at[source, origin], t_send.at[d, k], t_recv.at[d, k], tp=origin
                ).wait_recv()
        for copy in copies:
            copy.wait_send()


IDS = {"first": 0, "fwd": 1, "fwd_last": 2, "bwd": 3, "bwd_last": 4}


def boundary(mode, stream, gain=None, partial=None, grad_res=None):
    n_ctx, n_tp = lax.axis_size("ctx"), lax.axis_size("tp")
    rows, width = stream.shape
    operands = []
    if partial is not None:
        operands.append(partial.reshape(n_tp, rows, width))
    operands.append(stream)
    if gain is not None:
        operands.append(gain.reshape(1, width))
    if grad_res is not None:
        operands.append(grad_res)
    shapes = []
    if mode != "first":
        shapes.append(jax.ShapeDtypeStruct((rows, width), F32))
    if grad_res is not None:
        shapes.append(jax.ShapeDtypeStruct((1, width), F32))
    scratch = []
    dma = pltpu.SemaphoreType.DMA
    if partial is not None:
        scratch += [pltpu.VMEM((n_tp - 1, rows, width), BF16), dma((n_tp - 1,)), dma((n_tp - 1,))]
    if mode in ("first", "fwd", "bwd"):
        shapes.append(jax.ShapeDtypeStruct((n_ctx, n_tp, rows, width), BF16))
        scratch += [
            pltpu.VMEM((rows, width), BF16),
            dma((n_ctx - 1,)),
            dma((n_ctx - 1,)),
            dma((n_ctx, n_tp - 1)),
            dma((n_ctx, n_tp - 1)),
        ]
    vmem = pl.BlockSpec(memory_space=pltpu.VMEM)
    outs = pl.pallas_call(
        functools.partial(boundary_kernel, mode, n_ctx, n_tp),
        out_shape=shapes,
        in_specs=[vmem] * len(operands),
        out_specs=[vmem] * len(shapes),
        scratch_shapes=scratch,
        name="boundary_" + mode,
        compiler_params=pltpu.CompilerParams(
            collective_id=IDS[mode], has_side_effects=True, vmem_limit_bytes=32 * 2**20
        ),
    )(*operands)
    outs = list(outs)
    if mode in ("first", "fwd", "bwd"):
        outs[-1] = outs[-1].reshape(n_ctx * n_tp * rows, width)
    return outs


def gains_kernel(sizes, x_ref, o_ref, cur, land_0, land_1, land_2, send, recv):
    lands = (land_0, land_1, land_2)
    axes = list(sizes)
    barrier = pltpu.get_barrier_semaphore()
    peers = {}
    count = 0
    for axis in axes:
        me = lax.axis_index(axis)
        peers[axis] = [lax.rem(me + d, sizes[axis]) for d in range(1, sizes[axis])]
        for peer in peers[axis]:
            pl.semaphore_signal(barrier, inc=1, device_id={axis: peer}, device_id_type=MESH)
            count += 1
    pl.semaphore_wait(barrier, count)
    total = x_ref[...]
    base = 0
    for step, axis in enumerate(axes):
        cur[step] = total
        copies = [
            remote(
                cur.at[step], lands[step].at[d], send.at[base + d], recv.at[base + d], **{axis: peer}
            )
            for d, peer in enumerate(peers[axis])
        ]
        for copy in copies:
            copy.start()
        me = lax.axis_index(axis)
        parts = []
        for d, copy in enumerate(copies):
            copy.wait_recv()
        acc = jnp.zeros_like(total)
        for position in range(sizes[axis]):
            offset = lax.rem(me + sizes[axis] - position, sizes[axis])
            slot = jnp.maximum(offset - 1, 0)
            acc = acc + jnp.where(offset == 0, total, lands[step][slot])
        total = acc
        for copy in copies:
            copy.wait_send()
        base += len(copies)
    o_ref[...] = total


def sum_gains(x):
    sizes = {axis: lax.axis_size(axis) for axis in ("dp", "ctx", "tp")}
    count = sum(n - 1 for n in sizes.values())
    vmem = pl.BlockSpec(memory_space=pltpu.VMEM)
    return pl.pallas_call(
        functools.partial(gains_kernel, sizes),
        out_shape=jax.ShapeDtypeStruct(x.shape, F32),
        in_specs=[vmem],
        out_specs=vmem,
        scratch_shapes=[pltpu.VMEM((3,) + x.shape, F32)]
        + [pltpu.VMEM((max(n - 1, 1),) + x.shape, F32) for n in sizes.values()]
        + [pltpu.SemaphoreType.DMA((count,)), pltpu.SemaphoreType.DMA((count,))],
        name="sum_gains",
        compiler_params=pltpu.CompilerParams(collective_id=5, has_side_effects=True),
    )(x)


NT = (((1,), (1,)), ((), ()))
NN = (((1,), (0,)), ((), ()))
TN = (((0,), (0,)), ((), ()))


def dot(a, b, dims):
    return lax.dot_general(a, b, dims, preferred_element_type=F32)


def turn(x):
    return pltpu.roll(x, x.shape[-1] // 2, axis=1)


def prepared(x, gain, cosine, sine):
    normed, plain, inverse = rms_forward(x, gain)
    return (normed * cosine + turn(normed) * sine).astype(BF16), plain, inverse


def soft_weights(scale, bq, q, k):
    rows = pl.program_id(2) * bq + lax.broadcasted_iota(jnp.int32, (bq, k.shape[0]), 0)
    cols = lax.broadcasted_iota(jnp.int32, (bq, k.shape[0]), 1)
    scores = jnp.where(cols <= rows, dot(q, k, NT) * scale, -jnp.inf)
    weights = jnp.exp(scores - jnp.max(scores, axis=-1, keepdims=True))
    return weights, jnp.sum(weights, axis=-1, keepdims=True)


def attend_kernel(
    scale, bq, q_ref, k_ref, v_ref, cq_ref, sq_ref, ck_ref, sk_ref, qg_ref, kg_ref, o_ref, k_rot
):
    @pl.when((pl.program_id(1) == 0) & (pl.program_id(2) == 0))
    def _():
        k_rot[...] = prepared(k_ref[...], kg_ref[...], ck_ref[...], sk_ref[...])[0]

    q = prepared(q_ref[...], qg_ref[...], cq_ref[...], sq_ref[...])[0]
    weights, total = soft_weights(scale, bq, q, k_rot[...])
    o_ref[...] = (dot(weights.astype(BF16), v_ref[...], NN) / total).astype(BF16)


def attend_back_kernel(
    scale,
    bq,
    q_ref,
    k_ref,
    v_ref,
    cq_ref,
    sq_ref,
    ck_ref,
    sk_ref,
    qg_ref,
    kg_ref,
    o_ref,
    do_ref,
    dq_ref,
    dk_ref,
    dv_ref,
    qp_ref,
    kp_ref,
    k_rot,
    dk_sum,
    dv_sum,
):
    head, member, block = pl.program_id(0), pl.program_id(1), pl.program_id(2)

    @pl.when((head == 0) & (member == 0) & (block == 0))
    def _():
        qp_ref[...] = jnp.zeros_like(qp_ref)
        kp_ref[...] = jnp.zeros_like(kp_ref)

    @pl.when((member == 0) & (block == 0))
    def _():
        k_rot[...] = prepared(k_ref[...], kg_ref[...], ck_ref[...], sk_ref[...])[0]
        dk_sum[...] = jnp.zeros_like(dk_sum)
        dv_sum[...] = jnp.zeros_like(dv_sum)

    q, plain, inverse = prepared(q_ref[...], qg_ref[...], cq_ref[...], sq_ref[...])
    k, do = k_rot[...], do_ref[...]
    weights, total = soft_weights(scale, bq, q, k)
    probs = weights / total
    delta = jnp.sum(do.astype(F32) * o_ref[...].astype(F32), axis=-1, keepdims=True)
    dscore = (probs * (dot(do, v_ref[...], NT) - delta)).astype(BF16)
    dk_sum[...] += dot(dscore, q, TN) * scale
    dv_sum[...] += dot(probs.astype(BF16), do, TN)
    grad = dot(dscore, k, NN) * scale
    grad = grad * cq_ref[...] - turn(grad) * sq_ref[...]
    qp_ref[...] += jnp.sum(grad * plain, axis=0, keepdims=True)
    dq_ref[...] = rms_backward(grad, plain, inverse, qg_ref[...]).astype(BF16)

    @pl.when((member == pl.num_programs(1) - 1) & (block == pl.num_programs(2) - 1))
    def _():
        _, k_plain, k_inverse = prepared(k_ref[...], kg_ref[...], ck_ref[...], sk_ref[...])
        grad_k = dk_sum[...]
        grad_k = grad_k * ck_ref[...] - turn(grad_k) * sk_ref[...]
        kp_ref[...] += jnp.sum(grad_k * k_plain, axis=0, keepdims=True)
        dk_ref[...] = rms_backward(grad_k, k_plain, k_inverse, kg_ref[...]).astype(BF16)
        dv_ref[...] = dv_sum[...].astype(BF16)


def attention(scale, group, query, keys, values, cosine, sine, query_gain, key_gain, *back):
    length, kv_width = keys.shape
    head_dim = cosine.shape[-1]
    kv_heads = kv_width // head_dim
    bq = min(length, 256)
    rows = pl.BlockSpec((bq, head_dim), lambda h, g, i: (i, h * group + g))
    keyed = pl.BlockSpec((length, head_dim), lambda h, g, i: (0, h))
    table_q = pl.BlockSpec((bq, head_dim), lambda h, g, i: (i, 0))
    table_k = pl.BlockSpec((length, head_dim), lambda h, g, i: (0, 0))
    flat = pl.BlockSpec((1, head_dim), lambda h, g, i: (0, 0))
    wide = jax.ShapeDtypeStruct((length, kv_width * group), BF16)
    narrow = jax.ShapeDtypeStruct((length, kv_width), BF16)
    part = jax.ShapeDtypeStruct((1, head_dim), F32)
    work = 2 * length * length * head_dim * kv_heads * group
    scratch = [pltpu.VMEM((length, head_dim), BF16)]
    if back:
        scratch += [pltpu.VMEM((length, head_dim), F32)] * 2
    return pl.pallas_call(
        functools.partial(attend_back_kernel if back else attend_kernel, scale, bq),
        grid=(kv_heads, group, length // bq),
        out_shape=(wide, narrow, narrow, part, part) if back else wide,
        in_specs=[rows, keyed, keyed, table_q, table_q, table_k, table_k, flat, flat]
        + [rows] * len(back),
        out_specs=(rows, keyed, keyed, flat, flat) if back else rows,
        scratch_shapes=scratch,
        name="attend_back" if back else "attend",
        cost_estimate=pl.CostEstimate(
            flops=work * (5 if back else 2), bytes_accessed=4 * length * 1024, transcendentals=0
        ),
        compiler_params=pltpu.CompilerParams(vmem_limit_bytes=40 * 2**20),
    )(
        query,
        keys,
        values,
        cosine,
        sine,
        cosine,
        sine,
        query_gain.reshape(1, -1),
        key_gain.reshape(1, -1),
        *back,
    )


def on_device(
    block_input,
    input_gain,
    query_weight,
    key_weight,
    value_weight,
    query_gain,
    key_gain,
    out_weight,
    post_gain,
    gate_weight,
    up_weight,
    down_weight,
    grad_output,
):
    local_rows, seq_local, width = block_input.shape
    assert seq_local == 1 and lax.axis_size("dp") == 2
    layers = input_gain.shape[0]
    head_dim = query_gain.shape[-1]
    heads = query_weight.shape[-1] // head_dim
    kv_heads = key_weight.shape[-1] // head_dim
    n_ctx, n_tp = lax.axis_size("ctx"), lax.axis_size("tp")
    block_rows = local_rows * n_tp
    length = block_rows * n_ctx
    scale = head_dim ** (-0.5)
    first_row = lax.axis_index("ctx") * block_rows
    cosine, sine = rope_tables(jnp.arange(length, dtype=F32), head_dim)
    piece = width // (2 * n_ctx)
    my_cols = (lax.axis_index("dp") * n_ctx + lax.axis_index("ctx")) * piece
    other_cols = ((1 - lax.axis_index("dp")) * n_ctx + lax.axis_index("ctx")) * piece
    swap = [(0, 1), (1, 0)]

    def mine(x):
        return lax.dynamic_slice_in_dim(x, first_row, block_rows, 0)

    def slices(x):
        parts = [lax.dynamic_slice_in_dim(x, at, piece, 1) for at in (my_cols, other_cols)]
        return jnp.concatenate(parts, axis=1)

    def settle(grad, axis):
        own, other = jnp.split(grad, 2, axis=axis)
        return own + lax.ppermute(other.astype(BF16), "dp", swap).astype(F32)

    def settle_rows(*products):
        other = [x[piece:].astype(BF16) for x in products]
        other = lax.ppermute(jnp.concatenate(other, axis=1), "dp", swap).astype(F32)
        out = []
        at = 0
        for x in products:
            out.append(x[:piece] + other[:, at : at + x.shape[1]])
            at += x.shape[1]
        return out

    hidden = block_input[:, 0]
    grad_hidden = grad_output[:, 0]
    grad_rows = lax.all_gather(grad_hidden.astype(BF16), ("ctx", "tp"), axis=0, tiled=True)
    (first_in,) = boundary("first", hidden, input_gain[0])
    kept = []
    for l in range(layers):
        query = dot(first_in, query_weight[l], NN)
        keys = dot(first_in, key_weight[l], NN)
        values = dot(first_in, value_weight[l], NN).astype(BF16)
        attend_args = (scale, heads // kv_heads, query, keys, values, cosine, sine)
        attend_args += (query_gain[l], key_gain[l])
        attended = attention(*attend_args)
        partial = dot(mine(attended), out_weight[l], NN).astype(BF16)
        mixed, second_in = boundary("fwd", hidden, post_gain[l], partial)
        gate = dot(second_in, gate_weight[l], NN)
        upward = dot(second_in, up_weight[l], NN)
        swish = (jax.nn.silu(gate) * upward).astype(BF16)
        partial = dot(mine(swish), down_weight[l], NN).astype(BF16)
        kept.append(
            (hidden, first_in, attend_args, attended, mixed, second_in, gate, upward, swish)
        )
        if l + 1 < layers:
            hidden, first_in = boundary("fwd", mixed, input_gain[l + 1], partial)
        else:
            hidden = mixed + lax.psum_scatter(
                partial, "tp", scatter_dimension=0, tiled=True
            ).astype(F32)

    grads = [None] * layers
    gains = [None] * layers
    for l in reversed(range(layers)):
        x_in, first_in, attend_args, attended, mixed, second_in, gate, upward, swish = kept[l]
        grad_swish = dot(grad_rows, down_weight[l], NT)
        sigma = jax.nn.sigmoid(gate)
        grad_gate = (grad_swish * upward * (sigma * (1.0 + gate * (1.0 - sigma)))).astype(BF16)
        grad_up = (grad_swish * (gate * sigma)).astype(BF16)
        partial = dot(mine(grad_gate), gate_weight[l], NT) + dot(mine(grad_up), up_weight[l], NT)
        grad_mixed, post_part, mixed_rows = boundary(
            "bwd", mixed, post_gain[l], partial.astype(BF16), grad_hidden
        )
        second_cols = slices(second_in)
        down_grad = settle(dot(swish, slices(grad_rows), TN), 1)
        gate_grad, up_grad = settle_rows(
            dot(second_cols, grad_gate, TN), dot(second_cols, grad_up, TN)
        )

        grad_heads = dot(mixed_rows, out_weight[l], NT).astype(BF16)
        out_grad = settle(dot(attended, slices(mixed_rows), TN), 1)
        query_bf, key_bf, value_bf, q_part, k_part = attention(*attend_args, attended, grad_heads)
        partial = (
            dot(mine(query_bf), query_weight[l], NT)
            + dot(mine(key_bf), key_weight[l], NT)
            + dot(mine(value_bf), value_weight[l], NT)
        ).astype(BF16)
        if l:
            grad_hidden, input_part, grad_rows = boundary(
                "bwd", x_in, input_gain[l], partial, grad_mixed
            )
        else:
            grad_hidden, input_part = boundary(
                "bwd_last", x_in, input_gain[l], partial, grad_mixed
            )
        first_cols = slices(first_in)
        query_grad, key_grad, value_grad = settle_rows(
            dot(first_cols, query_bf, TN),
            dot(first_cols, key_bf, TN),
            dot(first_cols, value_bf, TN),
        )
        grads[l] = (query_grad, key_grad, value_grad, out_grad, gate_grad, up_grad, down_grad)
        gains[l] = (input_part[0], q_part[0] / n_ctx, k_part[0] / n_ctx, post_part[0])
    stacked = [jnp.stack([part[m] for part in grads]) for m in range(7)]
    packed = jnp.concatenate([v for part in gains for v in part])
    sizes = [v.shape[0] for part in gains for v in part]
    padded = -(-packed.shape[0] // 1024) * 1024
    packed = jnp.pad(packed, (0, padded - packed.shape[0])).reshape(-1, 128)
    summed = sum_gains(packed).reshape(-1)
    pieces = []
    at = 0
    for size in sizes:
        pieces.append(summed[at : at + size])
        at += size
    gains = [jnp.stack([pieces[4 * l + m] for l in range(layers)]) for m in range(4)]
    return (
        hidden[:, None],
        grad_hidden[:, None],
        gains[0],
        stacked[0],
        stacked[1],
        stacked[2],
        gains[1],
        gains[2],
        stacked[3],
        gains[3],
        stacked[4],
        stacked[5],
        stacked[6],
    )


def rope_constants(length, head_dim):
    half = head_dim // 2
    frequency = np.float32(THETA) ** (-(np.float32(2.0) * np.arange(half, dtype=np.float32)) / np.float32(head_dim))
    angles = np.arange(length, dtype=np.float32)[:, None] * frequency.astype(np.float32)[None, :]
    cosine, sine = np.cos(angles), np.sin(angles)
    return (
        np.concatenate([cosine, cosine], axis=-1).astype(np.float32),
        np.concatenate([-sine, sine], axis=-1).astype(np.float32),
    )


def chunks(total, step=256):
    step = step if total % step == 0 else 128
    return [(at, step) for at in range(0, total, step)]


def fused_kernel(sz, *refs):
    (layers, n_ctx, n_tp, rows, width, heads, kv_heads, head_dim, ff) = sz
    block = rows * n_tp
    length = block * n_ctx
    group = heads // kv_heads
    q_w, k_w = heads * head_dim, kv_heads * head_dim
    piece = width // (2 * n_ctx)
    log2e = 1.4426950408889634
    scale = head_dim ** (-0.5)
    (x_ref, go_ref, ig_ref, pg_ref, qg_ref, kg_ref, cos_ref, sin_ref) = refs[:8]
    (wq_h, wk_h, wv_h, wo_h, wg_h, wu_h, wd_h) = refs[8:15]
    (y_ref, gx_ref, gain_ref, oq_ref, ok_ref, ov_ref, oo_ref, og_ref, ou_ref, od_ref) = refs[15:25]
    (wqkv, wo, wgu, wd, G, P, land, q_raw, k_raw, q_rot, k_rot, vals, att, swish, fa, fb, ggu, d_o, dqkv,
     dk_acc, dv_acc, mixed_s, xs_s, gm_s, gains, g_dp, g_ctx, g_tp,
     s_qkv, s_out, s_gu, s_dn, l_qkv, l_out, l_gu, l_dn,
     w_sem, z_send, z_recv, t_send, t_recv, r_send, r_recv, d_send, d_recv, a_send, a_recv) = refs[25:]

    c, t, dp = lax.axis_index("ctx"), lax.axis_index("tp"), lax.axis_index("dp")
    tp_peers = [lax.rem(t + k, n_tp) for k in range(1, n_tp)]
    ctx_peers = [lax.rem(c + d, n_ctx) for d in range(1, n_ctx)]
    other = 1 - dp
    pending = []

    loads = []

    def load(src, dst):
        copy = pltpu.make_async_copy(src, dst, w_sem.at[len(loads)])
        copy.start()
        loads.append(copy)

    for l in range(layers):
        load(wk_h.at[l], wqkv.at[l, :, pl.ds(q_w, k_w)])
        load(wv_h.at[l], wqkv.at[l, :, pl.ds(q_w + k_w, k_w)])
        load(wq_h.at[l], wqkv.at[l, :, pl.ds(0, q_w)])
        load(wo_h.at[l], wo.at[l])
        load(wg_h.at[l], wgu.at[l, :, pl.ds(0, ff)])
        load(wu_h.at[l], wgu.at[l, :, pl.ds(ff, ff)])
        load(wd_h.at[l], wd.at[l])

    barrier = pltpu.get_barrier_semaphore()
    for peer in tp_peers:
        pl.semaphore_signal(barrier, inc=1, device_id={"tp": peer}, device_id_type=MESH)
    for peer in ctx_peers:
        pl.semaphore_signal(barrier, inc=1, device_id={"ctx": peer}, device_id_type=MESH)
    pl.semaphore_signal(barrier, inc=1, device_id={"dp": other}, device_id_type=MESH)
    pl.semaphore_wait(barrier, n_tp + n_ctx - 1)

    def push(copy):
        copy.start()
        pending.append(copy)

    def start_gather(g, value):
        own = G.at[g, c, t]
        G[g, c, t] = value
        for d, peer in enumerate(ctx_peers):
            push(remote(own, own, z_send.at[g, d], z_recv.at[g, d], ctx=peer))
        for k, peer in enumerate(tp_peers):
            push(remote(own, own, t_send.at[g, 0, k], t_recv.at[g, 0, k], tp=peer))

    def forward(g):
        for d in range(n_ctx - 1):
            source = lax.rem(c + n_ctx - (d + 1), n_ctx)
            slot = G.at[g, source, t]
            remote(slot, slot, z_send.at[g, d], z_recv.at[g, d], ctx=source).wait_recv()
            for k, peer in enumerate(tp_peers):
                push(remote(slot, slot, t_send.at[g, d + 1, k], t_recv.at[g, d + 1, k], tp=peer))

    def wait_block(g, d):
        source = lax.rem(c + n_ctx - d, n_ctx)
        for k in range(n_tp - 1):
            origin = lax.rem(t + n_tp - (k + 1), n_tp)
            slot = G.at[g, source, origin]
            remote(slot, slot, t_send.at[g, d, k], t_recv.at[g, d, k], tp=origin).wait_recv()

    def start_sum(r):
        for k, peer in enumerate(tp_peers):
            push(remote(P.at[r, peer], land.at[r, k], r_send.at[r, k], r_recv.at[r, k], tp=peer))

    def finish_sum(r):
        total = P[r, t].astype(F32)
        for k in range(n_tp - 1):
            remote(P.at[r, t], land.at[r, k], r_send.at[r, k], r_recv.at[r, k], tp=t).wait_recv()
            total = total + land[r, k].astype(F32)
        return total

    def others(body):
        def step(d, carry):
            body(d, lax.rem(c + n_ctx - d, n_ctx))
            return carry

        lax.fori_loop(1, n_ctx, step, 0)

    def tokens(g, s):
        return G[g, s].reshape(block, width)

    def put_partial(r, at, step, value):
        P[r, :, :, at : at + step] = value.astype(BF16).reshape(n_tp, rows, step)

    def qkv(l, s):
        x = tokens(l, s)
        cosine = cos_ref[pl.ds(pl.multiple_of(s * block, block), block), :]
        sine = sin_ref[pl.ds(pl.multiple_of(s * block, block), block), :]
        qg, kg = qg_ref[l : l + 1, :], kg_ref[l : l + 1, :]
        for at, step in chunks(q_w + 2 * k_w):
            y = dot(x, wqkv[l, :, at : at + step], NN)
            for sub in range(0, step, head_dim):
                yh = y[:, sub : sub + head_dim]
                h = (at + sub) // head_dim
                if h < heads:
                    q_raw[l, h, s] = yh
                    q_rot[l, h, s] = prepared(yh, qg, cosine, sine)[0]
                elif h < heads + kv_heads:
                    k_raw[l, h - heads, s] = yh
                    k_rot[l, h - heads, s] = prepared(yh, kg, cosine, sine)[0]
                else:
                    vals[l, h - heads - kv_heads, s] = yh.astype(BF16)

    def attend_block(l, i):
        at_row = i * block + lax.broadcasted_iota(jnp.int32, (block, length), 0)
        allowed = lax.broadcasted_iota(jnp.int32, (block, length), 1) <= at_row
        for h in range(heads):
            k = k_rot[l, h // group].reshape(length, head_dim)
            v = vals[l, h // group].reshape(length, head_dim)
            scores = dot(q_rot[l, h, i], k, NT) * (scale * log2e)
            weights = jnp.where(allowed, jnp.exp2(scores), 0.0)
            total = jnp.sum(weights, axis=-1, keepdims=True)
            out = dot(weights.astype(BF16), v, NN) / total
            att[l, i, :, h * head_dim : (h + 1) * head_dim] = out.astype(BF16)

    def out_partial(l):
        a = att[l, c]
        for at, step in chunks(width):
            put_partial(l, at, step, dot(a, wo[l, :, at : at + step], NN))

    def mlp_forward(l, s):
        x = tokens(layers + l, s)
        for at, step in chunks(ff):
            gate = dot(x, wgu[l, :, at : at + step], NN)
            up = dot(x, wgu[l, :, ff + at : ff + at + step], NN)
            sigma = jax.nn.sigmoid(gate)
            silu = gate * sigma
            swish[l, s, :, at : at + step] = (silu * up).astype(BF16)
            fa[l, s, :, at : at + step] = (up * (sigma * (1.0 + gate * (1.0 - sigma)))).astype(BF16)
            fb[l, s, :, at : at + step] = silu.astype(BF16)

    def down_partial(l):
        a = swish[l, c]
        for at, step in chunks(width):
            put_partial(layers + l, at, step, dot(a, wd[l, :, at : at + step], NN))

    def mlp_backward(l, s):
        x = tokens(2 * layers + l, s)
        for at, step in chunks(ff):
            grad = dot(x, wd[l, at : at + step, :], NT)
            ggu[s, :, at : at + step] = (grad * fa[l, s, :, at : at + step].astype(F32)).astype(BF16)
            ggu[s, :, ff + at : ff + at + step] = (
                grad * fb[l, s, :, at : at + step].astype(F32)
            ).astype(BF16)

    def mlp_back_partial(l):
        a = ggu[c]
        for at, step in chunks(width):
            put_partial(2 * layers + l, at, step, dot(a, wgu[l, at : at + step, :], NT))

    def heads_back(l, s):
        x = tokens(3 * layers + l, s)
        for at, step in chunks(q_w):
            d_o[s, :, at : at + step] = dot(x, wo[l, at : at + step, :], NT).astype(BF16)

    def attend_backward(l):
        dk_acc[...] = jnp.zeros_like(dk_acc)
        dv_acc[...] = jnp.zeros_like(dv_acc)
        half = length // 2
        per = n_ctx // 2
        causal = lax.broadcasted_iota(jnp.int32, (half, half), 1) <= lax.broadcasted_iota(
            jnp.int32, (half, half), 0
        )
        qg, kg = qg_ref[l : l + 1, :], kg_ref[l : l + 1, :]

        def one_head(h, part):
            lanes = pl.ds(pl.multiple_of(h * head_dim, head_dim), head_dim)
            kv = h // group
            for i in range(2):
                span = slice(i * per, (i + 1) * per)
                extent = (i + 1) * half
                q = q_rot[l, h, span].reshape(half, head_dim)
                do = d_o[span, :, lanes].reshape(half, head_dim)
                a = att[l, span, :, lanes].reshape(half, head_dim)
                k = k_rot[l, kv, : (i + 1) * per].reshape(extent, head_dim)
                v = vals[l, kv, : (i + 1) * per].reshape(extent, head_dim)
                weights = jnp.exp2(dot(q, k, NT) * (scale * log2e))
                last = jnp.where(causal, weights[:, i * half :], 0.0)
                weights = jnp.concatenate([weights[:, :half], last], axis=1) if i else last
                probs = weights / jnp.sum(weights, axis=-1, keepdims=True)
                delta = jnp.sum(do.astype(F32) * a.astype(F32), axis=-1, keepdims=True)
                dscore = (probs * (dot(do, v, NT) - delta)).astype(BF16)
                dk_acc[kv, :extent] += dot(dscore, q, TN)
                dv_acc[kv, :extent] += dot(probs.astype(BF16), do, TN)
                cosine = cos_ref[i * half : (i + 1) * half, :]
                sine = sin_ref[i * half : (i + 1) * half, :]
                grad = dot(dscore, k, NN) * scale
                grad = grad * cosine - turn(grad) * sine
                _, plain, inverse = rms_forward(q_raw[l, h, span].reshape(half, head_dim), qg)
                part = part + jnp.sum(grad * plain, axis=0, keepdims=True)
                grad = rms_backward(grad, plain, inverse, qg).astype(BF16)
                dqkv[span, :, lanes] = grad.reshape(per, block, head_dim)
            return part

        q_part = lax.fori_loop(0, heads, one_head, jnp.zeros((1, head_dim), F32))
        k_part = jnp.zeros((1, head_dim), F32)
        for kv in range(kv_heads):
            grad = dk_acc[kv] * scale
            grad = grad * cos_ref[...] - turn(grad) * sin_ref[...]
            _, plain, inverse = rms_forward(k_raw[l, kv].reshape(length, head_dim), kg)
            k_part = k_part + jnp.sum(grad * plain, axis=0, keepdims=True)
            grad = rms_backward(grad, plain, inverse, kg).astype(BF16)
            at = q_w + kv * head_dim
            dqkv[:, :, at : at + head_dim] = grad.reshape(n_ctx, block, head_dim)
            at += k_w
            dqkv[:, :, at : at + head_dim] = dv_acc[kv].astype(BF16).reshape(n_ctx, block, head_dim)
        at = 2 * layers
        gains[at : at + 1, 2 * l * head_dim : (2 * l + 1) * head_dim] = q_part / n_ctx
        gains[at : at + 1, (2 * l + 1) * head_dim : (2 * l + 2) * head_dim] = k_part / n_ctx

    def qkv_back_partial(l):
        a = dqkv[c]
        for at, step in chunks(width):
            put_partial(3 * layers + l, at, step, dot(a, wqkv[l, at : at + step, :], NT))

    my_cols = pl.ds(pl.multiple_of((dp * n_ctx + c) * piece, piece), piece)
    other_cols = pl.ds(pl.multiple_of((other * n_ctx + c) * piece, piece), piece)

    def columns(g):
        parts = [G[g, :, :, :, cols].reshape(length, piece) for cols in (my_cols, other_cols)]
        return jnp.concatenate(parts, axis=1)

    def exchange(i, src, dst):
        push(remote(src, dst, d_send.at[i], d_recv.at[i], dp=other))

    def grads_mlp(l):
        x = columns(layers + l)
        for at, step in chunks(2 * ff):
            g = dot(x, ggu[:, :, at : at + step].reshape(length, step), TN)
            ref, base = (og_ref, at) if at < ff else (ou_ref, at - ff)
            ref[l, :, base : base + step] = g[:piece]
            s_gu[l, :, at : at + step] = g[piece:].astype(BF16)
        exchange(4 * l, s_gu.at[l], l_gu.at[l])
        x = columns(2 * layers + l)
        for at, step in chunks(ff):
            g = dot(swish[l, :, :, at : at + step].reshape(length, step), x, TN)
            od_ref[l, at : at + step, :] = g[:, :piece]
            s_dn[l, at : at + step, :] = g[:, piece:].astype(BF16)
        exchange(4 * l + 1, s_dn.at[l], l_dn.at[l])

    def grads_out(l):
        x = columns(3 * layers + l)
        for at, step in chunks(q_w):
            g = dot(att[l, :, :, at : at + step].reshape(length, step), x, TN)
            oo_ref[l, at : at + step, :] = g[:, :piece]
            s_out[l, at : at + step, :] = g[:, piece:].astype(BF16)
        exchange(4 * l + 2, s_out.at[l], l_out.at[l])

    def grads_qkv(l):
        x = columns(l)
        for at, step in chunks(q_w + 2 * k_w):
            g = dot(x, dqkv[:, :, at : at + step].reshape(length, step), TN)
            if at < q_w:
                oq_ref[l, :, at : at + step] = g[:piece]
            elif at < q_w + k_w:
                ok_ref[l, :, at - q_w : at - q_w + step] = g[:piece]
            else:
                ov_ref[l, :, at - q_w - k_w : at - q_w - k_w + step] = g[:piece]
            s_qkv[l, :, at : at + step] = g[piece:].astype(BF16)
        exchange(4 * l + 3, s_qkv.at[l], l_qkv.at[l])

    def settle(l):
        def landed(i, dst):
            remote(dst, dst, d_send.at[i], d_recv.at[i], dp=other).wait_recv()

        landed(4 * l, l_gu.at[l])
        og_ref[l] += l_gu[l, :, :ff].astype(F32)
        ou_ref[l] += l_gu[l, :, ff:].astype(F32)
        landed(4 * l + 1, l_dn.at[l])
        od_ref[l] += l_dn[l].astype(F32)
        landed(4 * l + 2, l_out.at[l])
        oo_ref[l] += l_out[l].astype(F32)
        landed(4 * l + 3, l_qkv.at[l])
        oq_ref[l] += l_qkv[l, :, :q_w].astype(F32)
        ok_ref[l] += l_qkv[l, :, q_w : q_w + k_w].astype(F32)
        ov_ref[l] += l_qkv[l, :, q_w + k_w :].astype(F32)

    gains[...] = jnp.zeros_like(gains)

    xs_s[0] = x_ref[...]
    start_gather(0, rms_forward(x_ref[...], ig_ref[0:1, :])[0].astype(BF16))
    top = layers - 1
    for l in range(layers):
        if l == 0:
            for i in range(3):
                loads[i].wait()
        else:
            others(lambda d, s: mlp_forward(l - 1, s))
            for i in range(3):
                loads[7 * l + i].wait()
        forward(l)
        if l == 0:
            start_gather(2 * layers + top, go_ref[...].astype(BF16))
        wait_block(l, 0)
        qkv(l, c)

        def arrive(d, s):
            wait_block(l, d)
            qkv(l, s)

        others(arrive)
        attend_block(l, c)
        loads[7 * l + 3].wait()
        out_partial(l)
        start_sum(l)
        if l == 0:
            forward(2 * layers + top)
        others(lambda d, s: attend_block(l, s))
        mixed = xs_s[l] + finish_sum(l)
        mixed_s[l] = mixed
        g = layers + l
        start_gather(g, rms_forward(mixed, pg_ref[l : l + 1, :])[0].astype(BF16))
        for i in range(4, 7):
            loads[7 * l + i].wait()
        wait_block(g, 0)
        mlp_forward(l, c)
        if l < top:
            down_partial(l)
            start_sum(layers + l)
            forward(g)
            x_next = mixed_s[l] + finish_sum(layers + l)
            xs_s[l + 1] = x_next
            start_gather(l + 1, rms_forward(x_next, ig_ref[l + 1 : l + 2, :])[0].astype(BF16))
            for d in range(1, n_ctx):
                wait_block(g, d)

    for l in reversed(range(layers)):
        g = 2 * layers + l
        wait_block(g, 0)
        mlp_backward(l, c)
        mlp_back_partial(l)
        start_sum(2 * layers + l)
        if l == top:
            down_partial(l)
            start_sum(layers + l)
            forward(layers + l)
        else:
            forward(g)
        grad_res = go_ref[...] if l == top else gm_s[1]
        _, normed, inverse = rms_forward(mixed_s[l], pg_ref[l : l + 1, :])
        total = finish_sum(2 * layers + l)
        gains[layers + l : layers + l + 1, :] = jnp.sum(total * normed, axis=0, keepdims=True)
        grad_mixed = grad_res + rms_backward(total, normed, inverse, pg_ref[l : l + 1, :])
        gm_s[0] = grad_mixed
        start_gather(3 * layers + l, grad_mixed.astype(BF16))

        for d in range(1, n_ctx):
            if l == top:
                wait_block(layers + l, d)
            wait_block(g, d)

        def rest(d, s):
            if l == top:
                mlp_forward(l, s)
            mlp_backward(l, s)

        others(rest)
        forward(3 * layers + l)
        grads_mlp(l)
        if l == top:
            y_ref[...] = mixed_s[l] + finish_sum(layers + l)
        wait_block(3 * layers + l, 0)
        heads_back(l, c)

        def arrive_back(d, s):
            wait_block(3 * layers + l, d)
            heads_back(l, s)

        others(arrive_back)
        attend_backward(l)
        qkv_back_partial(l)
        start_sum(3 * layers + l)
        grads_out(l)
        grads_qkv(l)
        if l < top:
            settle(l + 1)
        _, normed, inverse = rms_forward(xs_s[l], ig_ref[l : l + 1, :])
        total = finish_sum(3 * layers + l)
        gains[l : l + 1, :] = jnp.sum(total * normed, axis=0, keepdims=True)
        grad_x = gm_s[0] + rms_backward(total, normed, inverse, ig_ref[l : l + 1, :])
        if l:
            gm_s[1] = grad_x
            start_gather(2 * layers + l - 1, grad_x.astype(BF16))
        else:
            gx_ref[...] = grad_x

    value = gains[...]
    base = 0
    for axis, me, peers, buf in (("dp", dp, [other], g_dp), ("ctx", c, ctx_peers, g_ctx), ("tp", t, tp_peers, g_tp)):
        n = len(peers) + 1
        buf[me] = value
        for i, peer in enumerate(peers):
            push(remote(buf.at[me], buf.at[me], a_send.at[base + i], a_recv.at[base + i], **{axis: peer}))
        if axis == "dp":
            settle(0)
        for i in range(n - 1):
            source = lax.rem(me + n - (i + 1), n)
            remote(buf.at[source], buf.at[source], a_send.at[base + i], a_recv.at[base + i], **{axis: source}).wait_recv()
        value = buf[0]
        for i in range(1, n):
            value = value + buf[i]
        base += n - 1
    gain_ref[...] = value

    for copy in pending:
        copy.wait_send()


def fused(sz, *operands):
    (layers, n_ctx, n_tp, rows, width, heads, kv_heads, head_dim, ff) = sz
    block = rows * n_tp
    length = block * n_ctx
    q_w, k_w = heads * head_dim, kv_heads * head_dim
    piece = width // (2 * n_ctx)
    vm = lambda *shape: pltpu.VMEM(shape, BF16)
    vf = lambda *shape: pltpu.VMEM(shape, F32)
    dma = pltpu.SemaphoreType.DMA
    sd = lambda *shape: jax.ShapeDtypeStruct(shape, F32)
    n_g = 4 * layers
    scratch = [
        vm(layers, width, q_w + 2 * k_w),
        vm(layers, q_w, width),
        vm(layers, width, 2 * ff),
        vm(layers, ff, width),
        vm(n_g, n_ctx, n_tp, rows, width),
        vm(n_g, n_tp, rows, width),
        vm(n_g, n_tp - 1, rows, width),
        vf(layers, heads, n_ctx, block, head_dim),
        vf(layers, kv_heads, n_ctx, block, head_dim),
        vm(layers, heads, n_ctx, block, head_dim),
        vm(layers, kv_heads, n_ctx, block, head_dim),
        vm(layers, kv_heads, n_ctx, block, head_dim),
        vm(layers, n_ctx, block, q_w),
        vm(layers, n_ctx, block, ff),
        vm(layers, n_ctx, block, ff),
        vm(layers, n_ctx, block, ff),
        vm(n_ctx, block, 2 * ff),
        vm(n_ctx, block, q_w),
        vm(n_ctx, block, q_w + 2 * k_w),
        vf(kv_heads, length, head_dim),
        vf(kv_heads, length, head_dim),
        vf(layers, rows, width),
        vf(layers, rows, width),
        vf(2, rows, width),
        vf(8, width),
        vf(2, 8, width),
        vf(n_ctx, 8, width),
        vf(n_tp, 8, width),
    ]
    for _ in range(2):
        scratch += [
            vm(layers, piece, q_w + 2 * k_w),
            vm(layers, q_w, piece),
            vm(layers, piece, 2 * ff),
            vm(layers, ff, piece),
        ]
    scratch += [
        dma((7 * layers,)),
        dma((n_g, n_ctx - 1)),
        dma((n_g, n_ctx - 1)),
        dma((n_g, n_ctx, n_tp - 1)),
        dma((n_g, n_ctx, n_tp - 1)),
        dma((n_g, n_tp - 1)),
        dma((n_g, n_tp - 1)),
        dma((4 * layers,)),
        dma((4 * layers,)),
        dma((n_ctx + n_tp - 1,)),
        dma((n_ctx + n_tp - 1,)),
    ]
    vmem = pl.BlockSpec(memory_space=pltpu.VMEM)
    hbm = pl.BlockSpec(memory_space=pl.ANY)
    return pl.pallas_call(
        functools.partial(fused_kernel, sz),
        out_shape=[
            sd(rows, width),
            sd(rows, width),
            sd(8, width),
            sd(layers, piece, q_w),
            sd(layers, piece, k_w),
            sd(layers, piece, k_w),
            sd(layers, q_w, piece),
            sd(layers, piece, ff),
            sd(layers, piece, ff),
            sd(layers, ff, piece),
        ],
        in_specs=[vmem] * 8 + [hbm] * 7,
        out_specs=[vmem] * 10,
        scratch_shapes=scratch,
        name="two_layers",
        compiler_params=pltpu.CompilerParams(
            collective_id=6, has_side_effects=True, vmem_limit_bytes=60 * 2**20
        ),
    )(*operands)


def on_device_fused(
    block_input,
    input_gain,
    query_weight,
    key_weight,
    value_weight,
    query_gain,
    key_gain,
    out_weight,
    post_gain,
    gate_weight,
    up_weight,
    down_weight,
    grad_output,
):
    rows, _, width = block_input.shape
    layers = input_gain.shape[0]
    head_dim = query_gain.shape[-1]
    n_ctx, n_tp = lax.axis_size("ctx"), lax.axis_size("tp")
    sz = (
        layers,
        n_ctx,
        n_tp,
        rows,
        width,
        query_weight.shape[-1] // head_dim,
        key_weight.shape[-1] // head_dim,
        head_dim,
        gate_weight.shape[-1],
    )
    cosine, sine = rope_constants(rows * n_tp * n_ctx, head_dim)
    y, gx, gains, wq, wk, wv, wo, wg, wu, wd = fused(
        sz,
        block_input[:, 0],
        grad_output[:, 0],
        input_gain,
        post_gain,
        query_gain,
        key_gain,
        cosine,
        sine,
        query_weight,
        key_weight,
        value_weight,
        out_weight,
        gate_weight,
        up_weight,
        down_weight,
    )
    head_gains = gains[2 * layers, : 2 * layers * head_dim].reshape(layers, 2, head_dim)
    return (
        y[:, None],
        gx[:, None],
        gains[:layers],
        wq,
        wk,
        wv,
        head_gains[:, 0],
        head_gains[:, 1],
        wo,
        gains[layers : 2 * layers],
        wg,
        wu,
        wd,
    )


def on_any_device(*arrays):
    rows, _, width = arrays[0].shape
    n_ctx, n_tp = lax.axis_size("ctx"), lax.axis_size("tp")
    small = rows * n_tp * n_ctx <= 512 and (width // (2 * n_ctx)) % 128 == 0
    return (on_device_fused if small else on_device)(*arrays)


def solution(mesh):
    placed = (
        P(("ctx", "tp"), "dp", None),
        P(),
        P(None, None, "tp"),
        P(None, None, "tp"),
        P(None, None, "tp"),
        P(),
        P(),
        P(None, "tp", None),
        P(),
        P(None, None, "tp"),
        P(None, None, "tp"),
        P(None, "tp", None),
        P(("ctx", "tp"), "dp", None),
    )
    return jax.shard_map(
        on_any_device,
        mesh=mesh,
        in_specs=placed,
        out_specs=(
            P(("ctx", "tp"), "dp", None),
            P(("ctx", "tp"), "dp", None),
            P(),
            P(None, ("dp", "ctx"), "tp"),
            P(None, ("dp", "ctx"), "tp"),
            P(None, ("dp", "ctx"), "tp"),
            P(),
            P(),
            P(None, "tp", ("dp", "ctx")),
            P(),
            P(None, ("dp", "ctx"), "tp"),
            P(None, ("dp", "ctx"), "tp"),
            P(None, "tp", ("dp", "ctx")),
        ),
        check_vma=False,
    )
```

```python
import functools

import jax
import jax.numpy as jnp
import numpy as np
from jax import lax
from jax.experimental import pallas as pl
from jax.experimental.pallas import tpu as pltpu
from jax.sharding import PartitionSpec as P

EPS = 1e-06
THETA = 1000000.0
MESH = pl.DeviceIdType.MESH
F32 = jnp.float32
BF16 = jnp.bfloat16


def rms_forward(field, gain):
    inverse = lax.rsqrt(jnp.mean(field * field, axis=-1, keepdims=True) + EPS)
    normed = field * inverse
    return (normed * gain, normed, inverse)


def rms_backward(grad_out, normed, inverse, gain):
    scaled = grad_out * gain
    return inverse * (scaled - normed * jnp.mean(scaled * normed, axis=-1, keepdims=True))


def rope_tables(positions, head_dim):
    half = head_dim // 2
    frequency = THETA ** (-(2.0 * jnp.arange(half, dtype=F32)) / head_dim)
    angles = positions[:, None] * frequency[None, :]
    cosine, sine = jnp.cos(angles), jnp.sin(angles)
    return (jnp.concatenate([cosine, cosine], axis=-1), jnp.concatenate([-sine, sine], axis=-1))


def remote(src, dst, send, recv, **where):
    return pltpu.make_async_remote_copy(
        src_ref=src,
        dst_ref=dst,
        send_sem=send,
        recv_sem=recv,
        device_id=where,
        device_id_type=MESH,
    )


def boundary_kernel(mode, n_ctx, n_tp, *refs):
    refs = list(refs)
    has_sum = mode != "first"
    has_gather = mode in ("first", "fwd", "bwd")
    partial = refs.pop(0) if has_sum else None
    stream = refs.pop(0)
    gain = refs.pop(0) if mode not in ("fwd_last",) else None
    grad_res = refs.pop(0) if mode in ("bwd", "bwd_last") else None
    fresh = refs.pop(0) if mode != "first" else None
    gain_part = refs.pop(0) if mode in ("bwd", "bwd_last") else None
    out = refs.pop(0) if has_gather else None
    if has_sum:
        landed, rs_send, rs_recv = refs.pop(0), refs.pop(0), refs.pop(0)
    if has_gather:
        own, z_send, z_recv, t_send, t_recv = refs

    me_c = lax.axis_index("ctx")
    me_t = lax.axis_index("tp")
    tp_peers = [lax.rem(me_t + d, n_tp) for d in range(1, n_tp)]
    ctx_peers = [lax.rem(me_c + d, n_ctx) for d in range(1, n_ctx)] if has_gather else []
    barrier = pltpu.get_barrier_semaphore()
    for peer in tp_peers:
        pl.semaphore_signal(barrier, inc=1, device_id={"tp": peer}, device_id_type=MESH)
    for peer in ctx_peers:
        pl.semaphore_signal(barrier, inc=1, device_id={"ctx": peer}, device_id_type=MESH)
    pl.semaphore_wait(barrier, len(tp_peers) + len(ctx_peers))

    if has_sum:
        sums = [
            remote(partial.at[peer], landed.at[d], rs_send.at[d], rs_recv.at[d], tp=peer)
            for d, peer in enumerate(tp_peers)
        ]
        for copy in sums:
            copy.start()
        total = partial[me_t].astype(F32)
        for d, copy in enumerate(sums):
            copy.wait_recv()
            total = total + landed[d].astype(F32)
        for copy in sums:
            copy.wait_send()

    field = stream[...]
    if mode == "first":
        sent = rms_forward(field, gain[...])[0].astype(BF16)
    elif mode in ("fwd", "fwd_last"):
        field = field + total
        fresh[...] = field
        if mode == "fwd":
            sent = rms_forward(field, gain[...])[0].astype(BF16)
    else:
        _, normed, inverse = rms_forward(field, gain[...])
        gain_part[...] = jnp.sum(total * normed, axis=0, keepdims=True)
        field = grad_res[...] + rms_backward(total, normed, inverse, gain[...])
        fresh[...] = field
        sent = field.astype(BF16)

    if has_gather:
        own[...] = sent
        copies = []
        for d, peer in enumerate(ctx_peers):
            copies.append(
                remote(own, out.at[me_c, me_t], z_send.at[d], z_recv.at[d], ctx=peer)
            )
        for d, peer in enumerate(tp_peers):
            copies.append(
                remote(own, out.at[me_c, me_t], t_send.at[0, d], t_recv.at[0, d], tp=peer)
            )
        for copy in copies:
            copy.start()
        out[me_c, me_t] = sent
        for d in range(n_ctx - 1):
            source = lax.rem(me_c + n_ctx - (d + 1), n_ctx)
            slot = out.at[source, me_t]
            remote(own, slot, z_send.at[d], z_recv.at[d], ctx=source).wait_recv()
            for k, peer in enumerate(tp_peers):
                copy = remote(slot, slot, t_send.at[d + 1, k], t_recv.at[d + 1, k], tp=peer)
                copy.start()
                copies.append(copy)
        for d in range(n_ctx):
            source = lax.rem(me_c + n_ctx - d, n_ctx)
            for k in range(n_tp - 1):
                origin = lax.rem(me_t + n_tp - (k + 1), n_tp)
                remote(
                    own, out.at[source, origin], t_send.at[d, k], t_recv.at[d, k], tp=origin
                ).wait_recv()
        for copy in copies:
            copy.wait_send()


IDS = {"first": 0, "fwd": 1, "fwd_last": 2, "bwd": 3, "bwd_last": 4}


def boundary(mode, stream, gain=None, partial=None, grad_res=None):
    n_ctx, n_tp = lax.axis_size("ctx"), lax.axis_size("tp")
    rows, width = stream.shape
    operands = []
    if partial is not None:
        operands.append(partial.reshape(n_tp, rows, width))
    operands.append(stream)
    if gain is not None:
        operands.append(gain.reshape(1, width))
    if grad_res is not None:
        operands.append(grad_res)
    shapes = []
    if mode != "first":
        shapes.append(jax.ShapeDtypeStruct((rows, width), F32))
    if grad_res is not None:
        shapes.append(jax.ShapeDtypeStruct((1, width), F32))
    scratch = []
    dma = pltpu.SemaphoreType.DMA
    if partial is not None:
        scratch += [pltpu.VMEM((n_tp - 1, rows, width), BF16), dma((n_tp - 1,)), dma((n_tp - 1,))]
    if mode in ("first", "fwd", "bwd"):
        shapes.append(jax.ShapeDtypeStruct((n_ctx, n_tp, rows, width), BF16))
        scratch += [
            pltpu.VMEM((rows, width), BF16),
            dma((n_ctx - 1,)),
            dma((n_ctx - 1,)),
            dma((n_ctx, n_tp - 1)),
            dma((n_ctx, n_tp - 1)),
        ]
    vmem = pl.BlockSpec(memory_space=pltpu.VMEM)
    outs = pl.pallas_call(
        functools.partial(boundary_kernel, mode, n_ctx, n_tp),
        out_shape=shapes,
        in_specs=[vmem] * len(operands),
        out_specs=[vmem] * len(shapes),
        scratch_shapes=scratch,
        name="boundary_" + mode,
        compiler_params=pltpu.CompilerParams(
            collective_id=IDS[mode], has_side_effects=True, vmem_limit_bytes=32 * 2**20
        ),
    )(*operands)
    outs = list(outs)
    if mode in ("first", "fwd", "bwd"):
        outs[-1] = outs[-1].reshape(n_ctx * n_tp * rows, width)
    return outs


def gains_kernel(sizes, x_ref, o_ref, cur, land_0, land_1, land_2, send, recv):
    lands = (land_0, land_1, land_2)
    axes = list(sizes)
    barrier = pltpu.get_barrier_semaphore()
    peers = {}
    count = 0
    for axis in axes:
        me = lax.axis_index(axis)
        peers[axis] = [lax.rem(me + d, sizes[axis]) for d in range(1, sizes[axis])]
        for peer in peers[axis]:
            pl.semaphore_signal(barrier, inc=1, device_id={axis: peer}, device_id_type=MESH)
            count += 1
    pl.semaphore_wait(barrier, count)
    total = x_ref[...]
    base = 0
    for step, axis in enumerate(axes):
        cur[step] = total
        copies = [
            remote(
                cur.at[step], lands[step].at[d], send.at[base + d], recv.at[base + d], **{axis: peer}
            )
            for d, peer in enumerate(peers[axis])
        ]
        for copy in copies:
            copy.start()
        me = lax.axis_index(axis)
        parts = []
        for d, copy in enumerate(copies):
            copy.wait_recv()
        acc = jnp.zeros_like(total)
        for position in range(sizes[axis]):
            offset = lax.rem(me + sizes[axis] - position, sizes[axis])
            slot = jnp.maximum(offset - 1, 0)
            acc = acc + jnp.where(offset == 0, total, lands[step][slot])
        total = acc
        for copy in copies:
            copy.wait_send()
        base += len(copies)
    o_ref[...] = total


def sum_gains(x):
    sizes = {axis: lax.axis_size(axis) for axis in ("dp", "ctx", "tp")}
    count = sum(n - 1 for n in sizes.values())
    vmem = pl.BlockSpec(memory_space=pltpu.VMEM)
    return pl.pallas_call(
        functools.partial(gains_kernel, sizes),
        out_shape=jax.ShapeDtypeStruct(x.shape, F32),
        in_specs=[vmem],
        out_specs=vmem,
        scratch_shapes=[pltpu.VMEM((3,) + x.shape, F32)]
        + [pltpu.VMEM((max(n - 1, 1),) + x.shape, F32) for n in sizes.values()]
        + [pltpu.SemaphoreType.DMA((count,)), pltpu.SemaphoreType.DMA((count,))],
        name="sum_gains",
        compiler_params=pltpu.CompilerParams(collective_id=5, has_side_effects=True),
    )(x)


NT = (((1,), (1,)), ((), ()))
NN = (((1,), (0,)), ((), ()))
TN = (((0,), (0,)), ((), ()))


def dot(a, b, dims):
    return lax.dot_general(a, b, dims, preferred_element_type=F32)


def turn(x):
    return pltpu.roll(x, x.shape[-1] // 2, axis=1)


def prepared(x, gain, cosine, sine):
    normed, plain, inverse = rms_forward(x, gain)
    return (normed * cosine + turn(normed) * sine).astype(BF16), plain, inverse


def soft_weights(scale, bq, q, k):
    rows = pl.program_id(2) * bq + lax.broadcasted_iota(jnp.int32, (bq, k.shape[0]), 0)
    cols = lax.broadcasted_iota(jnp.int32, (bq, k.shape[0]), 1)
    scores = jnp.where(cols <= rows, dot(q, k, NT) * scale, -jnp.inf)
    weights = jnp.exp(scores - jnp.max(scores, axis=-1, keepdims=True))
    return weights, jnp.sum(weights, axis=-1, keepdims=True)


def attend_kernel(
    scale, bq, q_ref, k_ref, v_ref, cq_ref, sq_ref, ck_ref, sk_ref, qg_ref, kg_ref, o_ref, k_rot
):
    @pl.when((pl.program_id(1) == 0) & (pl.program_id(2) == 0))
    def _():
        k_rot[...] = prepared(k_ref[...], kg_ref[...], ck_ref[...], sk_ref[...])[0]

    q = prepared(q_ref[...], qg_ref[...], cq_ref[...], sq_ref[...])[0]
    weights, total = soft_weights(scale, bq, q, k_rot[...])
    o_ref[...] = (dot(weights.astype(BF16), v_ref[...], NN) / total).astype(BF16)


def attend_back_kernel(
    scale,
    bq,
    q_ref,
    k_ref,
    v_ref,
    cq_ref,
    sq_ref,
    ck_ref,
    sk_ref,
    qg_ref,
    kg_ref,
    o_ref,
    do_ref,
    dq_ref,
    dk_ref,
    dv_ref,
    qp_ref,
    kp_ref,
    k_rot,
    dk_sum,
    dv_sum,
):
    head, member, block = pl.program_id(0), pl.program_id(1), pl.program_id(2)

    @pl.when((head == 0) & (member == 0) & (block == 0))
    def _():
        qp_ref[...] = jnp.zeros_like(qp_ref)
        kp_ref[...] = jnp.zeros_like(kp_ref)

    @pl.when((member == 0) & (block == 0))
    def _():
        k_rot[...] = prepared(k_ref[...], kg_ref[...], ck_ref[...], sk_ref[...])[0]
        dk_sum[...] = jnp.zeros_like(dk_sum)
        dv_sum[...] = jnp.zeros_like(dv_sum)

    q, plain, inverse = prepared(q_ref[...], qg_ref[...], cq_ref[...], sq_ref[...])
    k, do = k_rot[...], do_ref[...]
    weights, total = soft_weights(scale, bq, q, k)
    probs = weights / total
    delta = jnp.sum(do.astype(F32) * o_ref[...].astype(F32), axis=-1, keepdims=True)
    dscore = (probs * (dot(do, v_ref[...], NT) - delta)).astype(BF16)
    dk_sum[...] += dot(dscore, q, TN) * scale
    dv_sum[...] += dot(probs.astype(BF16), do, TN)
    grad = dot(dscore, k, NN) * scale
    grad = grad * cq_ref[...] - turn(grad) * sq_ref[...]
    qp_ref[...] += jnp.sum(grad * plain, axis=0, keepdims=True)
    dq_ref[...] = rms_backward(grad, plain, inverse, qg_ref[...]).astype(BF16)

    @pl.when((member == pl.num_programs(1) - 1) & (block == pl.num_programs(2) - 1))
    def _():
        _, k_plain, k_inverse = prepared(k_ref[...], kg_ref[...], ck_ref[...], sk_ref[...])
        grad_k = dk_sum[...]
        grad_k = grad_k * ck_ref[...] - turn(grad_k) * sk_ref[...]
        kp_ref[...] += jnp.sum(grad_k * k_plain, axis=0, keepdims=True)
        dk_ref[...] = rms_backward(grad_k, k_plain, k_inverse, kg_ref[...]).astype(BF16)
        dv_ref[...] = dv_sum[...].astype(BF16)


def attention(scale, group, query, keys, values, cosine, sine, query_gain, key_gain, *back):
    length, kv_width = keys.shape
    head_dim = cosine.shape[-1]
    kv_heads = kv_width // head_dim
    bq = min(length, 256)
    rows = pl.BlockSpec((bq, head_dim), lambda h, g, i: (i, h * group + g))
    keyed = pl.BlockSpec((length, head_dim), lambda h, g, i: (0, h))
    table_q = pl.BlockSpec((bq, head_dim), lambda h, g, i: (i, 0))
    table_k = pl.BlockSpec((length, head_dim), lambda h, g, i: (0, 0))
    flat = pl.BlockSpec((1, head_dim), lambda h, g, i: (0, 0))
    wide = jax.ShapeDtypeStruct((length, kv_width * group), BF16)
    narrow = jax.ShapeDtypeStruct((length, kv_width), BF16)
    part = jax.ShapeDtypeStruct((1, head_dim), F32)
    work = 2 * length * length * head_dim * kv_heads * group
    scratch = [pltpu.VMEM((length, head_dim), BF16)]
    if back:
        scratch += [pltpu.VMEM((length, head_dim), F32)] * 2
    return pl.pallas_call(
        functools.partial(attend_back_kernel if back else attend_kernel, scale, bq),
        grid=(kv_heads, group, length // bq),
        out_shape=(wide, narrow, narrow, part, part) if back else wide,
        in_specs=[rows, keyed, keyed, table_q, table_q, table_k, table_k, flat, flat]
        + [rows] * len(back),
        out_specs=(rows, keyed, keyed, flat, flat) if back else rows,
        scratch_shapes=scratch,
        name="attend_back" if back else "attend",
        cost_estimate=pl.CostEstimate(
            flops=work * (5 if back else 2), bytes_accessed=4 * length * 1024, transcendentals=0
        ),
        compiler_params=pltpu.CompilerParams(vmem_limit_bytes=40 * 2**20),
    )(
        query,
        keys,
        values,
        cosine,
        sine,
        cosine,
        sine,
        query_gain.reshape(1, -1),
        key_gain.reshape(1, -1),
        *back,
    )


def on_device(
    block_input,
    input_gain,
    query_weight,
    key_weight,
    value_weight,
    query_gain,
    key_gain,
    out_weight,
    post_gain,
    gate_weight,
    up_weight,
    down_weight,
    grad_output,
):
    local_rows, seq_local, width = block_input.shape
    assert seq_local == 1 and lax.axis_size("dp") == 2
    layers = input_gain.shape[0]
    head_dim = query_gain.shape[-1]
    heads = query_weight.shape[-1] // head_dim
    kv_heads = key_weight.shape[-1] // head_dim
    n_ctx, n_tp = lax.axis_size("ctx"), lax.axis_size("tp")
    block_rows = local_rows * n_tp
    length = block_rows * n_ctx
    scale = head_dim ** (-0.5)
    first_row = lax.axis_index("ctx") * block_rows
    cosine, sine = rope_tables(jnp.arange(length, dtype=F32), head_dim)
    piece = width // (2 * n_ctx)
    my_cols = (lax.axis_index("dp") * n_ctx + lax.axis_index("ctx")) * piece
    other_cols = ((1 - lax.axis_index("dp")) * n_ctx + lax.axis_index("ctx")) * piece
    swap = [(0, 1), (1, 0)]

    def mine(x):
        return lax.dynamic_slice_in_dim(x, first_row, block_rows, 0)

    def slices(x):
        parts = [lax.dynamic_slice_in_dim(x, at, piece, 1) for at in (my_cols, other_cols)]
        return jnp.concatenate(parts, axis=1)

    def settle(grad, axis):
        own, other = jnp.split(grad, 2, axis=axis)
        return own + lax.ppermute(other.astype(BF16), "dp", swap).astype(F32)

    def settle_rows(*products):
        other = [x[piece:].astype(BF16) for x in products]
        other = lax.ppermute(jnp.concatenate(other, axis=1), "dp", swap).astype(F32)
        out = []
        at = 0
        for x in products:
            out.append(x[:piece] + other[:, at : at + x.shape[1]])
            at += x.shape[1]
        return out

    hidden = block_input[:, 0]
    grad_hidden = grad_output[:, 0]
    grad_rows = lax.all_gather(grad_hidden.astype(BF16), ("ctx", "tp"), axis=0, tiled=True)
    (first_in,) = boundary("first", hidden, input_gain[0])
    kept = []
    for l in range(layers):
        query = dot(first_in, query_weight[l], NN)
        keys = dot(first_in, key_weight[l], NN)
        values = dot(first_in, value_weight[l], NN).astype(BF16)
        attend_args = (scale, heads // kv_heads, query, keys, values, cosine, sine)
        attend_args += (query_gain[l], key_gain[l])
        attended = attention(*attend_args)
        partial = dot(mine(attended), out_weight[l], NN).astype(BF16)
        mixed, second_in = boundary("fwd", hidden, post_gain[l], partial)
        gate = dot(second_in, gate_weight[l], NN)
        upward = dot(second_in, up_weight[l], NN)
        swish = (jax.nn.silu(gate) * upward).astype(BF16)
        partial = dot(mine(swish), down_weight[l], NN).astype(BF16)
        kept.append(
            (hidden, first_in, attend_args, attended, mixed, second_in, gate, upward, swish)
        )
        if l + 1 < layers:
            hidden, first_in = boundary("fwd", mixed, input_gain[l + 1], partial)
        else:
            hidden = mixed + lax.psum_scatter(
                partial, "tp", scatter_dimension=0, tiled=True
            ).astype(F32)

    grads = [None] * layers
    gains = [None] * layers
    for l in reversed(range(layers)):
        x_in, first_in, attend_args, attended, mixed, second_in, gate, upward, swish = kept[l]
        grad_swish = dot(grad_rows, down_weight[l], NT)
        sigma = jax.nn.sigmoid(gate)
        grad_gate = (grad_swish * upward * (sigma * (1.0 + gate * (1.0 - sigma)))).astype(BF16)
        grad_up = (grad_swish * (gate * sigma)).astype(BF16)
        partial = dot(mine(grad_gate), gate_weight[l], NT) + dot(mine(grad_up), up_weight[l], NT)
        grad_mixed, post_part, mixed_rows = boundary(
            "bwd", mixed, post_gain[l], partial.astype(BF16), grad_hidden
        )
        second_cols = slices(second_in)
        down_grad = settle(dot(swish, slices(grad_rows), TN), 1)
        gate_grad, up_grad = settle_rows(
            dot(second_cols, grad_gate, TN), dot(second_cols, grad_up, TN)
        )

        grad_heads = dot(mixed_rows, out_weight[l], NT).astype(BF16)
        out_grad = settle(dot(attended, slices(mixed_rows), TN), 1)
        query_bf, key_bf, value_bf, q_part, k_part = attention(*attend_args, attended, grad_heads)
        partial = (
            dot(mine(query_bf), query_weight[l], NT)
            + dot(mine(key_bf), key_weight[l], NT)
            + dot(mine(value_bf), value_weight[l], NT)
        ).astype(BF16)
        if l:
            grad_hidden, input_part, grad_rows = boundary(
                "bwd", x_in, input_gain[l], partial, grad_mixed
            )
        else:
            grad_hidden, input_part = boundary(
                "bwd_last", x_in, input_gain[l], partial, grad_mixed
            )
        first_cols = slices(first_in)
        query_grad, key_grad, value_grad = settle_rows(
            dot(first_cols, query_bf, TN),
            dot(first_cols, key_bf, TN),
            dot(first_cols, value_bf, TN),
        )
        grads[l] = (query_grad, key_grad, value_grad, out_grad, gate_grad, up_grad, down_grad)
        gains[l] = (input_part[0], q_part[0] / n_ctx, k_part[0] / n_ctx, post_part[0])
    stacked = [jnp.stack([part[m] for part in grads]) for m in range(7)]
    packed = jnp.concatenate([v for part in gains for v in part])
    sizes = [v.shape[0] for part in gains for v in part]
    padded = -(-packed.shape[0] // 1024) * 1024
    packed = jnp.pad(packed, (0, padded - packed.shape[0])).reshape(-1, 128)
    summed = sum_gains(packed).reshape(-1)
    pieces = []
    at = 0
    for size in sizes:
        pieces.append(summed[at : at + size])
        at += size
    gains = [jnp.stack([pieces[4 * l + m] for l in range(layers)]) for m in range(4)]
    return (
        hidden[:, None],
        grad_hidden[:, None],
        gains[0],
        stacked[0],
        stacked[1],
        stacked[2],
        gains[1],
        gains[2],
        stacked[3],
        gains[3],
        stacked[4],
        stacked[5],
        stacked[6],
    )


def rope_constants(length, head_dim):
    half = head_dim // 2
    frequency = np.float32(THETA) ** (-(np.float32(2.0) * np.arange(half, dtype=np.float32)) / np.float32(head_dim))
    angles = np.arange(length, dtype=np.float32)[:, None] * frequency.astype(np.float32)[None, :]
    cosine, sine = np.cos(angles), np.sin(angles)
    return (
        np.concatenate([cosine, cosine], axis=-1).astype(np.float32),
        np.concatenate([-sine, sine], axis=-1).astype(np.float32),
    )


def chunks(total, step=256):
    step = step if total % step == 0 else 128
    return [(at, step) for at in range(0, total, step)]


def fused_kernel(sz, *refs):
    (layers, n_ctx, n_tp, rows, width, heads, kv_heads, head_dim, ff) = sz
    block = rows * n_tp
    length = block * n_ctx
    group = heads // kv_heads
    q_w, k_w = heads * head_dim, kv_heads * head_dim
    piece = width // (2 * n_ctx)
    log2e = 1.4426950408889634
    scale = head_dim ** (-0.5)
    (x_ref, go_ref, ig_ref, pg_ref, qg_ref, kg_ref, cos_ref, sin_ref) = refs[:8]
    (wq_h, wk_h, wv_h, wo_h, wg_h, wu_h, wd_h) = refs[8:15]
    y_ref, gx_ref, gain_ref = refs[15:18]
    finals = refs[18:25]
    (wqkv, wo, wgu, wd, G, P, land, q_raw, k_raw, q_rot, k_rot, vals, att, swish, fa, fb, ggu, d_o, dqkv,
     dk_acc, dv_acc, mixed_s, xs_s, gm_s, gains, g_dp, g_ctx, g_tp,
     s_qkv, s_out, s_gu, s_dn, l_qkv, l_out, l_gu, l_dn,
     oq_ref, ok_ref, ov_ref, oo_ref, og_ref, ou_ref, od_ref, o_sem,
     w_sem, z_send, z_recv, t_send, t_recv, r_send, r_recv, d_send, d_recv, a_send, a_recv) = refs[25:]

    c, t, dp = lax.axis_index("ctx"), lax.axis_index("tp"), lax.axis_index("dp")
    tp_peers = [lax.rem(t + k, n_tp) for k in range(1, n_tp)]
    ctx_peers = [lax.rem(c + d, n_ctx) for d in range(1, n_ctx)]
    other = 1 - dp
    pending = []

    loads = []

    def load(src, dst):
        copy = pltpu.make_async_copy(src, dst, w_sem.at[len(loads)])
        copy.start()
        loads.append(copy)

    for l in range(layers):
        load(wk_h.at[l], wqkv.at[l, :, pl.ds(q_w, k_w)])
        load(wv_h.at[l], wqkv.at[l, :, pl.ds(q_w + k_w, k_w)])
        load(wq_h.at[l], wqkv.at[l, :, pl.ds(0, q_w)])
        load(wo_h.at[l], wo.at[l])
        load(wg_h.at[l], wgu.at[l, :, pl.ds(0, ff)])
        load(wu_h.at[l], wgu.at[l, :, pl.ds(ff, ff)])
        load(wd_h.at[l], wd.at[l])

    barrier = pltpu.get_barrier_semaphore()
    for peer in tp_peers:
        pl.semaphore_signal(barrier, inc=1, device_id={"tp": peer}, device_id_type=MESH)
    for peer in ctx_peers:
        pl.semaphore_signal(barrier, inc=1, device_id={"ctx": peer}, device_id_type=MESH)
    pl.semaphore_signal(barrier, inc=1, device_id={"dp": other}, device_id_type=MESH)
    pl.semaphore_wait(barrier, n_tp + n_ctx - 1)

    def push(copy):
        copy.start()
        pending.append(copy)

    def source_of(d):
        return lax.rem(c + n_ctx - d, n_ctx)

    def spread(g, d):
        slot = G.at[g, source_of(d), t]
        for k, peer in enumerate(tp_peers):
            push(remote(slot, slot, t_send.at[g, d, k], t_recv.at[g, d, k], tp=peer))

    def complete(g, d):
        for k in range(n_tp - 1):
            origin = lax.rem(t + n_tp - (k + 1), n_tp)
            slot = G.at[g, source_of(d), origin]
            remote(slot, slot, t_send.at[g, d, k], t_recv.at[g, d, k], tp=origin).wait_recv()

    def start_gather(g, value):
        own = G.at[g, c, t]
        G[g, c, t] = value
        for d, peer in enumerate(ctx_peers):
            push(remote(own, own, z_send.at[g, d], z_recv.at[g, d], ctx=peer))
        spread(g, 0)

    def late_spread(g, *steps):
        for d in steps:
            source = source_of(d)
            slot = G.at[g, source, t]
            remote(slot, slot, z_send.at[g, d - 1], z_recv.at[g, d - 1], ctx=source).wait_recv()
            spread(g, d)

    def full_gather(g, work, early=None):
        if early is not None:
            early()
        late_spread(g, 1)
        complete(g, 0)
        work(c)
        late_spread(g, 2, 3)
        for d in range(1, n_ctx):
            complete(g, d)
            work(source_of(d))

    def late_complete(g):
        for d in range(1, n_ctx):
            complete(g, d)

    def start_sum(r):
        for k, peer in enumerate(tp_peers):
            push(remote(P.at[r, peer], land.at[r, k], r_send.at[r, k], r_recv.at[r, k], tp=peer))

    def finish_sum(r):
        total = P[r, t].astype(F32)
        for k in range(n_tp - 1):
            remote(P.at[r, t], land.at[r, k], r_send.at[r, k], r_recv.at[r, k], tp=t).wait_recv()
            total = total + land[r, k].astype(F32)
        return total

    def others(body):
        def step(d, carry):
            body(d, lax.rem(c + n_ctx - d, n_ctx))
            return carry

        lax.fori_loop(1, n_ctx, step, 0)

    def tokens(g, s):
        return G[g, s].reshape(block, width)

    def put_partial(r, at, step, value):
        P[r, :, :, at : at + step] = value.astype(BF16).reshape(n_tp, rows, step)

    def qkv(l, s):
        x = tokens(l, s)
        cosine = cos_ref[pl.ds(pl.multiple_of(s * block, block), block), :]
        sine = sin_ref[pl.ds(pl.multiple_of(s * block, block), block), :]
        qg, kg = qg_ref[l : l + 1, :], kg_ref[l : l + 1, :]
        for at, step in chunks(q_w + 2 * k_w):
            y = dot(x, wqkv[l, :, at : at + step], NN)
            for sub in range(0, step, head_dim):
                yh = y[:, sub : sub + head_dim]
                h = (at + sub) // head_dim
                if h < heads:
                    q_raw[l, h, s] = yh
                    q_rot[l, h, s] = prepared(yh, qg, cosine, sine)[0]
                elif h < heads + kv_heads:
                    k_raw[l, h - heads, s] = yh
                    k_rot[l, h - heads, s] = prepared(yh, kg, cosine, sine)[0]
                else:
                    vals[l, h - heads - kv_heads, s] = yh.astype(BF16)

    def attend_block(l, i):
        at_row = i * block + lax.broadcasted_iota(jnp.int32, (block, length), 0)
        allowed = lax.broadcasted_iota(jnp.int32, (block, length), 1) <= at_row
        for h in range(heads):
            k = k_rot[l, h // group].reshape(length, head_dim)
            v = vals[l, h // group].reshape(length, head_dim)
            scores = dot(q_rot[l, h, i], k, NT) * (scale * log2e)
            weights = jnp.where(allowed, jnp.exp2(scores), 0.0)
            total = jnp.sum(weights, axis=-1, keepdims=True)
            out = dot(weights.astype(BF16), v, NN) / total
            att[l, i, :, h * head_dim : (h + 1) * head_dim] = out.astype(BF16)

    def out_partial(l):
        a = att[l, c]
        for at, step in chunks(width):
            put_partial(l, at, step, dot(a, wo[l, :, at : at + step], NN))

    def mlp_forward(l, s):
        x = tokens(layers + l, s)
        for at, step in chunks(ff):
            gate = dot(x, wgu[l, :, at : at + step], NN)
            up = dot(x, wgu[l, :, ff + at : ff + at + step], NN)
            sigma = jax.nn.sigmoid(gate)
            silu = gate * sigma
            swish[l, s, :, at : at + step] = (silu * up).astype(BF16)
            fa[l, s, :, at : at + step] = (up * (sigma * (1.0 + gate * (1.0 - sigma)))).astype(BF16)
            fb[l, s, :, at : at + step] = silu.astype(BF16)

    def down_partial(l):
        a = swish[l, c]
        for at, step in chunks(width):
            put_partial(layers + l, at, step, dot(a, wd[l, :, at : at + step], NN))

    def mlp_backward(l, s):
        x = tokens(2 * layers + l, s)
        for at, step in chunks(ff):
            grad = dot(x, wd[l, at : at + step, :], NT)
            ggu[l, s, :, at : at + step] = (grad * fa[l, s, :, at : at + step].astype(F32)).astype(BF16)
            ggu[l, s, :, ff + at : ff + at + step] = (
                grad * fb[l, s, :, at : at + step].astype(F32)
            ).astype(BF16)

    def mlp_back_partial(l):
        a = ggu[l, c]
        for at, step in chunks(width):
            put_partial(2 * layers + l, at, step, dot(a, wgu[l, at : at + step, :], NT))

    def heads_back(l, s):
        x = tokens(3 * layers + l, s)
        for at, step in chunks(q_w):
            d_o[s, :, at : at + step] = dot(x, wo[l, at : at + step, :], NT).astype(BF16)

    def attend_backward(l):
        dk_acc[...] = jnp.zeros_like(dk_acc)
        dv_acc[...] = jnp.zeros_like(dv_acc)
        half = length // 2
        per = n_ctx // 2
        causal = lax.broadcasted_iota(jnp.int32, (half, half), 1) <= lax.broadcasted_iota(
            jnp.int32, (half, half), 0
        )
        qg, kg = qg_ref[l : l + 1, :], kg_ref[l : l + 1, :]

        def one_head(h, part):
            lanes = pl.ds(pl.multiple_of(h * head_dim, head_dim), head_dim)
            kv = h // group
            for i in range(2):
                span = slice(i * per, (i + 1) * per)
                extent = (i + 1) * half
                q = q_rot[l, h, span].reshape(half, head_dim)
                do = d_o[span, :, lanes].reshape(half, head_dim)
                a = att[l, span, :, lanes].reshape(half, head_dim)
                k = k_rot[l, kv, : (i + 1) * per].reshape(extent, head_dim)
                v = vals[l, kv, : (i + 1) * per].reshape(extent, head_dim)
                weights = jnp.exp2(dot(q, k, NT) * (scale * log2e))
                last = jnp.where(causal, weights[:, i * half :], 0.0)
                weights = jnp.concatenate([weights[:, :half], last], axis=1) if i else last
                probs = weights / jnp.sum(weights, axis=-1, keepdims=True)
                delta = jnp.sum(do.astype(F32) * a.astype(F32), axis=-1, keepdims=True)
                dscore = (probs * (dot(do, v, NT) - delta)).astype(BF16)
                dk_acc[kv, :extent] += dot(dscore, q, TN)
                dv_acc[kv, :extent] += dot(probs.astype(BF16), do, TN)
                cosine = cos_ref[i * half : (i + 1) * half, :]
                sine = sin_ref[i * half : (i + 1) * half, :]
                grad = dot(dscore, k, NN) * scale
                grad = grad * cosine - turn(grad) * sine
                _, plain, inverse = rms_forward(q_raw[l, h, span].reshape(half, head_dim), qg)
                part = part + jnp.sum(grad * plain, axis=0, keepdims=True)
                grad = rms_backward(grad, plain, inverse, qg).astype(BF16)
                dqkv[span, :, lanes] = grad.reshape(per, block, head_dim)
            return part

        q_part = lax.fori_loop(0, heads, one_head, jnp.zeros((1, head_dim), F32))
        k_part = jnp.zeros((1, head_dim), F32)
        for kv in range(kv_heads):
            grad = dk_acc[kv] * scale
            grad = grad * cos_ref[...] - turn(grad) * sin_ref[...]
            _, plain, inverse = rms_forward(k_raw[l, kv].reshape(length, head_dim), kg)
            k_part = k_part + jnp.sum(grad * plain, axis=0, keepdims=True)
            grad = rms_backward(grad, plain, inverse, kg).astype(BF16)
            at = q_w + kv * head_dim
            dqkv[:, :, at : at + head_dim] = grad.reshape(n_ctx, block, head_dim)
            at += k_w
            dqkv[:, :, at : at + head_dim] = dv_acc[kv].astype(BF16).reshape(n_ctx, block, head_dim)
        at = 2 * layers
        gains[at : at + 1, 2 * l * head_dim : (2 * l + 1) * head_dim] = q_part / n_ctx
        gains[at : at + 1, (2 * l + 1) * head_dim : (2 * l + 2) * head_dim] = k_part / n_ctx

    def qkv_back_partial(l):
        a = dqkv[c]
        for at, step in chunks(width):
            put_partial(3 * layers + l, at, step, dot(a, wqkv[l, at : at + step, :], NT))

    my_cols = pl.ds(pl.multiple_of((dp * n_ctx + c) * piece, piece), piece)
    other_cols = pl.ds(pl.multiple_of((other * n_ctx + c) * piece, piece), piece)

    def columns(g):
        parts = [G[g, :, :, :, cols].reshape(length, piece) for cols in (my_cols, other_cols)]
        return jnp.concatenate(parts, axis=1)

    def exchange(i, src, dst):
        push(remote(src, dst, d_send.at[i], d_recv.at[i], dp=other))

    def grads_mlp(l):
        x = columns(layers + l)
        for at, step in chunks(2 * ff):
            g = dot(x, ggu[l, :, :, at : at + step].reshape(length, step), TN)
            ref, base = (og_ref, at) if at < ff else (ou_ref, at - ff)
            ref[l, :, base : base + step] = g[:piece]
            s_gu[l, :, at : at + step] = g[piece:].astype(BF16)
        exchange(4 * l, s_gu.at[l], l_gu.at[l])
        x = columns(2 * layers + l)
        for at, step in chunks(ff):
            g = dot(swish[l, :, :, at : at + step].reshape(length, step), x, TN)
            od_ref[l, at : at + step, :] = g[:, :piece]
            s_dn[l, at : at + step, :] = g[:, piece:].astype(BF16)
        exchange(4 * l + 1, s_dn.at[l], l_dn.at[l])

    def grads_out(l):
        x = columns(3 * layers + l)
        for at, step in chunks(q_w):
            g = dot(att[l, :, :, at : at + step].reshape(length, step), x, TN)
            oo_ref[l, at : at + step, :] = g[:, :piece]
            s_out[l, at : at + step, :] = g[:, piece:].astype(BF16)
        exchange(4 * l + 2, s_out.at[l], l_out.at[l])

    def grads_qkv(l):
        x = columns(l)
        for at, step in chunks(q_w + 2 * k_w):
            g = dot(x, dqkv[:, :, at : at + step].reshape(length, step), TN)
            if at < q_w:
                oq_ref[l, :, at : at + step] = g[:piece]
            elif at < q_w + k_w:
                ok_ref[l, :, at - q_w : at - q_w + step] = g[:piece]
            else:
                ov_ref[l, :, at - q_w - k_w : at - q_w - k_w + step] = g[:piece]
            s_qkv[l, :, at : at + step] = g[piece:].astype(BF16)
        exchange(4 * l + 3, s_qkv.at[l], l_qkv.at[l])

    def settle(l):
        def landed(i, dst):
            remote(dst, dst, d_send.at[i], d_recv.at[i], dp=other).wait_recv()

        landed(4 * l, l_gu.at[l])
        og_ref[l] += l_gu[l, :, :ff].astype(F32)
        ou_ref[l] += l_gu[l, :, ff:].astype(F32)
        landed(4 * l + 1, l_dn.at[l])
        od_ref[l] += l_dn[l].astype(F32)
        landed(4 * l + 2, l_out.at[l])
        oo_ref[l] += l_out[l].astype(F32)
        landed(4 * l + 3, l_qkv.at[l])
        oq_ref[l] += l_qkv[l, :, :q_w].astype(F32)
        ok_ref[l] += l_qkv[l, :, q_w : q_w + k_w].astype(F32)
        ov_ref[l] += l_qkv[l, :, q_w + k_w :].astype(F32)

    gains[...] = jnp.zeros_like(gains)

    leaving = []

    def deliver(l):
        staged = (oq_ref, ok_ref, ov_ref, oo_ref, og_ref, ou_ref, od_ref)
        for i, (src, dst) in enumerate(zip(staged, finals)):
            copy = pltpu.make_async_copy(src.at[l], dst.at[l], o_sem.at[i, l])
            copy.start()
            leaving.append(copy)

    stages = (("dp", dp, [other], g_dp, 0), ("ctx", c, ctx_peers, g_ctx, 1), ("tp", t, tp_peers, g_tp, n_ctx))

    def gain_start(stage, value):
        axis, me, peers, buf, base = stages[stage]
        buf[me] = value
        for i, peer in enumerate(peers):
            own = buf.at[me]
            push(remote(own, own, a_send.at[base + i], a_recv.at[base + i], **{axis: peer}))

    def gain_finish(stage):
        axis, me, peers, buf, base = stages[stage]
        n = len(peers) + 1
        for i in range(n - 1):
            source = lax.rem(me + n - (i + 1), n)
            slot = buf.at[source]
            remote(slot, slot, a_send.at[base + i], a_recv.at[base + i], **{axis: source}).wait_recv()
        value = buf[0]
        for i in range(1, n):
            value = value + buf[i]
        return value

    top = layers - 1
    X1, X2, GR, MR = (lambda l: l), (lambda l: layers + l), (lambda l: 2 * layers + l), (lambda l: 3 * layers + l)

    x_in = x_ref[:, 0, :]
    xs_s[0] = x_in
    start_gather(X1(0), rms_forward(x_in, ig_ref[0:1, :])[0].astype(BF16))
    for l in range(layers):
        for i in range(3):
            loads[7 * l + i].wait()
        full_gather(X1(l), lambda s: qkv(l, s))
        if l == 0:
            start_gather(GR(top), go_ref[:, 0, :].astype(BF16))
        else:
            late_spread(GR(top), 3)
        attend_block(l, c)
        loads[7 * l + 3].wait()
        out_partial(l)
        start_sum(l)
        if l:
            late_spread(X2(l - 1), 1)
        attend_block(l, source_of(1))
        attend_block(l, source_of(2))
        mixed = xs_s[l] + finish_sum(l)
        mixed_s[l] = mixed
        start_gather(X2(l), rms_forward(mixed, pg_ref[l : l + 1, :])[0].astype(BF16))
        if l == 0:
            late_spread(GR(top), 1)
        else:
            late_spread(X2(l - 1), 2)
        for i in range(4, 7):
            loads[7 * l + i].wait()
        attend_block(l, source_of(3))
        complete(X2(l), 0)
        mlp_forward(l, c)
        if l < top:
            down_partial(l)
            start_sum(layers + l)
            late_spread(GR(top), 2)
            x_next = mixed_s[l] + finish_sum(layers + l)
            xs_s[l + 1] = x_next
            start_gather(X1(l + 1), rms_forward(x_next, ig_ref[l + 1 : l + 2, :])[0].astype(BF16))

    for l in reversed(range(layers)):
        complete(GR(l), 0)
        mlp_backward(l, c)
        mlp_back_partial(l)
        start_sum(2 * layers + l)
        if l == top:
            down_partial(l)
            start_sum(layers + l)
            late_complete(GR(top))
        else:
            others(lambda d, s: mlp_backward(l + 1, s))
        grad_res = go_ref[:, 0, :] if l == top else gm_s[1]
        _, normed, inverse = rms_forward(mixed_s[l], pg_ref[l : l + 1, :])
        total = finish_sum(2 * layers + l)
        gains[layers + l : layers + l + 1, :] = jnp.sum(total * normed, axis=0, keepdims=True)
        grad_mixed = grad_res + rms_backward(total, normed, inverse, pg_ref[l : l + 1, :])
        gm_s[0] = grad_mixed
        start_gather(MR(l), grad_mixed.astype(BF16))
        if l == top:
            y_ref[...] = mixed_s[l] + finish_sum(layers + l)

        def early():
            if l < top:
                grads_mlp(l + 1)

        full_gather(MR(l), lambda s: heads_back(l, s), early)
        late_spread(X2(l) if l == top else GR(l), 1, 2, 3)
        attend_backward(l)
        qkv_back_partial(l)
        start_sum(3 * layers + l)
        if l == 0:
            plain = tokens(X1(l), c).astype(F32)
            back = P[3 * layers + l].reshape(block, width).astype(F32)
            gains[l : l + 1, :] = jnp.sum(back * plain, axis=0, keepdims=True) / ig_ref[l : l + 1, :]
            gain_start(0, gains[...])
        else:
            late_spread(X2(l - 1), 3)
        grads_out(l)
        grads_qkv(l)
        if l:
            _, normed, inverse = rms_forward(xs_s[l], ig_ref[l : l + 1, :])
            total = finish_sum(3 * layers + l)
            gains[l : l + 1, :] = jnp.sum(total * normed, axis=0, keepdims=True)
            grad_x = gm_s[0] + rms_backward(total, normed, inverse, ig_ref[l : l + 1, :])
            gm_s[1] = grad_x
            start_gather(GR(l - 1), grad_x.astype(BF16))
            for q in (l - 1, l):
                late_complete(X2(q))
                others(lambda d, s: mlp_forward(q, s))
        if l == 0:
            gain_start(1, gain_finish(0))
            late_complete(GR(l))
            others(lambda d, s: mlp_backward(l, s))
            grads_mlp(l)
            gain_start(2, gain_finish(1))
            settle(l + 1)
            deliver(l + 1)
            _, normed, inverse = rms_forward(xs_s[l], ig_ref[l : l + 1, :])
            total = finish_sum(3 * layers + l)
            gx_ref[...] = gm_s[0] + rms_backward(total, normed, inverse, ig_ref[l : l + 1, :])
            settle(l)
            deliver(l)
            gain_ref[...] = gain_finish(2)

    for copy in leaving:
        copy.wait()
    for copy in pending:
        copy.wait_send()


def fused(sz, *operands):
    (layers, n_ctx, n_tp, rows, width, heads, kv_heads, head_dim, ff) = sz
    block = rows * n_tp
    length = block * n_ctx
    q_w, k_w = heads * head_dim, kv_heads * head_dim
    piece = width // (2 * n_ctx)
    vm = lambda *shape: pltpu.VMEM(shape, BF16)
    vf = lambda *shape: pltpu.VMEM(shape, F32)
    dma = pltpu.SemaphoreType.DMA
    sd = lambda *shape: jax.ShapeDtypeStruct(shape, F32)
    n_g = 4 * layers
    scratch = [
        vm(layers, width, q_w + 2 * k_w),
        vm(layers, q_w, width),
        vm(layers, width, 2 * ff),
        vm(layers, ff, width),
        vm(n_g, n_ctx, n_tp, rows, width),
        vm(n_g, n_tp, rows, width),
        vm(n_g, n_tp - 1, rows, width),
        vf(layers, heads, n_ctx, block, head_dim),
        vf(layers, kv_heads, n_ctx, block, head_dim),
        vm(layers, heads, n_ctx, block, head_dim),
        vm(layers, kv_heads, n_ctx, block, head_dim),
        vm(layers, kv_heads, n_ctx, block, head_dim),
        vm(layers, n_ctx, block, q_w),
        vm(layers, n_ctx, block, ff),
        vm(layers, n_ctx, block, ff),
        vm(layers, n_ctx, block, ff),
        vm(layers, n_ctx, block, 2 * ff),
        vm(n_ctx, block, q_w),
        vm(n_ctx, block, q_w + 2 * k_w),
        vf(kv_heads, length, head_dim),
        vf(kv_heads, length, head_dim),
        vf(layers, rows, width),
        vf(layers, rows, width),
        vf(2, rows, width),
        vf(8, width),
        vf(2, 8, width),
        vf(n_ctx, 8, width),
        vf(n_tp, 8, width),
    ]
    outs = [
        sd(layers, piece, q_w),
        sd(layers, piece, k_w),
        sd(layers, piece, k_w),
        sd(layers, q_w, piece),
        sd(layers, piece, ff),
        sd(layers, piece, ff),
        sd(layers, ff, piece),
    ]
    for _ in range(2):
        scratch += [
            vm(layers, piece, q_w + 2 * k_w),
            vm(layers, q_w, piece),
            vm(layers, piece, 2 * ff),
            vm(layers, ff, piece),
        ]
    scratch += [pltpu.VMEM(out.shape, F32) for out in outs]
    scratch += [
        dma((7, layers)),
        dma((7 * layers,)),
        dma((n_g, n_ctx - 1)),
        dma((n_g, n_ctx - 1)),
        dma((n_g, n_ctx, n_tp - 1)),
        dma((n_g, n_ctx, n_tp - 1)),
        dma((n_g, n_tp - 1)),
        dma((n_g, n_tp - 1)),
        dma((4 * layers,)),
        dma((4 * layers,)),
        dma((n_ctx + n_tp - 1,)),
        dma((n_ctx + n_tp - 1,)),
    ]
    vmem = pl.BlockSpec(memory_space=pltpu.VMEM)
    hbm = pl.BlockSpec(memory_space=pl.ANY)
    return pl.pallas_call(
        functools.partial(fused_kernel, sz),
        out_shape=[
            sd(rows, width),
            sd(rows, width),
            sd(8, width),
        ]
        + outs,
        in_specs=[vmem] * 8 + [hbm] * 7,
        out_specs=[vmem] * 3 + [hbm] * 7,
        scratch_shapes=scratch,
        name="two_layers",
        compiler_params=pltpu.CompilerParams(
            collective_id=6, has_side_effects=True, vmem_limit_bytes=60 * 2**20
        ),
    )(*operands)


def finish_kernel(layers, head_dim, *refs):
    y_in, gx_in, gain_in = refs[:3]
    grads_in = refs[3:10]
    y, gx, input_gain, query_gain, key_gain, post_gain = refs[10:16]
    grads_out = refs[16:23]
    held = refs[23:30]
    sems_in, sems_out = refs[30:]
    arrive, leave = [], []
    for l in reversed(range(layers)):
        for i, (src, mid, dst) in enumerate(zip(grads_in, held, grads_out)):
            arrive.append(pltpu.make_async_copy(src.at[l], mid.at[l], sems_in.at[i, l]))
            leave.append(pltpu.make_async_copy(mid.at[l], dst.at[l], sems_out.at[i, l]))
    for copy in arrive:
        copy.start()
    for first, second in zip(arrive, leave):
        first.wait()
        second.start()
    y[:, 0, :] = y_in[...]
    gx[:, 0, :] = gx_in[...]
    input_gain[...] = gain_in[:layers, :]
    post_gain[...] = gain_in[layers : 2 * layers, :]
    for l in range(layers):
        at = 2 * l * head_dim
        query_gain[l : l + 1, :] = gain_in[2 * layers : 2 * layers + 1, at : at + head_dim]
        key_gain[l : l + 1, :] = gain_in[2 * layers : 2 * layers + 1, at + head_dim : at + 2 * head_dim]
    for copy in leave:
        copy.wait()


def finish(layers, head_dim, y, gx, gains, *grads):
    rows, width = y.shape
    sd = lambda *shape: jax.ShapeDtypeStruct(shape, F32)
    vmem = pl.BlockSpec(memory_space=pltpu.VMEM)
    hbm = pl.BlockSpec(memory_space=pl.ANY)
    return pl.pallas_call(
        functools.partial(finish_kernel, layers, head_dim),
        out_shape=[
            sd(rows, 1, width),
            sd(rows, 1, width),
            sd(layers, width),
            sd(layers, head_dim),
            sd(layers, head_dim),
            sd(layers, width),
        ]
        + [sd(*grad.shape) for grad in grads],
        in_specs=[vmem] * 3 + [hbm] * len(grads),
        out_specs=[vmem] * 6 + [hbm] * len(grads),
        scratch_shapes=[pltpu.VMEM(grad.shape, F32) for grad in grads]
        + [pltpu.SemaphoreType.DMA((len(grads), layers))] * 2,
        name="finish",
    )(y, gx, gains, *grads)


def on_device_fused(
    block_input,
    input_gain,
    query_weight,
    key_weight,
    value_weight,
    query_gain,
    key_gain,
    out_weight,
    post_gain,
    gate_weight,
    up_weight,
    down_weight,
    grad_output,
):
    rows, _, width = block_input.shape
    layers = input_gain.shape[0]
    head_dim = query_gain.shape[-1]
    n_ctx, n_tp = lax.axis_size("ctx"), lax.axis_size("tp")
    sz = (
        layers,
        n_ctx,
        n_tp,
        rows,
        width,
        query_weight.shape[-1] // head_dim,
        key_weight.shape[-1] // head_dim,
        head_dim,
        gate_weight.shape[-1],
    )
    cosine, sine = rope_constants(rows * n_tp * n_ctx, head_dim)
    y, gx, gains, *grads = fused(
        sz,
        block_input,
        grad_output,
        input_gain,
        post_gain,
        query_gain,
        key_gain,
        cosine,
        sine,
        query_weight,
        key_weight,
        value_weight,
        out_weight,
        gate_weight,
        up_weight,
        down_weight,
    )
    y, gx, input_part, q_part, k_part, post_part, wq, wk, wv, wo, wg, wu, wd = finish(
        layers, head_dim, y, gx, gains, *grads
    )
    return (y, gx, input_part, wq, wk, wv, q_part, k_part, wo, post_part, wg, wu, wd)


def on_any_device(*arrays):
    rows, _, width = arrays[0].shape
    n_ctx, n_tp = lax.axis_size("ctx"), lax.axis_size("tp")
    small = n_tp == 4 and n_ctx == 4 and arrays[1].shape[0] == 2 and rows * n_tp * n_ctx <= 512 and (width // (2 * n_ctx)) % 128 == 0
    return (on_device_fused if small else on_device)(*arrays)


def solution(mesh):
    placed = (
        P(("ctx", "tp"), "dp", None),
        P(),
        P(None, None, "tp"),
        P(None, None, "tp"),
        P(None, None, "tp"),
        P(),
        P(),
        P(None, "tp", None),
        P(),
        P(None, None, "tp"),
        P(None, None, "tp"),
        P(None, "tp", None),
        P(("ctx", "tp"), "dp", None),
    )
    return jax.shard_map(
        on_any_device,
        mesh=mesh,
        in_specs=placed,
        out_specs=(
            P(("ctx", "tp"), "dp", None),
            P(("ctx", "tp"), "dp", None),
            P(),
            P(None, ("dp", "ctx"), "tp"),
            P(None, ("dp", "ctx"), "tp"),
            P(None, ("dp", "ctx"), "tp"),
            P(),
            P(),
            P(None, "tp", ("dp", "ctx")),
            P(),
            P(None, ("dp", "ctx"), "tp"),
            P(None, ("dp", "ctx"), "tp"),
            P(None, "tp", ("dp", "ctx")),
        ),
        check_vma=False,
    )
```

```python
import functools

import jax
import jax.numpy as jnp
import numpy as np
from jax import lax
from jax.experimental import pallas as pl
from jax.experimental.pallas import tpu as pltpu
from jax.sharding import PartitionSpec as P

EPS = 1e-06
THETA = 1000000.0
MESH = pl.DeviceIdType.MESH
F32 = jnp.float32
BF16 = jnp.bfloat16


def rms_forward(field, gain):
    inverse = lax.rsqrt(jnp.mean(field * field, axis=-1, keepdims=True) + EPS)
    normed = field * inverse
    return (normed * gain, normed, inverse)


def rms_backward(grad_out, normed, inverse, gain):
    scaled = grad_out * gain
    return inverse * (scaled - normed * jnp.mean(scaled * normed, axis=-1, keepdims=True))


def rope_tables(positions, head_dim):
    half = head_dim // 2
    frequency = THETA ** (-(2.0 * jnp.arange(half, dtype=F32)) / head_dim)
    angles = positions[:, None] * frequency[None, :]
    cosine, sine = jnp.cos(angles), jnp.sin(angles)
    return (jnp.concatenate([cosine, cosine], axis=-1), jnp.concatenate([-sine, sine], axis=-1))


def remote(src, dst, send, recv, **where):
    return pltpu.make_async_remote_copy(
        src_ref=src,
        dst_ref=dst,
        send_sem=send,
        recv_sem=recv,
        device_id=where,
        device_id_type=MESH,
    )


def boundary_kernel(mode, n_ctx, n_tp, *refs):
    refs = list(refs)
    has_sum = mode != "first"
    has_gather = mode in ("first", "fwd", "bwd")
    partial = refs.pop(0) if has_sum else None
    stream = refs.pop(0)
    gain = refs.pop(0) if mode not in ("fwd_last",) else None
    grad_res = refs.pop(0) if mode in ("bwd", "bwd_last") else None
    fresh = refs.pop(0) if mode != "first" else None
    gain_part = refs.pop(0) if mode in ("bwd", "bwd_last") else None
    out = refs.pop(0) if has_gather else None
    if has_sum:
        landed, rs_send, rs_recv = refs.pop(0), refs.pop(0), refs.pop(0)
    if has_gather:
        own, z_send, z_recv, t_send, t_recv = refs

    me_c = lax.axis_index("ctx")
    me_t = lax.axis_index("tp")
    tp_peers = [lax.rem(me_t + d, n_tp) for d in range(1, n_tp)]
    ctx_peers = [lax.rem(me_c + d, n_ctx) for d in range(1, n_ctx)] if has_gather else []
    barrier = pltpu.get_barrier_semaphore()
    for peer in tp_peers:
        pl.semaphore_signal(barrier, inc=1, device_id={"tp": peer}, device_id_type=MESH)
    for peer in ctx_peers:
        pl.semaphore_signal(barrier, inc=1, device_id={"ctx": peer}, device_id_type=MESH)
    pl.semaphore_wait(barrier, len(tp_peers) + len(ctx_peers))

    if has_sum:
        sums = [
            remote(partial.at[peer], landed.at[d], rs_send.at[d], rs_recv.at[d], tp=peer)
            for d, peer in enumerate(tp_peers)
        ]
        for copy in sums:
            copy.start()
        total = partial[me_t].astype(F32)
        for d, copy in enumerate(sums):
            copy.wait_recv()
            total = total + landed[d].astype(F32)
        for copy in sums:
            copy.wait_send()

    field = stream[...]
    if mode == "first":
        sent = rms_forward(field, gain[...])[0].astype(BF16)
    elif mode in ("fwd", "fwd_last"):
        field = field + total
        fresh[...] = field
        if mode == "fwd":
            sent = rms_forward(field, gain[...])[0].astype(BF16)
    else:
        _, normed, inverse = rms_forward(field, gain[...])
        gain_part[...] = jnp.sum(total * normed, axis=0, keepdims=True)
        field = grad_res[...] + rms_backward(total, normed, inverse, gain[...])
        fresh[...] = field
        sent = field.astype(BF16)

    if has_gather:
        own[...] = sent
        copies = []
        for d, peer in enumerate(ctx_peers):
            copies.append(
                remote(own, out.at[me_c, me_t], z_send.at[d], z_recv.at[d], ctx=peer)
            )
        for d, peer in enumerate(tp_peers):
            copies.append(
                remote(own, out.at[me_c, me_t], t_send.at[0, d], t_recv.at[0, d], tp=peer)
            )
        for copy in copies:
            copy.start()
        out[me_c, me_t] = sent
        for d in range(n_ctx - 1):
            source = lax.rem(me_c + n_ctx - (d + 1), n_ctx)
            slot = out.at[source, me_t]
            remote(own, slot, z_send.at[d], z_recv.at[d], ctx=source).wait_recv()
            for k, peer in enumerate(tp_peers):
                copy = remote(slot, slot, t_send.at[d + 1, k], t_recv.at[d + 1, k], tp=peer)
                copy.start()
                copies.append(copy)
        for d in range(n_ctx):
            source = lax.rem(me_c + n_ctx - d, n_ctx)
            for k in range(n_tp - 1):
                origin = lax.rem(me_t + n_tp - (k + 1), n_tp)
                remote(
                    own, out.at[source, origin], t_send.at[d, k], t_recv.at[d, k], tp=origin
                ).wait_recv()
        for copy in copies:
            copy.wait_send()


IDS = {"first": 0, "fwd": 1, "fwd_last": 2, "bwd": 3, "bwd_last": 4}


def boundary(mode, stream, gain=None, partial=None, grad_res=None):
    n_ctx, n_tp = lax.axis_size("ctx"), lax.axis_size("tp")
    rows, width = stream.shape
    operands = []
    if partial is not None:
        operands.append(partial.reshape(n_tp, rows, width))
    operands.append(stream)
    if gain is not None:
        operands.append(gain.reshape(1, width))
    if grad_res is not None:
        operands.append(grad_res)
    shapes = []
    if mode != "first":
        shapes.append(jax.ShapeDtypeStruct((rows, width), F32))
    if grad_res is not None:
        shapes.append(jax.ShapeDtypeStruct((1, width), F32))
    scratch = []
    dma = pltpu.SemaphoreType.DMA
    if partial is not None:
        scratch += [pltpu.VMEM((n_tp - 1, rows, width), BF16), dma((n_tp - 1,)), dma((n_tp - 1,))]
    if mode in ("first", "fwd", "bwd"):
        shapes.append(jax.ShapeDtypeStruct((n_ctx, n_tp, rows, width), BF16))
        scratch += [
            pltpu.VMEM((rows, width), BF16),
            dma((n_ctx - 1,)),
            dma((n_ctx - 1,)),
            dma((n_ctx, n_tp - 1)),
            dma((n_ctx, n_tp - 1)),
        ]
    vmem = pl.BlockSpec(memory_space=pltpu.VMEM)
    outs = pl.pallas_call(
        functools.partial(boundary_kernel, mode, n_ctx, n_tp),
        out_shape=shapes,
        in_specs=[vmem] * len(operands),
        out_specs=[vmem] * len(shapes),
        scratch_shapes=scratch,
        name="boundary_" + mode,
        compiler_params=pltpu.CompilerParams(
            collective_id=IDS[mode], has_side_effects=True, vmem_limit_bytes=32 * 2**20
        ),
    )(*operands)
    outs = list(outs)
    if mode in ("first", "fwd", "bwd"):
        outs[-1] = outs[-1].reshape(n_ctx * n_tp * rows, width)
    return outs


def gains_kernel(sizes, x_ref, o_ref, cur, land_0, land_1, land_2, send, recv):
    lands = (land_0, land_1, land_2)
    axes = list(sizes)
    barrier = pltpu.get_barrier_semaphore()
    peers = {}
    count = 0
    for axis in axes:
        me = lax.axis_index(axis)
        peers[axis] = [lax.rem(me + d, sizes[axis]) for d in range(1, sizes[axis])]
        for peer in peers[axis]:
            pl.semaphore_signal(barrier, inc=1, device_id={axis: peer}, device_id_type=MESH)
            count += 1
    pl.semaphore_wait(barrier, count)
    total = x_ref[...]
    base = 0
    for step, axis in enumerate(axes):
        cur[step] = total
        copies = [
            remote(
                cur.at[step], lands[step].at[d], send.at[base + d], recv.at[base + d], **{axis: peer}
            )
            for d, peer in enumerate(peers[axis])
        ]
        for copy in copies:
            copy.start()
        me = lax.axis_index(axis)
        parts = []
        for d, copy in enumerate(copies):
            copy.wait_recv()
        acc = jnp.zeros_like(total)
        for position in range(sizes[axis]):
            offset = lax.rem(me + sizes[axis] - position, sizes[axis])
            slot = jnp.maximum(offset - 1, 0)
            acc = acc + jnp.where(offset == 0, total, lands[step][slot])
        total = acc
        for copy in copies:
            copy.wait_send()
        base += len(copies)
    o_ref[...] = total


def sum_gains(x):
    sizes = {axis: lax.axis_size(axis) for axis in ("dp", "ctx", "tp")}
    count = sum(n - 1 for n in sizes.values())
    vmem = pl.BlockSpec(memory_space=pltpu.VMEM)
    return pl.pallas_call(
        functools.partial(gains_kernel, sizes),
        out_shape=jax.ShapeDtypeStruct(x.shape, F32),
        in_specs=[vmem],
        out_specs=vmem,
        scratch_shapes=[pltpu.VMEM((3,) + x.shape, F32)]
        + [pltpu.VMEM((max(n - 1, 1),) + x.shape, F32) for n in sizes.values()]
        + [pltpu.SemaphoreType.DMA((count,)), pltpu.SemaphoreType.DMA((count,))],
        name="sum_gains",
        compiler_params=pltpu.CompilerParams(collective_id=5, has_side_effects=True),
    )(x)


NT = (((1,), (1,)), ((), ()))
NN = (((1,), (0,)), ((), ()))
TN = (((0,), (0,)), ((), ()))


def dot(a, b, dims):
    return lax.dot_general(a, b, dims, preferred_element_type=F32)


def turn(x):
    return pltpu.roll(x, x.shape[-1] // 2, axis=1)


def prepared(x, gain, cosine, sine):
    normed, plain, inverse = rms_forward(x, gain)
    return (normed * cosine + turn(normed) * sine).astype(BF16), plain, inverse


def soft_weights(scale, bq, q, k):
    rows = pl.program_id(2) * bq + lax.broadcasted_iota(jnp.int32, (bq, k.shape[0]), 0)
    cols = lax.broadcasted_iota(jnp.int32, (bq, k.shape[0]), 1)
    scores = jnp.where(cols <= rows, dot(q, k, NT) * scale, -jnp.inf)
    weights = jnp.exp(scores - jnp.max(scores, axis=-1, keepdims=True))
    return weights, jnp.sum(weights, axis=-1, keepdims=True)


def attend_kernel(
    scale, bq, q_ref, k_ref, v_ref, cq_ref, sq_ref, ck_ref, sk_ref, qg_ref, kg_ref, o_ref, k_rot
):
    @pl.when((pl.program_id(1) == 0) & (pl.program_id(2) == 0))
    def _():
        k_rot[...] = prepared(k_ref[...], kg_ref[...], ck_ref[...], sk_ref[...])[0]

    q = prepared(q_ref[...], qg_ref[...], cq_ref[...], sq_ref[...])[0]
    weights, total = soft_weights(scale, bq, q, k_rot[...])
    o_ref[...] = (dot(weights.astype(BF16), v_ref[...], NN) / total).astype(BF16)


def attend_back_kernel(
    scale,
    bq,
    q_ref,
    k_ref,
    v_ref,
    cq_ref,
    sq_ref,
    ck_ref,
    sk_ref,
    qg_ref,
    kg_ref,
    o_ref,
    do_ref,
    dq_ref,
    dk_ref,
    dv_ref,
    qp_ref,
    kp_ref,
    k_rot,
    dk_sum,
    dv_sum,
):
    head, member, block = pl.program_id(0), pl.program_id(1), pl.program_id(2)

    @pl.when((head == 0) & (member == 0) & (block == 0))
    def _():
        qp_ref[...] = jnp.zeros_like(qp_ref)
        kp_ref[...] = jnp.zeros_like(kp_ref)

    @pl.when((member == 0) & (block == 0))
    def _():
        k_rot[...] = prepared(k_ref[...], kg_ref[...], ck_ref[...], sk_ref[...])[0]
        dk_sum[...] = jnp.zeros_like(dk_sum)
        dv_sum[...] = jnp.zeros_like(dv_sum)

    q, plain, inverse = prepared(q_ref[...], qg_ref[...], cq_ref[...], sq_ref[...])
    k, do = k_rot[...], do_ref[...]
    weights, total = soft_weights(scale, bq, q, k)
    probs = weights / total
    delta = jnp.sum(do.astype(F32) * o_ref[...].astype(F32), axis=-1, keepdims=True)
    dscore = (probs * (dot(do, v_ref[...], NT) - delta)).astype(BF16)
    dk_sum[...] += dot(dscore, q, TN) * scale
    dv_sum[...] += dot(probs.astype(BF16), do, TN)
    grad = dot(dscore, k, NN) * scale
    grad = grad * cq_ref[...] - turn(grad) * sq_ref[...]
    qp_ref[...] += jnp.sum(grad * plain, axis=0, keepdims=True)
    dq_ref[...] = rms_backward(grad, plain, inverse, qg_ref[...]).astype(BF16)

    @pl.when((member == pl.num_programs(1) - 1) & (block == pl.num_programs(2) - 1))
    def _():
        _, k_plain, k_inverse = prepared(k_ref[...], kg_ref[...], ck_ref[...], sk_ref[...])
        grad_k = dk_sum[...]
        grad_k = grad_k * ck_ref[...] - turn(grad_k) * sk_ref[...]
        kp_ref[...] += jnp.sum(grad_k * k_plain, axis=0, keepdims=True)
        dk_ref[...] = rms_backward(grad_k, k_plain, k_inverse, kg_ref[...]).astype(BF16)
        dv_ref[...] = dv_sum[...].astype(BF16)


def attention(scale, group, query, keys, values, cosine, sine, query_gain, key_gain, *back):
    length, kv_width = keys.shape
    head_dim = cosine.shape[-1]
    kv_heads = kv_width // head_dim
    bq = min(length, 256)
    rows = pl.BlockSpec((bq, head_dim), lambda h, g, i: (i, h * group + g))
    keyed = pl.BlockSpec((length, head_dim), lambda h, g, i: (0, h))
    table_q = pl.BlockSpec((bq, head_dim), lambda h, g, i: (i, 0))
    table_k = pl.BlockSpec((length, head_dim), lambda h, g, i: (0, 0))
    flat = pl.BlockSpec((1, head_dim), lambda h, g, i: (0, 0))
    wide = jax.ShapeDtypeStruct((length, kv_width * group), BF16)
    narrow = jax.ShapeDtypeStruct((length, kv_width), BF16)
    part = jax.ShapeDtypeStruct((1, head_dim), F32)
    work = 2 * length * length * head_dim * kv_heads * group
    scratch = [pltpu.VMEM((length, head_dim), BF16)]
    if back:
        scratch += [pltpu.VMEM((length, head_dim), F32)] * 2
    return pl.pallas_call(
        functools.partial(attend_back_kernel if back else attend_kernel, scale, bq),
        grid=(kv_heads, group, length // bq),
        out_shape=(wide, narrow, narrow, part, part) if back else wide,
        in_specs=[rows, keyed, keyed, table_q, table_q, table_k, table_k, flat, flat]
        + [rows] * len(back),
        out_specs=(rows, keyed, keyed, flat, flat) if back else rows,
        scratch_shapes=scratch,
        name="attend_back" if back else "attend",
        cost_estimate=pl.CostEstimate(
            flops=work * (5 if back else 2), bytes_accessed=4 * length * 1024, transcendentals=0
        ),
        compiler_params=pltpu.CompilerParams(vmem_limit_bytes=40 * 2**20),
    )(
        query,
        keys,
        values,
        cosine,
        sine,
        cosine,
        sine,
        query_gain.reshape(1, -1),
        key_gain.reshape(1, -1),
        *back,
    )


def on_device(
    block_input,
    input_gain,
    query_weight,
    key_weight,
    value_weight,
    query_gain,
    key_gain,
    out_weight,
    post_gain,
    gate_weight,
    up_weight,
    down_weight,
    grad_output,
):
    local_rows, seq_local, width = block_input.shape
    assert seq_local == 1 and lax.axis_size("dp") == 2
    layers = input_gain.shape[0]
    head_dim = query_gain.shape[-1]
    heads = query_weight.shape[-1] // head_dim
    kv_heads = key_weight.shape[-1] // head_dim
    n_ctx, n_tp = lax.axis_size("ctx"), lax.axis_size("tp")
    block_rows = local_rows * n_tp
    length = block_rows * n_ctx
    scale = head_dim ** (-0.5)
    first_row = lax.axis_index("ctx") * block_rows
    cosine, sine = rope_tables(jnp.arange(length, dtype=F32), head_dim)
    piece = width // (2 * n_ctx)
    my_cols = (lax.axis_index("dp") * n_ctx + lax.axis_index("ctx")) * piece
    other_cols = ((1 - lax.axis_index("dp")) * n_ctx + lax.axis_index("ctx")) * piece
    swap = [(0, 1), (1, 0)]

    def mine(x):
        return lax.dynamic_slice_in_dim(x, first_row, block_rows, 0)

    def slices(x):
        parts = [lax.dynamic_slice_in_dim(x, at, piece, 1) for at in (my_cols, other_cols)]
        return jnp.concatenate(parts, axis=1)

    def settle(grad, axis):
        own, other = jnp.split(grad, 2, axis=axis)
        return own + lax.ppermute(other.astype(BF16), "dp", swap).astype(F32)

    def settle_rows(*products):
        other = [x[piece:].astype(BF16) for x in products]
        other = lax.ppermute(jnp.concatenate(other, axis=1), "dp", swap).astype(F32)
        out = []
        at = 0
        for x in products:
            out.append(x[:piece] + other[:, at : at + x.shape[1]])
            at += x.shape[1]
        return out

    hidden = block_input[:, 0]
    grad_hidden = grad_output[:, 0]
    grad_rows = lax.all_gather(grad_hidden.astype(BF16), ("ctx", "tp"), axis=0, tiled=True)
    (first_in,) = boundary("first", hidden, input_gain[0])
    kept = []
    for l in range(layers):
        query = dot(first_in, query_weight[l], NN)
        keys = dot(first_in, key_weight[l], NN)
        values = dot(first_in, value_weight[l], NN).astype(BF16)
        attend_args = (scale, heads // kv_heads, query, keys, values, cosine, sine)
        attend_args += (query_gain[l], key_gain[l])
        attended = attention(*attend_args)
        partial = dot(mine(attended), out_weight[l], NN).astype(BF16)
        mixed, second_in = boundary("fwd", hidden, post_gain[l], partial)
        gate = dot(second_in, gate_weight[l], NN)
        upward = dot(second_in, up_weight[l], NN)
        swish = (jax.nn.silu(gate) * upward).astype(BF16)
        partial = dot(mine(swish), down_weight[l], NN).astype(BF16)
        kept.append(
            (hidden, first_in, attend_args, attended, mixed, second_in, gate, upward, swish)
        )
        if l + 1 < layers:
            hidden, first_in = boundary("fwd", mixed, input_gain[l + 1], partial)
        else:
            hidden = mixed + lax.psum_scatter(
                partial, "tp", scatter_dimension=0, tiled=True
            ).astype(F32)

    grads = [None] * layers
    gains = [None] * layers
    for l in reversed(range(layers)):
        x_in, first_in, attend_args, attended, mixed, second_in, gate, upward, swish = kept[l]
        grad_swish = dot(grad_rows, down_weight[l], NT)
        sigma = jax.nn.sigmoid(gate)
        grad_gate = (grad_swish * upward * (sigma * (1.0 + gate * (1.0 - sigma)))).astype(BF16)
        grad_up = (grad_swish * (gate * sigma)).astype(BF16)
        partial = dot(mine(grad_gate), gate_weight[l], NT) + dot(mine(grad_up), up_weight[l], NT)
        grad_mixed, post_part, mixed_rows = boundary(
            "bwd", mixed, post_gain[l], partial.astype(BF16), grad_hidden
        )
        second_cols = slices(second_in)
        down_grad = settle(dot(swish, slices(grad_rows), TN), 1)
        gate_grad, up_grad = settle_rows(
            dot(second_cols, grad_gate, TN), dot(second_cols, grad_up, TN)
        )

        grad_heads = dot(mixed_rows, out_weight[l], NT).astype(BF16)
        out_grad = settle(dot(attended, slices(mixed_rows), TN), 1)
        query_bf, key_bf, value_bf, q_part, k_part = attention(*attend_args, attended, grad_heads)
        partial = (
            dot(mine(query_bf), query_weight[l], NT)
            + dot(mine(key_bf), key_weight[l], NT)
            + dot(mine(value_bf), value_weight[l], NT)
        ).astype(BF16)
        if l:
            grad_hidden, input_part, grad_rows = boundary(
                "bwd", x_in, input_gain[l], partial, grad_mixed
            )
        else:
            grad_hidden, input_part = boundary(
                "bwd_last", x_in, input_gain[l], partial, grad_mixed
            )
        first_cols = slices(first_in)
        query_grad, key_grad, value_grad = settle_rows(
            dot(first_cols, query_bf, TN),
            dot(first_cols, key_bf, TN),
            dot(first_cols, value_bf, TN),
        )
        grads[l] = (query_grad, key_grad, value_grad, out_grad, gate_grad, up_grad, down_grad)
        gains[l] = (input_part[0], q_part[0] / n_ctx, k_part[0] / n_ctx, post_part[0])
    stacked = [jnp.stack([part[m] for part in grads]) for m in range(7)]
    packed = jnp.concatenate([v for part in gains for v in part])
    sizes = [v.shape[0] for part in gains for v in part]
    padded = -(-packed.shape[0] // 1024) * 1024
    packed = jnp.pad(packed, (0, padded - packed.shape[0])).reshape(-1, 128)
    summed = sum_gains(packed).reshape(-1)
    pieces = []
    at = 0
    for size in sizes:
        pieces.append(summed[at : at + size])
        at += size
    gains = [jnp.stack([pieces[4 * l + m] for l in range(layers)]) for m in range(4)]
    return (
        hidden[:, None],
        grad_hidden[:, None],
        gains[0],
        stacked[0],
        stacked[1],
        stacked[2],
        gains[1],
        gains[2],
        stacked[3],
        gains[3],
        stacked[4],
        stacked[5],
        stacked[6],
    )


def rope_constants(length, head_dim):
    half = head_dim // 2
    frequency = np.float32(THETA) ** (-(np.float32(2.0) * np.arange(half, dtype=np.float32)) / np.float32(head_dim))
    angles = np.arange(length, dtype=np.float32)[:, None] * frequency.astype(np.float32)[None, :]
    cosine, sine = np.cos(angles), np.sin(angles)
    return (
        np.concatenate([cosine, cosine], axis=-1).astype(np.float32),
        np.concatenate([-sine, sine], axis=-1).astype(np.float32),
    )


def chunks(total, step=256):
    step = step if total % step == 0 else 128
    return [(at, step) for at in range(0, total, step)]


def fused_kernel(sz, *refs):
    (layers, n_ctx, n_tp, rows, width, heads, kv_heads, head_dim, ff) = sz
    block = rows * n_tp
    length = block * n_ctx
    group = heads // kv_heads
    q_w, k_w = heads * head_dim, kv_heads * head_dim
    piece = width // (2 * n_ctx)
    log2e = 1.4426950408889634
    scale = head_dim ** (-0.5)
    (x_ref, go_ref, ig_ref, pg_ref, qg_ref, kg_ref, cos_ref, sin_ref) = refs[:8]
    (wq_h, wk_h, wv_h, wo_h, wg_h, wu_h, wd_h) = refs[8:15]
    y_ref, gx_ref, gain_ref = refs[15:18]
    finals = refs[18:25]
    (wqkv, wo, wgu, wd, G, P, land, q_raw, k_raw, q_rot, k_rot, vals, att, swish, fa, fb, ggu, d_o, dqkv,
     dk_acc, dv_acc, mixed_s, xs_s, gm_s, gains, g_dp, g_ctx, g_tp,
     s_qkv, s_out, s_gu, s_dn, l_qkv, l_out, l_gu, l_dn,
     oq_ref, ok_ref, ov_ref, oo_ref, og_ref, ou_ref, od_ref, o_sem,
     w_sem, z_send, z_recv, t_send, t_recv, r_send, r_recv, d_send, d_recv, a_send, a_recv) = refs[25:]

    c, t, dp = lax.axis_index("ctx"), lax.axis_index("tp"), lax.axis_index("dp")
    tp_peers = [lax.rem(t + k, n_tp) for k in range(1, n_tp)]
    ctx_peers = [lax.rem(c + d, n_ctx) for d in range(1, n_ctx)]
    other = 1 - dp
    pending = []

    loads = []

    def load(src, dst):
        copy = pltpu.make_async_copy(src, dst, w_sem.at[len(loads)])
        copy.start()
        loads.append(copy)

    for l in range(layers):
        load(wk_h.at[l], wqkv.at[l, :, pl.ds(q_w, k_w)])
        load(wv_h.at[l], wqkv.at[l, :, pl.ds(q_w + k_w, k_w)])
        load(wq_h.at[l], wqkv.at[l, :, pl.ds(0, q_w)])
        load(wo_h.at[l], wo.at[l])
        load(wg_h.at[l], wgu.at[l, :, pl.ds(0, ff)])
        load(wu_h.at[l], wgu.at[l, :, pl.ds(ff, ff)])
        load(wd_h.at[l], wd.at[l])

    barrier = pltpu.get_barrier_semaphore()
    for peer in tp_peers:
        pl.semaphore_signal(barrier, inc=1, device_id={"tp": peer}, device_id_type=MESH)
    for peer in ctx_peers:
        pl.semaphore_signal(barrier, inc=1, device_id={"ctx": peer}, device_id_type=MESH)
    pl.semaphore_signal(barrier, inc=1, device_id={"dp": other}, device_id_type=MESH)
    pl.semaphore_wait(barrier, n_tp + n_ctx - 1)

    def push(copy):
        copy.start()
        pending.append(copy)

    near = [1, n_ctx - 1] + list(range(2, n_ctx - 1))

    def source_of(d):
        return lax.rem(c + n_ctx - d, n_ctx)

    def spread(g, d):
        slot = G.at[g, source_of(d), t]
        for k, peer in enumerate(tp_peers):
            push(remote(slot, slot, t_send.at[g, d, k], t_recv.at[g, d, k], tp=peer))

    def complete(g, d):
        for k in range(n_tp - 1):
            origin = lax.rem(t + n_tp - (k + 1), n_tp)
            slot = G.at[g, source_of(d), origin]
            remote(slot, slot, t_send.at[g, d, k], t_recv.at[g, d, k], tp=origin).wait_recv()

    def start_gather(g, value, planes=False):
        own = G.at[g, c, t]
        G[g, c, t] = value
        if not planes:
            for d in near:
                push(remote(own, own, z_send.at[g, d - 1], z_recv.at[g, d - 1], ctx=ctx_peers[d - 1]))
        spread(g, 0)

    def plane_send(g, *steps):
        own = G.at[g, c]
        for d in steps:
            push(remote(own, own, z_send.at[g, d - 1], z_recv.at[g, d - 1], ctx=ctx_peers[d - 1]))

    def plane_complete(g):
        for d in range(1, n_ctx):
            slot = G.at[g, source_of(d)]
            remote(slot, slot, z_send.at[g, d - 1], z_recv.at[g, d - 1], ctx=source_of(d)).wait_recv()

    def late_spread(g, *steps):
        for d in steps:
            source = source_of(d)
            slot = G.at[g, source, t]
            remote(slot, slot, z_send.at[g, d - 1], z_recv.at[g, d - 1], ctx=source).wait_recv()
            spread(g, d)

    def full_gather(g, work, early=None):
        if early is not None:
            early()
        late_spread(g, near[0], near[1])
        complete(g, 0)
        work(c)
        late_spread(g, *near[2:])
        for d in near:
            complete(g, d)
            work(source_of(d))

    def late_complete(g):
        for d in range(1, n_ctx):
            complete(g, d)

    wide = 512 if width % 512 == 0 else width

    def sum_part(r, k, at, peer):
        lanes = pl.ds(at, wide)
        src, dst = P.at[r, peer, :, lanes], land.at[r, k, :, lanes]
        return remote(src, dst, r_send.at[r, k, at // wide], r_recv.at[r, k, at // wide], tp=peer)

    def start_sum(r, value_of):
        for at in range(0, width, wide):
            P[r, :, :, at : at + wide] = value_of(at, at + wide).astype(BF16).reshape(n_tp, rows, wide)
            for k, peer in enumerate(tp_peers):
                push(sum_part(r, k, at, peer))

    def finish_sum(r):
        for at in range(0, width, wide):
            for k, peer in enumerate(tp_peers):
                sum_part(r, k, at, peer).wait_recv()
        total = P[r, t].astype(F32)
        for k in range(n_tp - 1):
            total = total + land[r, k].astype(F32)
        return total

    def others(body):
        def step(d, carry):
            body(d, lax.rem(c + n_ctx - d, n_ctx))
            return carry

        lax.fori_loop(1, n_ctx, step, 0)

    def tokens(g, s):
        return G[g, s].reshape(block, width)

    def qkv(l, s):
        x = tokens(l, s)
        cosine = cos_ref[pl.ds(pl.multiple_of(s * block, block), block), :]
        sine = sin_ref[pl.ds(pl.multiple_of(s * block, block), block), :]
        qg, kg = qg_ref[l : l + 1, :], kg_ref[l : l + 1, :]
        for at, step in chunks(q_w + 2 * k_w):
            y = dot(x, wqkv[l, :, at : at + step], NN)
            for sub in range(0, step, head_dim):
                yh = y[:, sub : sub + head_dim]
                h = (at + sub) // head_dim
                if h < heads:
                    q_raw[l, h, s] = yh
                    q_rot[l, h, s] = prepared(yh, qg, cosine, sine)[0]
                elif h < heads + kv_heads:
                    k_raw[l, h - heads, s] = yh
                    k_rot[l, h - heads, s] = prepared(yh, kg, cosine, sine)[0]
                else:
                    vals[l, h - heads - kv_heads, s] = yh.astype(BF16)

    def attend_block(l, i):
        at_row = i * block + lax.broadcasted_iota(jnp.int32, (block, length), 0)
        allowed = lax.broadcasted_iota(jnp.int32, (block, length), 1) <= at_row
        for h in range(heads):
            k = k_rot[l, h // group].reshape(length, head_dim)
            v = vals[l, h // group].reshape(length, head_dim)
            scores = dot(q_rot[l, h, i], k, NT) * (scale * log2e)
            weights = jnp.where(allowed, jnp.exp2(scores), 0.0)
            total = jnp.sum(weights, axis=-1, keepdims=True)
            out = dot(weights.astype(BF16), v, NN) / total
            att[l, i, :, h * head_dim : (h + 1) * head_dim] = out.astype(BF16)

    def out_partial(l):
        a = att[l, c]
        start_sum(l, lambda lo, hi: dot(a, wo[l, :, lo:hi], NN))

    def mlp_forward(l, s):
        x = tokens(layers + l, s)
        for at, step in chunks(ff):
            gate = dot(x, wgu[l, :, at : at + step], NN)
            up = dot(x, wgu[l, :, ff + at : ff + at + step], NN)
            sigma = jax.nn.sigmoid(gate)
            silu = gate * sigma
            swish[l, s, :, at : at + step] = (silu * up).astype(BF16)
            fa[l, s, :, at : at + step] = (up * (sigma * (1.0 + gate * (1.0 - sigma)))).astype(BF16)
            fb[l, s, :, at : at + step] = silu.astype(BF16)

    def down_partial(l):
        a = swish[l, c]
        start_sum(layers + l, lambda lo, hi: dot(a, wd[l, :, lo:hi], NN))

    def mlp_backward(l, s):
        x = tokens(2 * layers + l, s)
        for at, step in chunks(ff):
            grad = dot(x, wd[l, at : at + step, :], NT)
            ggu[l, s, :, at : at + step] = (grad * fa[l, s, :, at : at + step].astype(F32)).astype(BF16)
            ggu[l, s, :, ff + at : ff + at + step] = (
                grad * fb[l, s, :, at : at + step].astype(F32)
            ).astype(BF16)

    def mlp_back_partial(l):
        a = ggu[l, c]
        start_sum(2 * layers + l, lambda lo, hi: dot(a, wgu[l, lo:hi, :], NT))

    def heads_back(l, s):
        x = tokens(3 * layers + l, s)
        for at, step in chunks(q_w):
            d_o[s, :, at : at + step] = dot(x, wo[l, at : at + step, :], NT).astype(BF16)

    def attend_backward(l):
        dk_acc[...] = jnp.zeros_like(dk_acc)
        dv_acc[...] = jnp.zeros_like(dv_acc)
        half = length // 2
        per = n_ctx // 2
        causal = lax.broadcasted_iota(jnp.int32, (half, half), 1) <= lax.broadcasted_iota(
            jnp.int32, (half, half), 0
        )
        qg, kg = qg_ref[l : l + 1, :], kg_ref[l : l + 1, :]

        def one_head(h, part):
            lanes = pl.ds(pl.multiple_of(h * head_dim, head_dim), head_dim)
            kv = h // group
            for i in range(2):
                span = slice(i * per, (i + 1) * per)
                extent = (i + 1) * half
                q = q_rot[l, h, span].reshape(half, head_dim)
                do = d_o[span, :, lanes].reshape(half, head_dim)
                a = att[l, span, :, lanes].reshape(half, head_dim)
                k = k_rot[l, kv, : (i + 1) * per].reshape(extent, head_dim)
                v = vals[l, kv, : (i + 1) * per].reshape(extent, head_dim)
                weights = jnp.exp2(dot(q, k, NT) * (scale * log2e))
                last = jnp.where(causal, weights[:, i * half :], 0.0)
                weights = jnp.concatenate([weights[:, :half], last], axis=1) if i else last
                probs = weights / jnp.sum(weights, axis=-1, keepdims=True)
                delta = jnp.sum(do.astype(F32) * a.astype(F32), axis=-1, keepdims=True)
                dscore = (probs * (dot(do, v, NT) - delta)).astype(BF16)
                dk_acc[kv, :extent] += dot(dscore, q, TN)
                dv_acc[kv, :extent] += dot(probs.astype(BF16), do, TN)
                cosine = cos_ref[i * half : (i + 1) * half, :]
                sine = sin_ref[i * half : (i + 1) * half, :]
                grad = dot(dscore, k, NN) * scale
                grad = grad * cosine - turn(grad) * sine
                _, plain, inverse = rms_forward(q_raw[l, h, span].reshape(half, head_dim), qg)
                part = part + jnp.sum(grad * plain, axis=0, keepdims=True)
                grad = rms_backward(grad, plain, inverse, qg).astype(BF16)
                dqkv[span, :, lanes] = grad.reshape(per, block, head_dim)
            return part

        q_part = lax.fori_loop(0, heads, one_head, jnp.zeros((1, head_dim), F32))
        k_part = jnp.zeros((1, head_dim), F32)
        for kv in range(kv_heads):
            grad = dk_acc[kv] * scale
            grad = grad * cos_ref[...] - turn(grad) * sin_ref[...]
            _, plain, inverse = rms_forward(k_raw[l, kv].reshape(length, head_dim), kg)
            k_part = k_part + jnp.sum(grad * plain, axis=0, keepdims=True)
            grad = rms_backward(grad, plain, inverse, kg).astype(BF16)
            at = q_w + kv * head_dim
            dqkv[:, :, at : at + head_dim] = grad.reshape(n_ctx, block, head_dim)
            at += k_w
            dqkv[:, :, at : at + head_dim] = dv_acc[kv].astype(BF16).reshape(n_ctx, block, head_dim)
        at = 2 * layers
        gains[at : at + 1, 2 * l * head_dim : (2 * l + 1) * head_dim] = q_part / n_ctx
        gains[at : at + 1, (2 * l + 1) * head_dim : (2 * l + 2) * head_dim] = k_part / n_ctx

    def qkv_back_partial(l):
        a = dqkv[c]
        start_sum(3 * layers + l, lambda lo, hi: dot(a, wqkv[l, lo:hi, :], NT))

    my_cols = pl.ds(pl.multiple_of((dp * n_ctx + c) * piece, piece), piece)
    other_cols = pl.ds(pl.multiple_of((other * n_ctx + c) * piece, piece), piece)

    def columns(g):
        parts = [G[g, :, :, :, cols].reshape(length, piece) for cols in (my_cols, other_cols)]
        return jnp.concatenate(parts, axis=1)

    def exchange(i, src, dst):
        push(remote(src, dst, d_send.at[i], d_recv.at[i], dp=other))

    def grads_mlp(l):
        x = columns(layers + l)
        for at, step in chunks(2 * ff):
            g = dot(x, ggu[l, :, :, at : at + step].reshape(length, step), TN)
            ref, base = (og_ref, at) if at < ff else (ou_ref, at - ff)
            ref[l, :, base : base + step] = g[:piece]
            s_gu[l, :, at : at + step] = g[piece:].astype(BF16)
        exchange(4 * l, s_gu.at[l], l_gu.at[l])
        x = columns(2 * layers + l)
        for at, step in chunks(ff):
            g = dot(swish[l, :, :, at : at + step].reshape(length, step), x, TN)
            od_ref[l, at : at + step, :] = g[:, :piece]
            s_dn[l, at : at + step, :] = g[:, piece:].astype(BF16)
        exchange(4 * l + 1, s_dn.at[l], l_dn.at[l])

    def grads_out(l):
        x = columns(3 * layers + l)
        for at, step in chunks(q_w):
            g = dot(att[l, :, :, at : at + step].reshape(length, step), x, TN)
            oo_ref[l, at : at + step, :] = g[:, :piece]
            s_out[l, at : at + step, :] = g[:, piece:].astype(BF16)
        exchange(4 * l + 2, s_out.at[l], l_out.at[l])

    def grads_qkv(l):
        x = columns(l)
        for at, step in chunks(q_w + 2 * k_w):
            g = dot(x, dqkv[:, :, at : at + step].reshape(length, step), TN)
            if at < q_w:
                oq_ref[l, :, at : at + step] = g[:piece]
            elif at < q_w + k_w:
                ok_ref[l, :, at - q_w : at - q_w + step] = g[:piece]
            else:
                ov_ref[l, :, at - q_w - k_w : at - q_w - k_w + step] = g[:piece]
            s_qkv[l, :, at : at + step] = g[piece:].astype(BF16)
        exchange(4 * l + 3, s_qkv.at[l], l_qkv.at[l])

    def settle(l):
        def landed(i, dst):
            remote(dst, dst, d_send.at[i], d_recv.at[i], dp=other).wait_recv()

        landed(4 * l, l_gu.at[l])
        og_ref[l] += l_gu[l, :, :ff].astype(F32)
        ou_ref[l] += l_gu[l, :, ff:].astype(F32)
        landed(4 * l + 1, l_dn.at[l])
        od_ref[l] += l_dn[l].astype(F32)
        landed(4 * l + 2, l_out.at[l])
        oo_ref[l] += l_out[l].astype(F32)
        landed(4 * l + 3, l_qkv.at[l])
        oq_ref[l] += l_qkv[l, :, :q_w].astype(F32)
        ok_ref[l] += l_qkv[l, :, q_w : q_w + k_w].astype(F32)
        ov_ref[l] += l_qkv[l, :, q_w + k_w :].astype(F32)

    gains[...] = jnp.zeros_like(gains)

    leaving = []

    def deliver(l):
        staged = (oq_ref, ok_ref, ov_ref, oo_ref, og_ref, ou_ref, od_ref)
        for i, (src, dst) in enumerate(zip(staged, finals)):
            copy = pltpu.make_async_copy(src.at[l], dst.at[l], o_sem.at[i, l])
            copy.start()
            leaving.append(copy)

    stages = (("dp", dp, [other], g_dp, 0), ("ctx", c, ctx_peers, g_ctx, 1), ("tp", t, tp_peers, g_tp, n_ctx))

    def gain_start(stage, value):
        axis, me, peers, buf, base = stages[stage]
        buf[me] = value
        for i, peer in enumerate(peers):
            own = buf.at[me]
            push(remote(own, own, a_send.at[base + i], a_recv.at[base + i], **{axis: peer}))

    def gain_finish(stage):
        axis, me, peers, buf, base = stages[stage]
        n = len(peers) + 1
        for i in range(n - 1):
            source = lax.rem(me + n - (i + 1), n)
            slot = buf.at[source]
            remote(slot, slot, a_send.at[base + i], a_recv.at[base + i], **{axis: source}).wait_recv()
        value = buf[0]
        for i in range(1, n):
            value = value + buf[i]
        return value

    top = layers - 1
    X1, X2, GR, MR = (lambda l: l), (lambda l: layers + l), (lambda l: 2 * layers + l), (lambda l: 3 * layers + l)

    x_in = x_ref[:, 0, :]
    xs_s[0] = x_in
    start_gather(X1(0), rms_forward(x_in, ig_ref[0:1, :])[0].astype(BF16))
    for l in range(layers):
        for i in range(3):
            loads[7 * l + i].wait()
        full_gather(X1(l), lambda s: qkv(l, s))
        if l == 0:
            start_gather(GR(top), go_ref[:, 0, :].astype(BF16), True)
        else:
            plane_send(GR(top), 2)
        attend_block(l, c)
        loads[7 * l + 3].wait()
        out_partial(l)
        attend_block(l, source_of(1))
        if l == 0:
            complete(GR(top), 0)
            plane_send(GR(top), 1, 3)
        else:
            plane_send(X2(l - 1), 1, 3)
        attend_block(l, source_of(2))
        mixed = xs_s[l] + finish_sum(l)
        mixed_s[l] = mixed
        start_gather(X2(l), rms_forward(mixed, pg_ref[l : l + 1, :])[0].astype(BF16), l < top)
        for i in range(4, 7):
            loads[7 * l + i].wait()
        attend_block(l, source_of(3))
        complete(X2(l), 0)
        mlp_forward(l, c)
        if l < top:
            down_partial(l)
            x_next = mixed_s[l] + finish_sum(layers + l)
            xs_s[l + 1] = x_next
            start_gather(X1(l + 1), rms_forward(x_next, ig_ref[l + 1 : l + 2, :])[0].astype(BF16))

    for l in reversed(range(layers)):
        if l < top:
            complete(GR(l), 0)
        mlp_backward(l, c)
        mlp_back_partial(l)
        if l == top:
            down_partial(l)
            plane_complete(GR(top))
        else:
            others(lambda d, s: mlp_backward(l + 1, s))
        grad_res = go_ref[:, 0, :] if l == top else gm_s[1]
        _, normed, inverse = rms_forward(mixed_s[l], pg_ref[l : l + 1, :])
        total = finish_sum(2 * layers + l)
        gains[layers + l : layers + l + 1, :] = jnp.sum(total * normed, axis=0, keepdims=True)
        grad_mixed = grad_res + rms_backward(total, normed, inverse, pg_ref[l : l + 1, :])
        gm_s[0] = grad_mixed
        start_gather(MR(l), grad_mixed.astype(BF16))
        if l == top:
            y_ref[...] = mixed_s[l] + finish_sum(layers + l)

        def early():
            if l < top:
                grads_mlp(l + 1)
                plane_complete(X2(l))
                others(lambda d, s: mlp_forward(l, s))

        full_gather(MR(l), lambda s: heads_back(l, s), early)
        late_spread(X2(l) if l == top else GR(l), 1, 2, 3)
        attend_backward(l)
        qkv_back_partial(l)
        if l == 0:
            plain = tokens(X1(l), c).astype(F32)
            back = P[3 * layers + l].reshape(block, width).astype(F32)
            gains[l : l + 1, :] = jnp.sum(back * plain, axis=0, keepdims=True) / ig_ref[l : l + 1, :]
            gain_start(0, gains[...])
        else:
            plane_send(X2(l - 1), 2)
        grads_out(l)
        grads_qkv(l)
        if l:
            _, normed, inverse = rms_forward(xs_s[l], ig_ref[l : l + 1, :])
            total = finish_sum(3 * layers + l)
            gains[l : l + 1, :] = jnp.sum(total * normed, axis=0, keepdims=True)
            grad_x = gm_s[0] + rms_backward(total, normed, inverse, ig_ref[l : l + 1, :])
            gm_s[1] = grad_x
            start_gather(GR(l - 1), grad_x.astype(BF16))
            late_complete(X2(l))
            others(lambda d, s: mlp_forward(l, s))
        if l == 0:
            gain_start(1, gain_finish(0))
            late_complete(GR(l))
            others(lambda d, s: mlp_backward(l, s))
            grads_mlp(l)
            gain_start(2, gain_finish(1))
            settle(l + 1)
            deliver(l + 1)
            _, normed, inverse = rms_forward(xs_s[l], ig_ref[l : l + 1, :])
            total = finish_sum(3 * layers + l)
            gx_ref[...] = gm_s[0] + rms_backward(total, normed, inverse, ig_ref[l : l + 1, :])
            settle(l)
            deliver(l)
            gain_ref[...] = gain_finish(2)

    for copy in leaving:
        copy.wait()
    for copy in pending:
        copy.wait_send()


def fused(sz, *operands):
    (layers, n_ctx, n_tp, rows, width, heads, kv_heads, head_dim, ff) = sz
    block = rows * n_tp
    length = block * n_ctx
    q_w, k_w = heads * head_dim, kv_heads * head_dim
    piece = width // (2 * n_ctx)
    vm = lambda *shape: pltpu.VMEM(shape, BF16)
    vf = lambda *shape: pltpu.VMEM(shape, F32)
    dma = pltpu.SemaphoreType.DMA
    sd = lambda *shape: jax.ShapeDtypeStruct(shape, F32)
    n_g = 4 * layers
    scratch = [
        vm(layers, width, q_w + 2 * k_w),
        vm(layers, q_w, width),
        vm(layers, width, 2 * ff),
        vm(layers, ff, width),
        vm(n_g, n_ctx, n_tp, rows, width),
        vm(n_g, n_tp, rows, width),
        vm(n_g, n_tp - 1, rows, width),
        vf(layers, heads, n_ctx, block, head_dim),
        vf(layers, kv_heads, n_ctx, block, head_dim),
        vm(layers, heads, n_ctx, block, head_dim),
        vm(layers, kv_heads, n_ctx, block, head_dim),
        vm(layers, kv_heads, n_ctx, block, head_dim),
        vm(layers, n_ctx, block, q_w),
        vm(layers, n_ctx, block, ff),
        vm(layers, n_ctx, block, ff),
        vm(layers, n_ctx, block, ff),
        vm(layers, n_ctx, block, 2 * ff),
        vm(n_ctx, block, q_w),
        vm(n_ctx, block, q_w + 2 * k_w),
        vf(kv_heads, length, head_dim),
        vf(kv_heads, length, head_dim),
        vf(layers, rows, width),
        vf(layers, rows, width),
        vf(2, rows, width),
        vf(8, width),
        vf(2, 8, width),
        vf(n_ctx, 8, width),
        vf(n_tp, 8, width),
    ]
    outs = [
        sd(layers, piece, q_w),
        sd(layers, piece, k_w),
        sd(layers, piece, k_w),
        sd(layers, q_w, piece),
        sd(layers, piece, ff),
        sd(layers, piece, ff),
        sd(layers, ff, piece),
    ]
    for _ in range(2):
        scratch += [
            vm(layers, piece, q_w + 2 * k_w),
            vm(layers, q_w, piece),
            vm(layers, piece, 2 * ff),
            vm(layers, ff, piece),
        ]
    scratch += [pltpu.VMEM(out.shape, F32) for out in outs]
    scratch += [
        dma((7, layers)),
        dma((7 * layers,)),
        dma((n_g, n_ctx - 1)),
        dma((n_g, n_ctx - 1)),
        dma((n_g, n_ctx, n_tp - 1)),
        dma((n_g, n_ctx, n_tp - 1)),
        dma((n_g, n_tp - 1, 2)),
        dma((n_g, n_tp - 1, 2)),
        dma((4 * layers,)),
        dma((4 * layers,)),
        dma((n_ctx + n_tp - 1,)),
        dma((n_ctx + n_tp - 1,)),
    ]
    vmem = pl.BlockSpec(memory_space=pltpu.VMEM)
    hbm = pl.BlockSpec(memory_space=pl.ANY)
    return pl.pallas_call(
        functools.partial(fused_kernel, sz),
        out_shape=[
            sd(rows, width),
            sd(rows, width),
            sd(8, width),
        ]
        + outs,
        in_specs=[vmem] * 8 + [hbm] * 7,
        out_specs=[vmem] * 3 + [hbm] * 7,
        scratch_shapes=scratch,
        name="two_layers",
        compiler_params=pltpu.CompilerParams(
            collective_id=6, has_side_effects=True, vmem_limit_bytes=60 * 2**20
        ),
    )(*operands)


def finish_kernel(layers, head_dim, *refs):
    y_in, gx_in, gain_in = refs[:3]
    grads_in = refs[3:10]
    y, gx, input_gain, query_gain, key_gain, post_gain = refs[10:16]
    grads_out = refs[16:23]
    held = refs[23:30]
    sems_in, sems_out = refs[30:]
    arrive, leave = [], []
    for l in reversed(range(layers)):
        for i, (src, mid, dst) in enumerate(zip(grads_in, held, grads_out)):
            arrive.append(pltpu.make_async_copy(src.at[l], mid.at[l], sems_in.at[i, l]))
            leave.append(pltpu.make_async_copy(mid.at[l], dst.at[l], sems_out.at[i, l]))
    for copy in arrive:
        copy.start()
    for first, second in zip(arrive, leave):
        first.wait()
        second.start()
    y[:, 0, :] = y_in[...]
    gx[:, 0, :] = gx_in[...]
    input_gain[...] = gain_in[:layers, :]
    post_gain[...] = gain_in[layers : 2 * layers, :]
    for l in range(layers):
        at = 2 * l * head_dim
        query_gain[l : l + 1, :] = gain_in[2 * layers : 2 * layers + 1, at : at + head_dim]
        key_gain[l : l + 1, :] = gain_in[2 * layers : 2 * layers + 1, at + head_dim : at + 2 * head_dim]
    for copy in leave:
        copy.wait()


def finish(layers, head_dim, y, gx, gains, *grads):
    rows, width = y.shape
    sd = lambda *shape: jax.ShapeDtypeStruct(shape, F32)
    vmem = pl.BlockSpec(memory_space=pltpu.VMEM)
    hbm = pl.BlockSpec(memory_space=pl.ANY)
    return pl.pallas_call(
        functools.partial(finish_kernel, layers, head_dim),
        out_shape=[
            sd(rows, 1, width),
            sd(rows, 1, width),
            sd(layers, width),
            sd(layers, head_dim),
            sd(layers, head_dim),
            sd(layers, width),
        ]
        + [sd(*grad.shape) for grad in grads],
        in_specs=[vmem] * 3 + [hbm] * len(grads),
        out_specs=[vmem] * 6 + [hbm] * len(grads),
        scratch_shapes=[pltpu.VMEM(grad.shape, F32) for grad in grads]
        + [pltpu.SemaphoreType.DMA((len(grads), layers))] * 2,
        name="finish",
    )(y, gx, gains, *grads)


def on_device_fused(
    block_input,
    input_gain,
    query_weight,
    key_weight,
    value_weight,
    query_gain,
    key_gain,
    out_weight,
    post_gain,
    gate_weight,
    up_weight,
    down_weight,
    grad_output,
):
    rows, _, width = block_input.shape
    layers = input_gain.shape[0]
    head_dim = query_gain.shape[-1]
    n_ctx, n_tp = lax.axis_size("ctx"), lax.axis_size("tp")
    sz = (
        layers,
        n_ctx,
        n_tp,
        rows,
        width,
        query_weight.shape[-1] // head_dim,
        key_weight.shape[-1] // head_dim,
        head_dim,
        gate_weight.shape[-1],
    )
    cosine, sine = rope_constants(rows * n_tp * n_ctx, head_dim)
    y, gx, gains, *grads = fused(
        sz,
        block_input,
        grad_output,
        input_gain,
        post_gain,
        query_gain,
        key_gain,
        cosine,
        sine,
        query_weight,
        key_weight,
        value_weight,
        out_weight,
        gate_weight,
        up_weight,
        down_weight,
    )
    y, gx, input_part, q_part, k_part, post_part, wq, wk, wv, wo, wg, wu, wd = finish(
        layers, head_dim, y, gx, gains, *grads
    )
    return (y, gx, input_part, wq, wk, wv, q_part, k_part, wo, post_part, wg, wu, wd)


def on_any_device(*arrays):
    rows, _, width = arrays[0].shape
    n_ctx, n_tp = lax.axis_size("ctx"), lax.axis_size("tp")
    small = n_tp == 4 and n_ctx == 4 and arrays[1].shape[0] == 2 and rows * n_tp * n_ctx <= 512 and (width // (2 * n_ctx)) % 128 == 0
    return (on_device_fused if small else on_device)(*arrays)


def solution(mesh):
    placed = (
        P(("ctx", "tp"), "dp", None),
        P(),
        P(None, None, "tp"),
        P(None, None, "tp"),
        P(None, None, "tp"),
        P(),
        P(),
        P(None, "tp", None),
        P(),
        P(None, None, "tp"),
        P(None, None, "tp"),
        P(None, "tp", None),
        P(("ctx", "tp"), "dp", None),
    )
    return jax.shard_map(
        on_any_device,
        mesh=mesh,
        in_specs=placed,
        out_specs=(
            P(("ctx", "tp"), "dp", None),
            P(("ctx", "tp"), "dp", None),
            P(),
            P(None, ("dp", "ctx"), "tp"),
            P(None, ("dp", "ctx"), "tp"),
            P(None, ("dp", "ctx"), "tp"),
            P(),
            P(),
            P(None, "tp", ("dp", "ctx")),
            P(),
            P(None, ("dp", "ctx"), "tp"),
            P(None, ("dp", "ctx"), "tp"),
            P(None, "tp", ("dp", "ctx")),
        ),
        check_vma=False,
    )
```

```python
import functools

import jax
import jax.numpy as jnp
import numpy as np
from jax import lax
from jax.experimental import pallas as pl
from jax.experimental.pallas import tpu as pltpu
from jax.sharding import PartitionSpec as P

EPS = 1e-06
THETA = 1000000.0
MESH = pl.DeviceIdType.MESH
F32 = jnp.float32
BF16 = jnp.bfloat16


def rms_forward(field, gain):
    inverse = lax.rsqrt(jnp.mean(field * field, axis=-1, keepdims=True) + EPS)
    normed = field * inverse
    return (normed * gain, normed, inverse)


def rms_backward(grad_out, normed, inverse, gain):
    scaled = grad_out * gain
    return inverse * (scaled - normed * jnp.mean(scaled * normed, axis=-1, keepdims=True))


def rope_tables(positions, head_dim):
    half = head_dim // 2
    frequency = THETA ** (-(2.0 * jnp.arange(half, dtype=F32)) / head_dim)
    angles = positions[:, None] * frequency[None, :]
    cosine, sine = jnp.cos(angles), jnp.sin(angles)
    return (jnp.concatenate([cosine, cosine], axis=-1), jnp.concatenate([-sine, sine], axis=-1))


def remote(src, dst, send, recv, **where):
    return pltpu.make_async_remote_copy(
        src_ref=src,
        dst_ref=dst,
        send_sem=send,
        recv_sem=recv,
        device_id=where,
        device_id_type=MESH,
    )


def boundary_kernel(mode, n_ctx, n_tp, *refs):
    refs = list(refs)
    has_sum = mode != "first"
    has_gather = mode in ("first", "fwd", "bwd")
    partial = refs.pop(0) if has_sum else None
    stream = refs.pop(0)
    gain = refs.pop(0) if mode not in ("fwd_last",) else None
    grad_res = refs.pop(0) if mode in ("bwd", "bwd_last") else None
    fresh = refs.pop(0) if mode != "first" else None
    gain_part = refs.pop(0) if mode in ("bwd", "bwd_last") else None
    out = refs.pop(0) if has_gather else None
    if has_sum:
        landed, rs_send, rs_recv = refs.pop(0), refs.pop(0), refs.pop(0)
    if has_gather:
        own, z_send, z_recv, t_send, t_recv = refs

    me_c = lax.axis_index("ctx")
    me_t = lax.axis_index("tp")
    tp_peers = [lax.rem(me_t + d, n_tp) for d in range(1, n_tp)]
    ctx_peers = [lax.rem(me_c + d, n_ctx) for d in range(1, n_ctx)] if has_gather else []
    barrier = pltpu.get_barrier_semaphore()
    for peer in tp_peers:
        pl.semaphore_signal(barrier, inc=1, device_id={"tp": peer}, device_id_type=MESH)
    for peer in ctx_peers:
        pl.semaphore_signal(barrier, inc=1, device_id={"ctx": peer}, device_id_type=MESH)
    pl.semaphore_wait(barrier, len(tp_peers) + len(ctx_peers))

    if has_sum:
        sums = [
            remote(partial.at[peer], landed.at[d], rs_send.at[d], rs_recv.at[d], tp=peer)
            for d, peer in enumerate(tp_peers)
        ]
        for copy in sums:
            copy.start()
        total = partial[me_t].astype(F32)
        for d, copy in enumerate(sums):
            copy.wait_recv()
            total = total + landed[d].astype(F32)
        for copy in sums:
            copy.wait_send()

    field = stream[...]
    if mode == "first":
        sent = rms_forward(field, gain[...])[0].astype(BF16)
    elif mode in ("fwd", "fwd_last"):
        field = field + total
        fresh[...] = field
        if mode == "fwd":
            sent = rms_forward(field, gain[...])[0].astype(BF16)
    else:
        _, normed, inverse = rms_forward(field, gain[...])
        gain_part[...] = jnp.sum(total * normed, axis=0, keepdims=True)
        field = grad_res[...] + rms_backward(total, normed, inverse, gain[...])
        fresh[...] = field
        sent = field.astype(BF16)

    if has_gather:
        own[...] = sent
        copies = []
        for d, peer in enumerate(ctx_peers):
            copies.append(
                remote(own, out.at[me_c, me_t], z_send.at[d], z_recv.at[d], ctx=peer)
            )
        for d, peer in enumerate(tp_peers):
            copies.append(
                remote(own, out.at[me_c, me_t], t_send.at[0, d], t_recv.at[0, d], tp=peer)
            )
        for copy in copies:
            copy.start()
        out[me_c, me_t] = sent
        for d in range(n_ctx - 1):
            source = lax.rem(me_c + n_ctx - (d + 1), n_ctx)
            slot = out.at[source, me_t]
            remote(own, slot, z_send.at[d], z_recv.at[d], ctx=source).wait_recv()
            for k, peer in enumerate(tp_peers):
                copy = remote(slot, slot, t_send.at[d + 1, k], t_recv.at[d + 1, k], tp=peer)
                copy.start()
                copies.append(copy)
        for d in range(n_ctx):
            source = lax.rem(me_c + n_ctx - d, n_ctx)
            for k in range(n_tp - 1):
                origin = lax.rem(me_t + n_tp - (k + 1), n_tp)
                remote(
                    own, out.at[source, origin], t_send.at[d, k], t_recv.at[d, k], tp=origin
                ).wait_recv()
        for copy in copies:
            copy.wait_send()


IDS = {"first": 0, "fwd": 1, "fwd_last": 2, "bwd": 3, "bwd_last": 4}


def boundary(mode, stream, gain=None, partial=None, grad_res=None):
    n_ctx, n_tp = lax.axis_size("ctx"), lax.axis_size("tp")
    rows, width = stream.shape
    operands = []
    if partial is not None:
        operands.append(partial.reshape(n_tp, rows, width))
    operands.append(stream)
    if gain is not None:
        operands.append(gain.reshape(1, width))
    if grad_res is not None:
        operands.append(grad_res)
    shapes = []
    if mode != "first":
        shapes.append(jax.ShapeDtypeStruct((rows, width), F32))
    if grad_res is not None:
        shapes.append(jax.ShapeDtypeStruct((1, width), F32))
    scratch = []
    dma = pltpu.SemaphoreType.DMA
    if partial is not None:
        scratch += [pltpu.VMEM((n_tp - 1, rows, width), BF16), dma((n_tp - 1,)), dma((n_tp - 1,))]
    if mode in ("first", "fwd", "bwd"):
        shapes.append(jax.ShapeDtypeStruct((n_ctx, n_tp, rows, width), BF16))
        scratch += [
            pltpu.VMEM((rows, width), BF16),
            dma((n_ctx - 1,)),
            dma((n_ctx - 1,)),
            dma((n_ctx, n_tp - 1)),
            dma((n_ctx, n_tp - 1)),
        ]
    vmem = pl.BlockSpec(memory_space=pltpu.VMEM)
    outs = pl.pallas_call(
        functools.partial(boundary_kernel, mode, n_ctx, n_tp),
        out_shape=shapes,
        in_specs=[vmem] * len(operands),
        out_specs=[vmem] * len(shapes),
        scratch_shapes=scratch,
        name="boundary_" + mode,
        compiler_params=pltpu.CompilerParams(
            collective_id=IDS[mode], has_side_effects=True, vmem_limit_bytes=32 * 2**20
        ),
    )(*operands)
    outs = list(outs)
    if mode in ("first", "fwd", "bwd"):
        outs[-1] = outs[-1].reshape(n_ctx * n_tp * rows, width)
    return outs


def gains_kernel(sizes, x_ref, o_ref, cur, land_0, land_1, land_2, send, recv):
    lands = (land_0, land_1, land_2)
    axes = list(sizes)
    barrier = pltpu.get_barrier_semaphore()
    peers = {}
    count = 0
    for axis in axes:
        me = lax.axis_index(axis)
        peers[axis] = [lax.rem(me + d, sizes[axis]) for d in range(1, sizes[axis])]
        for peer in peers[axis]:
            pl.semaphore_signal(barrier, inc=1, device_id={axis: peer}, device_id_type=MESH)
            count += 1
    pl.semaphore_wait(barrier, count)
    total = x_ref[...]
    base = 0
    for step, axis in enumerate(axes):
        cur[step] = total
        copies = [
            remote(
                cur.at[step], lands[step].at[d], send.at[base + d], recv.at[base + d], **{axis: peer}
            )
            for d, peer in enumerate(peers[axis])
        ]
        for copy in copies:
            copy.start()
        me = lax.axis_index(axis)
        parts = []
        for d, copy in enumerate(copies):
            copy.wait_recv()
        acc = jnp.zeros_like(total)
        for position in range(sizes[axis]):
            offset = lax.rem(me + sizes[axis] - position, sizes[axis])
            slot = jnp.maximum(offset - 1, 0)
            acc = acc + jnp.where(offset == 0, total, lands[step][slot])
        total = acc
        for copy in copies:
            copy.wait_send()
        base += len(copies)
    o_ref[...] = total


def sum_gains(x):
    sizes = {axis: lax.axis_size(axis) for axis in ("dp", "ctx", "tp")}
    count = sum(n - 1 for n in sizes.values())
    vmem = pl.BlockSpec(memory_space=pltpu.VMEM)
    return pl.pallas_call(
        functools.partial(gains_kernel, sizes),
        out_shape=jax.ShapeDtypeStruct(x.shape, F32),
        in_specs=[vmem],
        out_specs=vmem,
        scratch_shapes=[pltpu.VMEM((3,) + x.shape, F32)]
        + [pltpu.VMEM((max(n - 1, 1),) + x.shape, F32) for n in sizes.values()]
        + [pltpu.SemaphoreType.DMA((count,)), pltpu.SemaphoreType.DMA((count,))],
        name="sum_gains",
        compiler_params=pltpu.CompilerParams(collective_id=5, has_side_effects=True),
    )(x)


NT = (((1,), (1,)), ((), ()))
NN = (((1,), (0,)), ((), ()))
TN = (((0,), (0,)), ((), ()))


def dot(a, b, dims):
    return lax.dot_general(a, b, dims, preferred_element_type=F32)


def turn(x):
    return pltpu.roll(x, x.shape[-1] // 2, axis=1)


def prepared(x, gain, cosine, sine):
    normed, plain, inverse = rms_forward(x, gain)
    return (normed * cosine + turn(normed) * sine).astype(BF16), plain, inverse


def soft_weights(scale, bq, q, k):
    rows = pl.program_id(2) * bq + lax.broadcasted_iota(jnp.int32, (bq, k.shape[0]), 0)
    cols = lax.broadcasted_iota(jnp.int32, (bq, k.shape[0]), 1)
    scores = jnp.where(cols <= rows, dot(q, k, NT) * scale, -jnp.inf)
    weights = jnp.exp(scores - jnp.max(scores, axis=-1, keepdims=True))
    return weights, jnp.sum(weights, axis=-1, keepdims=True)


def attend_kernel(
    scale, bq, q_ref, k_ref, v_ref, cq_ref, sq_ref, ck_ref, sk_ref, qg_ref, kg_ref, o_ref, k_rot
):
    @pl.when((pl.program_id(1) == 0) & (pl.program_id(2) == 0))
    def _():
        k_rot[...] = prepared(k_ref[...], kg_ref[...], ck_ref[...], sk_ref[...])[0]

    q = prepared(q_ref[...], qg_ref[...], cq_ref[...], sq_ref[...])[0]
    weights, total = soft_weights(scale, bq, q, k_rot[...])
    o_ref[...] = (dot(weights.astype(BF16), v_ref[...], NN) / total).astype(BF16)


def attend_back_kernel(
    scale,
    bq,
    q_ref,
    k_ref,
    v_ref,
    cq_ref,
    sq_ref,
    ck_ref,
    sk_ref,
    qg_ref,
    kg_ref,
    o_ref,
    do_ref,
    dq_ref,
    dk_ref,
    dv_ref,
    qp_ref,
    kp_ref,
    k_rot,
    dk_sum,
    dv_sum,
):
    head, member, block = pl.program_id(0), pl.program_id(1), pl.program_id(2)

    @pl.when((head == 0) & (member == 0) & (block == 0))
    def _():
        qp_ref[...] = jnp.zeros_like(qp_ref)
        kp_ref[...] = jnp.zeros_like(kp_ref)

    @pl.when((member == 0) & (block == 0))
    def _():
        k_rot[...] = prepared(k_ref[...], kg_ref[...], ck_ref[...], sk_ref[...])[0]
        dk_sum[...] = jnp.zeros_like(dk_sum)
        dv_sum[...] = jnp.zeros_like(dv_sum)

    q, plain, inverse = prepared(q_ref[...], qg_ref[...], cq_ref[...], sq_ref[...])
    k, do = k_rot[...], do_ref[...]
    weights, total = soft_weights(scale, bq, q, k)
    probs = weights / total
    delta = jnp.sum(do.astype(F32) * o_ref[...].astype(F32), axis=-1, keepdims=True)
    dscore = (probs * (dot(do, v_ref[...], NT) - delta)).astype(BF16)
    dk_sum[...] += dot(dscore, q, TN) * scale
    dv_sum[...] += dot(probs.astype(BF16), do, TN)
    grad = dot(dscore, k, NN) * scale
    grad = grad * cq_ref[...] - turn(grad) * sq_ref[...]
    qp_ref[...] += jnp.sum(grad * plain, axis=0, keepdims=True)
    dq_ref[...] = rms_backward(grad, plain, inverse, qg_ref[...]).astype(BF16)

    @pl.when((member == pl.num_programs(1) - 1) & (block == pl.num_programs(2) - 1))
    def _():
        _, k_plain, k_inverse = prepared(k_ref[...], kg_ref[...], ck_ref[...], sk_ref[...])
        grad_k = dk_sum[...]
        grad_k = grad_k * ck_ref[...] - turn(grad_k) * sk_ref[...]
        kp_ref[...] += jnp.sum(grad_k * k_plain, axis=0, keepdims=True)
        dk_ref[...] = rms_backward(grad_k, k_plain, k_inverse, kg_ref[...]).astype(BF16)
        dv_ref[...] = dv_sum[...].astype(BF16)


def attention(scale, group, query, keys, values, cosine, sine, query_gain, key_gain, *back):
    length, kv_width = keys.shape
    head_dim = cosine.shape[-1]
    kv_heads = kv_width // head_dim
    bq = min(length, 256)
    rows = pl.BlockSpec((bq, head_dim), lambda h, g, i: (i, h * group + g))
    keyed = pl.BlockSpec((length, head_dim), lambda h, g, i: (0, h))
    table_q = pl.BlockSpec((bq, head_dim), lambda h, g, i: (i, 0))
    table_k = pl.BlockSpec((length, head_dim), lambda h, g, i: (0, 0))
    flat = pl.BlockSpec((1, head_dim), lambda h, g, i: (0, 0))
    wide = jax.ShapeDtypeStruct((length, kv_width * group), BF16)
    narrow = jax.ShapeDtypeStruct((length, kv_width), BF16)
    part = jax.ShapeDtypeStruct((1, head_dim), F32)
    work = 2 * length * length * head_dim * kv_heads * group
    scratch = [pltpu.VMEM((length, head_dim), BF16)]
    if back:
        scratch += [pltpu.VMEM((length, head_dim), F32)] * 2
    return pl.pallas_call(
        functools.partial(attend_back_kernel if back else attend_kernel, scale, bq),
        grid=(kv_heads, group, length // bq),
        out_shape=(wide, narrow, narrow, part, part) if back else wide,
        in_specs=[rows, keyed, keyed, table_q, table_q, table_k, table_k, flat, flat]
        + [rows] * len(back),
        out_specs=(rows, keyed, keyed, flat, flat) if back else rows,
        scratch_shapes=scratch,
        name="attend_back" if back else "attend",
        cost_estimate=pl.CostEstimate(
            flops=work * (5 if back else 2), bytes_accessed=4 * length * 1024, transcendentals=0
        ),
        compiler_params=pltpu.CompilerParams(vmem_limit_bytes=40 * 2**20),
    )(
        query,
        keys,
        values,
        cosine,
        sine,
        cosine,
        sine,
        query_gain.reshape(1, -1),
        key_gain.reshape(1, -1),
        *back,
    )


def on_device(
    block_input,
    input_gain,
    query_weight,
    key_weight,
    value_weight,
    query_gain,
    key_gain,
    out_weight,
    post_gain,
    gate_weight,
    up_weight,
    down_weight,
    grad_output,
):
    local_rows, seq_local, width = block_input.shape
    assert seq_local == 1 and lax.axis_size("dp") == 2
    layers = input_gain.shape[0]
    head_dim = query_gain.shape[-1]
    heads = query_weight.shape[-1] // head_dim
    kv_heads = key_weight.shape[-1] // head_dim
    n_ctx, n_tp = lax.axis_size("ctx"), lax.axis_size("tp")
    block_rows = local_rows * n_tp
    length = block_rows * n_ctx
    scale = head_dim ** (-0.5)
    first_row = lax.axis_index("ctx") * block_rows
    cosine, sine = rope_tables(jnp.arange(length, dtype=F32), head_dim)
    piece = width // (2 * n_ctx)
    my_cols = (lax.axis_index("dp") * n_ctx + lax.axis_index("ctx")) * piece
    other_cols = ((1 - lax.axis_index("dp")) * n_ctx + lax.axis_index("ctx")) * piece
    swap = [(0, 1), (1, 0)]

    def mine(x):
        return lax.dynamic_slice_in_dim(x, first_row, block_rows, 0)

    def slices(x):
        parts = [lax.dynamic_slice_in_dim(x, at, piece, 1) for at in (my_cols, other_cols)]
        return jnp.concatenate(parts, axis=1)

    def settle(grad, axis):
        own, other = jnp.split(grad, 2, axis=axis)
        return own + lax.ppermute(other.astype(BF16), "dp", swap).astype(F32)

    def settle_rows(*products):
        other = [x[piece:].astype(BF16) for x in products]
        other = lax.ppermute(jnp.concatenate(other, axis=1), "dp", swap).astype(F32)
        out = []
        at = 0
        for x in products:
            out.append(x[:piece] + other[:, at : at + x.shape[1]])
            at += x.shape[1]
        return out

    hidden = block_input[:, 0]
    grad_hidden = grad_output[:, 0]
    grad_rows = lax.all_gather(grad_hidden.astype(BF16), ("ctx", "tp"), axis=0, tiled=True)
    (first_in,) = boundary("first", hidden, input_gain[0])
    kept = []
    for l in range(layers):
        query = dot(first_in, query_weight[l], NN)
        keys = dot(first_in, key_weight[l], NN)
        values = dot(first_in, value_weight[l], NN).astype(BF16)
        attend_args = (scale, heads // kv_heads, query, keys, values, cosine, sine)
        attend_args += (query_gain[l], key_gain[l])
        attended = attention(*attend_args)
        partial = dot(mine(attended), out_weight[l], NN).astype(BF16)
        mixed, second_in = boundary("fwd", hidden, post_gain[l], partial)
        gate = dot(second_in, gate_weight[l], NN)
        upward = dot(second_in, up_weight[l], NN)
        swish = (jax.nn.silu(gate) * upward).astype(BF16)
        partial = dot(mine(swish), down_weight[l], NN).astype(BF16)
        kept.append(
            (hidden, first_in, attend_args, attended, mixed, second_in, gate, upward, swish)
        )
        if l + 1 < layers:
            hidden, first_in = boundary("fwd", mixed, input_gain[l + 1], partial)
        else:
            hidden = mixed + lax.psum_scatter(
                partial, "tp", scatter_dimension=0, tiled=True
            ).astype(F32)

    grads = [None] * layers
    gains = [None] * layers
    for l in reversed(range(layers)):
        x_in, first_in, attend_args, attended, mixed, second_in, gate, upward, swish = kept[l]
        grad_swish = dot(grad_rows, down_weight[l], NT)
        sigma = jax.nn.sigmoid(gate)
        grad_gate = (grad_swish * upward * (sigma * (1.0 + gate * (1.0 - sigma)))).astype(BF16)
        grad_up = (grad_swish * (gate * sigma)).astype(BF16)
        partial = dot(mine(grad_gate), gate_weight[l], NT) + dot(mine(grad_up), up_weight[l], NT)
        grad_mixed, post_part, mixed_rows = boundary(
            "bwd", mixed, post_gain[l], partial.astype(BF16), grad_hidden
        )
        second_cols = slices(second_in)
        down_grad = settle(dot(swish, slices(grad_rows), TN), 1)
        gate_grad, up_grad = settle_rows(
            dot(second_cols, grad_gate, TN), dot(second_cols, grad_up, TN)
        )

        grad_heads = dot(mixed_rows, out_weight[l], NT).astype(BF16)
        out_grad = settle(dot(attended, slices(mixed_rows), TN), 1)
        query_bf, key_bf, value_bf, q_part, k_part = attention(*attend_args, attended, grad_heads)
        partial = (
            dot(mine(query_bf), query_weight[l], NT)
            + dot(mine(key_bf), key_weight[l], NT)
            + dot(mine(value_bf), value_weight[l], NT)
        ).astype(BF16)
        if l:
            grad_hidden, input_part, grad_rows = boundary(
                "bwd", x_in, input_gain[l], partial, grad_mixed
            )
        else:
            grad_hidden, input_part = boundary(
                "bwd_last", x_in, input_gain[l], partial, grad_mixed
            )
        first_cols = slices(first_in)
        query_grad, key_grad, value_grad = settle_rows(
            dot(first_cols, query_bf, TN),
            dot(first_cols, key_bf, TN),
            dot(first_cols, value_bf, TN),
        )
        grads[l] = (query_grad, key_grad, value_grad, out_grad, gate_grad, up_grad, down_grad)
        gains[l] = (input_part[0], q_part[0] / n_ctx, k_part[0] / n_ctx, post_part[0])
    stacked = [jnp.stack([part[m] for part in grads]) for m in range(7)]
    packed = jnp.concatenate([v for part in gains for v in part])
    sizes = [v.shape[0] for part in gains for v in part]
    padded = -(-packed.shape[0] // 1024) * 1024
    packed = jnp.pad(packed, (0, padded - packed.shape[0])).reshape(-1, 128)
    summed = sum_gains(packed).reshape(-1)
    pieces = []
    at = 0
    for size in sizes:
        pieces.append(summed[at : at + size])
        at += size
    gains = [jnp.stack([pieces[4 * l + m] for l in range(layers)]) for m in range(4)]
    return (
        hidden[:, None],
        grad_hidden[:, None],
        gains[0],
        stacked[0],
        stacked[1],
        stacked[2],
        gains[1],
        gains[2],
        stacked[3],
        gains[3],
        stacked[4],
        stacked[5],
        stacked[6],
    )


def rope_constants(length, head_dim):
    half = head_dim // 2
    frequency = np.float32(THETA) ** (-(np.float32(2.0) * np.arange(half, dtype=np.float32)) / np.float32(head_dim))
    angles = np.arange(length, dtype=np.float32)[:, None] * frequency.astype(np.float32)[None, :]
    cosine, sine = np.cos(angles), np.sin(angles)
    return (
        np.concatenate([cosine, cosine], axis=-1).astype(np.float32),
        np.concatenate([-sine, sine], axis=-1).astype(np.float32),
    )


def chunks(total, step=256):
    step = step if total % step == 0 else 128
    return [(at, step) for at in range(0, total, step)]


def fused_kernel(sz, *refs):
    (layers, n_ctx, n_tp, rows, width, heads, kv_heads, head_dim, ff) = sz
    block = rows * n_tp
    length = block * n_ctx
    group = heads // kv_heads
    q_w, k_w = heads * head_dim, kv_heads * head_dim
    piece = width // (2 * n_ctx)
    log2e = 1.4426950408889634
    scale = head_dim ** (-0.5)
    (x_ref, go_ref, ig_ref, pg_ref, qg_ref, kg_ref, cos_ref, sin_ref) = refs[:8]
    (wq_h, wk_h, wv_h, wo_h, wg_h, wu_h, wd_h) = refs[8:15]
    y_ref, gx_ref, gain_ref = refs[15:18]
    finals = refs[18:25]
    (wqkv, wo, wgu, wd, G, P, land, q_raw, k_raw, q_rot, k_rot, vals, att, swish, fa, fb, ggu, d_o, dqkv,
     dk_acc, dv_acc, mixed_s, xs_s, gm_s, gains, g_dp, g_ctx, g_tp,
     s_qkv, s_out, s_gu, s_dn, l_qkv, l_out, l_gu, l_dn,
     oq_ref, ok_ref, ov_ref, oo_ref, og_ref, ou_ref, od_ref, o_sem,
     w_sem, z_send, z_recv, t_send, t_recv, r_send, r_recv, d_send, d_recv, a_send, a_recv) = refs[25:]

    c, t, dp = lax.axis_index("ctx"), lax.axis_index("tp"), lax.axis_index("dp")
    tp_peers = [n_tp - 1 - t, t + 1 - 2 * lax.rem(t, 2), lax.rem(t + 2, n_tp)]
    ctx_peers = [lax.rem(c + d, n_ctx) for d in range(1, n_ctx)]
    other = 1 - dp
    pending = []

    loads = []

    def load(src, dst):
        copy = pltpu.make_async_copy(src, dst, w_sem.at[len(loads)])
        copy.start()
        loads.append(copy)

    for l in range(layers):
        load(wk_h.at[l], wqkv.at[l, :, pl.ds(q_w, k_w)])
        load(wv_h.at[l], wqkv.at[l, :, pl.ds(q_w + k_w, k_w)])
        load(wq_h.at[l], wqkv.at[l, :, pl.ds(0, q_w)])
        load(wo_h.at[l], wo.at[l])
        load(wg_h.at[l], wgu.at[l, :, pl.ds(0, ff)])
        load(wu_h.at[l], wgu.at[l, :, pl.ds(ff, ff)])
        load(wd_h.at[l], wd.at[l])

    barrier = pltpu.get_barrier_semaphore()
    for peer in tp_peers:
        pl.semaphore_signal(barrier, inc=1, device_id={"tp": peer}, device_id_type=MESH)
    for peer in ctx_peers:
        pl.semaphore_signal(barrier, inc=1, device_id={"ctx": peer}, device_id_type=MESH)
    pl.semaphore_signal(barrier, inc=1, device_id={"dp": other}, device_id_type=MESH)
    pl.semaphore_wait(barrier, n_tp + n_ctx - 1)

    def push(copy):
        copy.start()
        pending.append(copy)

    near = [1, n_ctx - 1] + list(range(2, n_ctx - 1))

    def source_of(d):
        return lax.rem(c + n_ctx - d, n_ctx)

    def spread(g, d):
        slot = G.at[g, source_of(d), t]
        for k, peer in enumerate(tp_peers):
            push(remote(slot, slot, t_send.at[g, d, k], t_recv.at[g, d, k], tp=peer))

    def complete(g, d):
        for k in range(n_tp - 1):
            origin = tp_peers[k]
            slot = G.at[g, source_of(d), origin]
            remote(slot, slot, t_send.at[g, d, k], t_recv.at[g, d, k], tp=origin).wait_recv()

    def start_gather(g, value, planes=False):
        own = G.at[g, c, t]
        G[g, c, t] = value
        mlp = layers <= g < 3 * layers
        if mlp:
            spread(g, 0)
        if not planes:
            for d in near:
                push(remote(own, own, z_send.at[g, d - 1], z_recv.at[g, d - 1], ctx=ctx_peers[d - 1]))
        if not mlp:
            spread(g, 0)

    def plane_send(g, *steps):
        own = G.at[g, c]
        for d in steps:
            push(remote(own, own, z_send.at[g, d - 1], z_recv.at[g, d - 1], ctx=ctx_peers[d - 1]))

    def plane_complete(g):
        for d in range(1, n_ctx):
            slot = G.at[g, source_of(d)]
            remote(slot, slot, z_send.at[g, d - 1], z_recv.at[g, d - 1], ctx=source_of(d)).wait_recv()

    def late_spread(g, *steps):
        for d in steps:
            source = source_of(d)
            slot = G.at[g, source, t]
            remote(slot, slot, z_send.at[g, d - 1], z_recv.at[g, d - 1], ctx=source).wait_recv()
            spread(g, d)

    def full_gather(g, work, early=None):
        if early is not None:
            early()
        late_spread(g, near[0], near[1])
        complete(g, 0)
        work(c)
        late_spread(g, *near[2:])
        for d in near:
            complete(g, d)
            work(source_of(d))

    def late_complete(g):
        for d in range(1, n_ctx):
            complete(g, d)

    wide = 512 if width % 512 == 0 else width

    def sum_part(r, k, at, peer):
        lanes = pl.ds(at, wide)
        src, dst = P.at[r, peer, :, lanes], land.at[r, k, :, lanes]
        return remote(src, dst, r_send.at[r, k, at // wide], r_recv.at[r, k, at // wide], tp=peer)

    def start_sum(r, value_of):
        for at in range(0, width, wide):
            P[r, :, :, at : at + wide] = value_of(at, at + wide).astype(BF16).reshape(n_tp, rows, wide)
            for k, peer in enumerate(tp_peers):
                push(sum_part(r, k, at, peer))

    def finish_sum(r):
        for at in range(0, width, wide):
            for k, peer in enumerate(tp_peers):
                sum_part(r, k, at, peer).wait_recv()
        total = P[r, t].astype(F32)
        for k in range(n_tp - 1):
            total = total + land[r, k].astype(F32)
        return total

    def others(body):
        def step(d, carry):
            body(d, lax.rem(c + n_ctx - d, n_ctx))
            return carry

        lax.fori_loop(1, n_ctx, step, 0)

    def tokens(g, s):
        return G[g, s].reshape(block, width)

    def qkv(l, s):
        x = tokens(l, s)
        cosine = cos_ref[pl.ds(pl.multiple_of(s * block, block), block), :]
        sine = sin_ref[pl.ds(pl.multiple_of(s * block, block), block), :]
        qg, kg = qg_ref[l : l + 1, :], kg_ref[l : l + 1, :]
        for at, step in chunks(q_w + 2 * k_w):
            y = dot(x, wqkv[l, :, at : at + step], NN)
            for sub in range(0, step, head_dim):
                yh = y[:, sub : sub + head_dim]
                h = (at + sub) // head_dim
                if h < heads:
                    q_raw[l, h, s] = yh
                    q_rot[l, h, s] = prepared(yh, qg, cosine, sine)[0]
                elif h < heads + kv_heads:
                    k_raw[l, h - heads, s] = yh
                    k_rot[l, h - heads, s] = prepared(yh, kg, cosine, sine)[0]
                else:
                    vals[l, h - heads - kv_heads, s] = yh.astype(BF16)

    def attend_block(l, i):
        at_row = i * block + lax.broadcasted_iota(jnp.int32, (block, length), 0)
        allowed = lax.broadcasted_iota(jnp.int32, (block, length), 1) <= at_row
        for h in range(heads):
            k = k_rot[l, h // group].reshape(length, head_dim)
            v = vals[l, h // group].reshape(length, head_dim)
            scores = dot(q_rot[l, h, i], k, NT) * (scale * log2e)
            weights = jnp.where(allowed, jnp.exp2(scores), 0.0)
            total = jnp.sum(weights, axis=-1, keepdims=True)
            out = dot(weights.astype(BF16), v, NN) / total
            att[l, i, :, h * head_dim : (h + 1) * head_dim] = out.astype(BF16)

    def out_partial(l):
        a = att[l, c]
        start_sum(l, lambda lo, hi: dot(a, wo[l, :, lo:hi], NN))

    def mlp_forward(l, s):
        x = tokens(layers + l, s)
        for at, step in chunks(ff):
            gate = dot(x, wgu[l, :, at : at + step], NN)
            up = dot(x, wgu[l, :, ff + at : ff + at + step], NN)
            sigma = jax.nn.sigmoid(gate)
            silu = gate * sigma
            swish[l, s, :, at : at + step] = (silu * up).astype(BF16)
            fa[l, s, :, at : at + step] = (up * (sigma * (1.0 + gate * (1.0 - sigma)))).astype(BF16)
            fb[l, s, :, at : at + step] = silu.astype(BF16)

    def down_partial(l):
        a = swish[l, c]
        start_sum(layers + l, lambda lo, hi: dot(a, wd[l, :, lo:hi], NN))

    def mlp_backward(l, s):
        x = tokens(2 * layers + l, s)
        for at, step in chunks(ff):
            grad = dot(x, wd[l, at : at + step, :], NT)
            ggu[l, s, :, at : at + step] = (grad * fa[l, s, :, at : at + step].astype(F32)).astype(BF16)
            ggu[l, s, :, ff + at : ff + at + step] = (
                grad * fb[l, s, :, at : at + step].astype(F32)
            ).astype(BF16)

    def mlp_back_partial(l):
        a = ggu[l, c]
        start_sum(2 * layers + l, lambda lo, hi: dot(a, wgu[l, lo:hi, :], NT))

    def heads_back(l, s):
        x = tokens(3 * layers + l, s)
        for at, step in chunks(q_w):
            d_o[s, :, at : at + step] = dot(x, wo[l, at : at + step, :], NT).astype(BF16)

    def attend_backward(l):
        dk_acc[...] = jnp.zeros_like(dk_acc)
        dv_acc[...] = jnp.zeros_like(dv_acc)
        half = length // 2
        per = n_ctx // 2
        causal = lax.broadcasted_iota(jnp.int32, (half, half), 1) <= lax.broadcasted_iota(
            jnp.int32, (half, half), 0
        )
        qg, kg = qg_ref[l : l + 1, :], kg_ref[l : l + 1, :]

        def one_head(h, part):
            lanes = pl.ds(pl.multiple_of(h * head_dim, head_dim), head_dim)
            kv = h // group
            for i in range(2):
                span = slice(i * per, (i + 1) * per)
                extent = (i + 1) * half
                q = q_rot[l, h, span].reshape(half, head_dim)
                do = d_o[span, :, lanes].reshape(half, head_dim)
                a = att[l, span, :, lanes].reshape(half, head_dim)
                k = k_rot[l, kv, : (i + 1) * per].reshape(extent, head_dim)
                v = vals[l, kv, : (i + 1) * per].reshape(extent, head_dim)
                weights = jnp.exp2(dot(q, k, NT) * (scale * log2e))
                last = jnp.where(causal, weights[:, i * half :], 0.0)
                weights = jnp.concatenate([weights[:, :half], last], axis=1) if i else last
                probs = weights / jnp.sum(weights, axis=-1, keepdims=True)
                delta = jnp.sum(do.astype(F32) * a.astype(F32), axis=-1, keepdims=True)
                dscore = (probs * (dot(do, v, NT) - delta)).astype(BF16)
                dk_acc[kv, :extent] += dot(dscore, q, TN)
                dv_acc[kv, :extent] += dot(probs.astype(BF16), do, TN)
                cosine = cos_ref[i * half : (i + 1) * half, :]
                sine = sin_ref[i * half : (i + 1) * half, :]
                grad = dot(dscore, k, NN) * scale
                grad = grad * cosine - turn(grad) * sine
                _, plain, inverse = rms_forward(q_raw[l, h, span].reshape(half, head_dim), qg)
                part = part + jnp.sum(grad * plain, axis=0, keepdims=True)
                grad = rms_backward(grad, plain, inverse, qg).astype(BF16)
                dqkv[span, :, lanes] = grad.reshape(per, block, head_dim)
            return part

        q_part = lax.fori_loop(0, heads, one_head, jnp.zeros((1, head_dim), F32))
        k_part = jnp.zeros((1, head_dim), F32)
        for kv in range(kv_heads):
            grad = dk_acc[kv] * scale
            grad = grad * cos_ref[...] - turn(grad) * sin_ref[...]
            _, plain, inverse = rms_forward(k_raw[l, kv].reshape(length, head_dim), kg)
            k_part = k_part + jnp.sum(grad * plain, axis=0, keepdims=True)
            grad = rms_backward(grad, plain, inverse, kg).astype(BF16)
            at = q_w + kv * head_dim
            dqkv[:, :, at : at + head_dim] = grad.reshape(n_ctx, block, head_dim)
            at += k_w
            dqkv[:, :, at : at + head_dim] = dv_acc[kv].astype(BF16).reshape(n_ctx, block, head_dim)
        at = 2 * layers
        gains[at : at + 1, 2 * l * head_dim : (2 * l + 1) * head_dim] = q_part / n_ctx
        gains[at : at + 1, (2 * l + 1) * head_dim : (2 * l + 2) * head_dim] = k_part / n_ctx

    def qkv_back_partial(l):
        a = dqkv[c]
        start_sum(3 * layers + l, lambda lo, hi: dot(a, wqkv[l, lo:hi, :], NT))

    my_cols = pl.ds(pl.multiple_of((dp * n_ctx + c) * piece, piece), piece)
    other_cols = pl.ds(pl.multiple_of((other * n_ctx + c) * piece, piece), piece)

    def columns(g):
        parts = [G[g, :, :, :, cols].reshape(length, piece) for cols in (my_cols, other_cols)]
        return jnp.concatenate(parts, axis=1)

    def exchange(i, src, dst):
        push(remote(src, dst, d_send.at[i], d_recv.at[i], dp=other))

    def grads_mlp(l):
        x = columns(layers + l)
        for at, step in chunks(2 * ff):
            g = dot(x, ggu[l, :, :, at : at + step].reshape(length, step), TN)
            ref, base = (og_ref, at) if at < ff else (ou_ref, at - ff)
            ref[l, :, base : base + step] = g[:piece]
            s_gu[l, :, at : at + step] = g[piece:].astype(BF16)
        exchange(4 * l, s_gu.at[l], l_gu.at[l])
        x = columns(2 * layers + l)
        for at, step in chunks(ff):
            g = dot(swish[l, :, :, at : at + step].reshape(length, step), x, TN)
            od_ref[l, at : at + step, :] = g[:, :piece]
            s_dn[l, at : at + step, :] = g[:, piece:].astype(BF16)
        exchange(4 * l + 1, s_dn.at[l], l_dn.at[l])

    def grads_out(l):
        x = columns(3 * layers + l)
        for at, step in chunks(q_w):
            g = dot(att[l, :, :, at : at + step].reshape(length, step), x, TN)
            oo_ref[l, at : at + step, :] = g[:, :piece]
            s_out[l, at : at + step, :] = g[:, piece:].astype(BF16)
        exchange(4 * l + 2, s_out.at[l], l_out.at[l])

    def grads_qkv(l):
        x = columns(l)
        for at, step in chunks(q_w + 2 * k_w):
            g = dot(x, dqkv[:, :, at : at + step].reshape(length, step), TN)
            if at < q_w:
                oq_ref[l, :, at : at + step] = g[:piece]
            elif at < q_w + k_w:
                ok_ref[l, :, at - q_w : at - q_w + step] = g[:piece]
            else:
                ov_ref[l, :, at - q_w - k_w : at - q_w - k_w + step] = g[:piece]
            s_qkv[l, :, at : at + step] = g[piece:].astype(BF16)
        exchange(4 * l + 3, s_qkv.at[l], l_qkv.at[l])

    def settle(l):
        def landed(i, dst):
            remote(dst, dst, d_send.at[i], d_recv.at[i], dp=other).wait_recv()

        landed(4 * l, l_gu.at[l])
        og_ref[l] += l_gu[l, :, :ff].astype(F32)
        ou_ref[l] += l_gu[l, :, ff:].astype(F32)
        landed(4 * l + 1, l_dn.at[l])
        od_ref[l] += l_dn[l].astype(F32)
        landed(4 * l + 2, l_out.at[l])
        oo_ref[l] += l_out[l].astype(F32)
        landed(4 * l + 3, l_qkv.at[l])
        oq_ref[l] += l_qkv[l, :, :q_w].astype(F32)
        ok_ref[l] += l_qkv[l, :, q_w : q_w + k_w].astype(F32)
        ov_ref[l] += l_qkv[l, :, q_w + k_w :].astype(F32)

    gains[...] = jnp.zeros_like(gains)

    leaving = []

    def deliver(l):
        staged = (oq_ref, ok_ref, ov_ref, oo_ref, og_ref, ou_ref, od_ref)
        for i, (src, dst) in enumerate(zip(staged, finals)):
            copy = pltpu.make_async_copy(src.at[l], dst.at[l], o_sem.at[i, l])
            copy.start()
            leaving.append(copy)

    stages = (("dp", dp, [other], g_dp, 0), ("ctx", c, ctx_peers, g_ctx, 1), ("tp", t, [lax.rem(t + k, n_tp) for k in range(1, n_tp)], g_tp, n_ctx))

    def gain_start(stage, value):
        axis, me, peers, buf, base = stages[stage]
        buf[me] = value
        for i, peer in enumerate(peers):
            own = buf.at[me]
            push(remote(own, own, a_send.at[base + i], a_recv.at[base + i], **{axis: peer}))

    def gain_finish(stage):
        axis, me, peers, buf, base = stages[stage]
        n = len(peers) + 1
        for i in range(n - 1):
            source = lax.rem(me + n - (i + 1), n)
            slot = buf.at[source]
            remote(slot, slot, a_send.at[base + i], a_recv.at[base + i], **{axis: source}).wait_recv()
        value = buf[0]
        for i in range(1, n):
            value = value + buf[i]
        return value

    top = layers - 1
    X1, X2, GR, MR = (lambda l: l), (lambda l: layers + l), (lambda l: 2 * layers + l), (lambda l: 3 * layers + l)

    x_in = x_ref[:, 0, :]
    xs_s[0] = x_in
    start_gather(X1(0), rms_forward(x_in, ig_ref[0:1, :])[0].astype(BF16))
    for l in range(layers):
        for i in range(3):
            loads[7 * l + i].wait()
        full_gather(X1(l), lambda s: qkv(l, s))
        if l == 0:
            start_gather(GR(top), go_ref[:, 0, :].astype(BF16), True)
        else:
            plane_send(GR(top), 2)
        attend_block(l, c)
        loads[7 * l + 3].wait()
        out_partial(l)
        attend_block(l, source_of(1))
        if l == 0:
            complete(GR(top), 0)
            plane_send(GR(top), 1, 3)
        attend_block(l, source_of(2))
        mixed = xs_s[l] + finish_sum(l)
        mixed_s[l] = mixed
        start_gather(X2(l), rms_forward(mixed, pg_ref[l : l + 1, :])[0].astype(BF16), l < top)
        for i in range(4, 7):
            loads[7 * l + i].wait()
        attend_block(l, source_of(3))
        complete(X2(l), 0)
        mlp_forward(l, c)
        if l < top:
            down_partial(l)
            x_next = mixed_s[l] + finish_sum(layers + l)
            xs_s[l + 1] = x_next
            start_gather(X1(l + 1), rms_forward(x_next, ig_ref[l + 1 : l + 2, :])[0].astype(BF16))

    for l in reversed(range(layers)):
        if l < top:
            complete(GR(l), 0)
        mlp_backward(l, c)
        mlp_back_partial(l)
        if l == top:
            down_partial(l)
            plane_complete(GR(top))
        else:
            others(lambda d, s: mlp_backward(l + 1, s))
        grad_res = go_ref[:, 0, :] if l == top else gm_s[1]
        _, normed, inverse = rms_forward(mixed_s[l], pg_ref[l : l + 1, :])
        total = finish_sum(2 * layers + l)
        gains[layers + l : layers + l + 1, :] = jnp.sum(total * normed, axis=0, keepdims=True)
        grad_mixed = grad_res + rms_backward(total, normed, inverse, pg_ref[l : l + 1, :])
        gm_s[0] = grad_mixed
        start_gather(MR(l), grad_mixed.astype(BF16))
        if l == top:
            y_ref[...] = mixed_s[l] + finish_sum(layers + l)

        def early():
            if l < top:
                grads_mlp(l + 1)
                plane_complete(X2(l))
                others(lambda d, s: mlp_forward(l, s))

        full_gather(MR(l), lambda s: heads_back(l, s), early)
        late_spread(X2(l) if l == top else GR(l), 1, 2, 3)
        if l:
            plane_send(X2(l - 1), 1, 3)
        attend_backward(l)
        qkv_back_partial(l)
        if l == 0:
            plain = tokens(X1(l), c).astype(F32)
            back = P[3 * layers + l].reshape(block, width).astype(F32)
            gains[l : l + 1, :] = jnp.sum(back * plain, axis=0, keepdims=True) / ig_ref[l : l + 1, :]
            gain_start(0, gains[...])
        else:
            plane_send(X2(l - 1), 2)
        grads_out(l)
        if l == 0:
            gain_start(1, gain_finish(0))
        grads_qkv(l)
        if l:
            _, normed, inverse = rms_forward(xs_s[l], ig_ref[l : l + 1, :])
            total = finish_sum(3 * layers + l)
            gains[l : l + 1, :] = jnp.sum(total * normed, axis=0, keepdims=True)
            grad_x = gm_s[0] + rms_backward(total, normed, inverse, ig_ref[l : l + 1, :])
            gm_s[1] = grad_x
            start_gather(GR(l - 1), grad_x.astype(BF16))
            late_complete(X2(l))
            others(lambda d, s: mlp_forward(l, s))
        if l == 0:
            late_complete(GR(l))
            others(lambda d, s: mlp_backward(l, s))
            gain_start(2, gain_finish(1))
            grads_mlp(l)
            settle(l + 1)
            deliver(l + 1)
            _, normed, inverse = rms_forward(xs_s[l], ig_ref[l : l + 1, :])
            total = finish_sum(3 * layers + l)
            gx_ref[...] = gm_s[0] + rms_backward(total, normed, inverse, ig_ref[l : l + 1, :])
            settle(l)
            deliver(l)
            gain_ref[...] = gain_finish(2)

    for copy in leaving:
        copy.wait()
    for copy in pending:
        copy.wait_send()


def fused(sz, *operands):
    (layers, n_ctx, n_tp, rows, width, heads, kv_heads, head_dim, ff) = sz
    block = rows * n_tp
    length = block * n_ctx
    q_w, k_w = heads * head_dim, kv_heads * head_dim
    piece = width // (2 * n_ctx)
    vm = lambda *shape: pltpu.VMEM(shape, BF16)
    vf = lambda *shape: pltpu.VMEM(shape, F32)
    dma = pltpu.SemaphoreType.DMA
    sd = lambda *shape: jax.ShapeDtypeStruct(shape, F32)
    n_g = 4 * layers
    scratch = [
        vm(layers, width, q_w + 2 * k_w),
        vm(layers, q_w, width),
        vm(layers, width, 2 * ff),
        vm(layers, ff, width),
        vm(n_g, n_ctx, n_tp, rows, width),
        vm(n_g, n_tp, rows, width),
        vm(n_g, n_tp - 1, rows, width),
        vf(layers, heads, n_ctx, block, head_dim),
        vf(layers, kv_heads, n_ctx, block, head_dim),
        vm(layers, heads, n_ctx, block, head_dim),
        vm(layers, kv_heads, n_ctx, block, head_dim),
        vm(layers, kv_heads, n_ctx, block, head_dim),
        vm(layers, n_ctx, block, q_w),
        vm(layers, n_ctx, block, ff),
        vm(layers, n_ctx, block, ff),
        vm(layers, n_ctx, block, ff),
        vm(layers, n_ctx, block, 2 * ff),
        vm(n_ctx, block, q_w),
        vm(n_ctx, block, q_w + 2 * k_w),
        vf(kv_heads, length, head_dim),
        vf(kv_heads, length, head_dim),
        vf(layers, rows, width),
        vf(layers, rows, width),
        vf(2, rows, width),
        vf(8, width),
        vf(2, 8, width),
        vf(n_ctx, 8, width),
        vf(n_tp, 8, width),
    ]
    outs = [
        sd(layers, piece, q_w),
        sd(layers, piece, k_w),
        sd(layers, piece, k_w),
        sd(layers, q_w, piece),
        sd(layers, piece, ff),
        sd(layers, piece, ff),
        sd(layers, ff, piece),
    ]
    for _ in range(2):
        scratch += [
            vm(layers, piece, q_w + 2 * k_w),
            vm(layers, q_w, piece),
            vm(layers, piece, 2 * ff),
            vm(layers, ff, piece),
        ]
    scratch += [pltpu.VMEM(out.shape, F32) for out in outs]
    scratch += [
        dma((7, layers)),
        dma((7 * layers,)),
        dma((n_g, n_ctx - 1)),
        dma((n_g, n_ctx - 1)),
        dma((n_g, n_ctx, n_tp - 1)),
        dma((n_g, n_ctx, n_tp - 1)),
        dma((n_g, n_tp - 1, 2)),
        dma((n_g, n_tp - 1, 2)),
        dma((4 * layers,)),
        dma((4 * layers,)),
        dma((n_ctx + n_tp - 1,)),
        dma((n_ctx + n_tp - 1,)),
    ]
    vmem = pl.BlockSpec(memory_space=pltpu.VMEM)
    hbm = pl.BlockSpec(memory_space=pl.ANY)
    return pl.pallas_call(
        functools.partial(fused_kernel, sz),
        out_shape=[
            sd(rows, width),
            sd(rows, width),
            sd(8, width),
        ]
        + outs,
        in_specs=[vmem] * 8 + [hbm] * 7,
        out_specs=[vmem] * 3 + [hbm] * 7,
        scratch_shapes=scratch,
        name="two_layers",
        compiler_params=pltpu.CompilerParams(
            collective_id=6, has_side_effects=True, vmem_limit_bytes=60 * 2**20
        ),
    )(*operands)


def finish_kernel(layers, head_dim, *refs):
    y_in, gx_in, gain_in = refs[:3]
    grads_in = refs[3:10]
    y, gx, input_gain, query_gain, key_gain, post_gain = refs[10:16]
    grads_out = refs[16:23]
    held = refs[23:30]
    sems_in, sems_out = refs[30:]
    arrive, leave = [], []
    for l in reversed(range(layers)):
        for i, (src, mid, dst) in enumerate(zip(grads_in, held, grads_out)):
            arrive.append(pltpu.make_async_copy(src.at[l], mid.at[l], sems_in.at[i, l]))
            leave.append(pltpu.make_async_copy(mid.at[l], dst.at[l], sems_out.at[i, l]))
    for copy in arrive:
        copy.start()
    for first, second in zip(arrive, leave):
        first.wait()
        second.start()
    y[:, 0, :] = y_in[...]
    gx[:, 0, :] = gx_in[...]
    input_gain[...] = gain_in[:layers, :]
    post_gain[...] = gain_in[layers : 2 * layers, :]
    for l in range(layers):
        at = 2 * l * head_dim
        query_gain[l : l + 1, :] = gain_in[2 * layers : 2 * layers + 1, at : at + head_dim]
        key_gain[l : l + 1, :] = gain_in[2 * layers : 2 * layers + 1, at + head_dim : at + 2 * head_dim]
    for copy in leave:
        copy.wait()


def finish(layers, head_dim, y, gx, gains, *grads):
    rows, width = y.shape
    sd = lambda *shape: jax.ShapeDtypeStruct(shape, F32)
    vmem = pl.BlockSpec(memory_space=pltpu.VMEM)
    hbm = pl.BlockSpec(memory_space=pl.ANY)
    return pl.pallas_call(
        functools.partial(finish_kernel, layers, head_dim),
        out_shape=[
            sd(rows, 1, width),
            sd(rows, 1, width),
            sd(layers, width),
            sd(layers, head_dim),
            sd(layers, head_dim),
            sd(layers, width),
        ]
        + [sd(*grad.shape) for grad in grads],
        in_specs=[vmem] * 3 + [hbm] * len(grads),
        out_specs=[vmem] * 6 + [hbm] * len(grads),
        scratch_shapes=[pltpu.VMEM(grad.shape, F32) for grad in grads]
        + [pltpu.SemaphoreType.DMA((len(grads), layers))] * 2,
        name="finish",
    )(y, gx, gains, *grads)


def on_device_fused(
    block_input,
    input_gain,
    query_weight,
    key_weight,
    value_weight,
    query_gain,
    key_gain,
    out_weight,
    post_gain,
    gate_weight,
    up_weight,
    down_weight,
    grad_output,
):
    rows, _, width = block_input.shape
    layers = input_gain.shape[0]
    head_dim = query_gain.shape[-1]
    n_ctx, n_tp = lax.axis_size("ctx"), lax.axis_size("tp")
    sz = (
        layers,
        n_ctx,
        n_tp,
        rows,
        width,
        query_weight.shape[-1] // head_dim,
        key_weight.shape[-1] // head_dim,
        head_dim,
        gate_weight.shape[-1],
    )
    cosine, sine = rope_constants(rows * n_tp * n_ctx, head_dim)
    y, gx, gains, *grads = fused(
        sz,
        block_input,
        grad_output,
        input_gain,
        post_gain,
        query_gain,
        key_gain,
        cosine,
        sine,
        query_weight,
        key_weight,
        value_weight,
        out_weight,
        gate_weight,
        up_weight,
        down_weight,
    )
    y, gx, input_part, q_part, k_part, post_part, wq, wk, wv, wo, wg, wu, wd = finish(
        layers, head_dim, y, gx, gains, *grads
    )
    return (y, gx, input_part, wq, wk, wv, q_part, k_part, wo, post_part, wg, wu, wd)


def on_any_device(*arrays):
    rows, _, width = arrays[0].shape
    n_ctx, n_tp = lax.axis_size("ctx"), lax.axis_size("tp")
    small = n_tp == 4 and n_ctx == 4 and arrays[1].shape[0] == 2 and rows * n_tp * n_ctx <= 512 and (width // (2 * n_ctx)) % 128 == 0
    return (on_device_fused if small else on_device)(*arrays)


def solution(mesh):
    placed = (
        P(("ctx", "tp"), "dp", None),
        P(),
        P(None, None, "tp"),
        P(None, None, "tp"),
        P(None, None, "tp"),
        P(),
        P(),
        P(None, "tp", None),
        P(),
        P(None, None, "tp"),
        P(None, None, "tp"),
        P(None, "tp", None),
        P(("ctx", "tp"), "dp", None),
    )
    return jax.shard_map(
        on_any_device,
        mesh=mesh,
        in_specs=placed,
        out_specs=(
            P(("ctx", "tp"), "dp", None),
            P(("ctx", "tp"), "dp", None),
            P(),
            P(None, ("dp", "ctx"), "tp"),
            P(None, ("dp", "ctx"), "tp"),
            P(None, ("dp", "ctx"), "tp"),
            P(),
            P(),
            P(None, "tp", ("dp", "ctx")),
            P(),
            P(None, ("dp", "ctx"), "tp"),
            P(None, ("dp", "ctx"), "tp"),
            P(None, "tp", ("dp", "ctx")),
        ),
        check_vma=False,
    )
```

```python
import functools

import jax
import jax.numpy as jnp
import numpy as np
from jax import lax
from jax.experimental import pallas as pl
from jax.experimental.pallas import tpu as pltpu
from jax.sharding import PartitionSpec as P

EPS = 1e-06
THETA = 1000000.0
MESH = pl.DeviceIdType.MESH
F32 = jnp.float32
BF16 = jnp.bfloat16


def rms_forward(field, gain):
    inverse = lax.rsqrt(jnp.mean(field * field, axis=-1, keepdims=True) + EPS)
    normed = field * inverse
    return (normed * gain, normed, inverse)


def rms_backward(grad_out, normed, inverse, gain):
    scaled = grad_out * gain
    return inverse * (scaled - normed * jnp.mean(scaled * normed, axis=-1, keepdims=True))


def rope_tables(positions, head_dim):
    half = head_dim // 2
    frequency = THETA ** (-(2.0 * jnp.arange(half, dtype=F32)) / head_dim)
    angles = positions[:, None] * frequency[None, :]
    cosine, sine = jnp.cos(angles), jnp.sin(angles)
    return (jnp.concatenate([cosine, cosine], axis=-1), jnp.concatenate([-sine, sine], axis=-1))


def remote(src, dst, send, recv, **where):
    return pltpu.make_async_remote_copy(
        src_ref=src,
        dst_ref=dst,
        send_sem=send,
        recv_sem=recv,
        device_id=where,
        device_id_type=MESH,
    )


def boundary_kernel(mode, n_ctx, n_tp, *refs):
    refs = list(refs)
    has_sum = mode != "first"
    has_gather = mode in ("first", "fwd", "bwd")
    partial = refs.pop(0) if has_sum else None
    stream = refs.pop(0)
    gain = refs.pop(0) if mode not in ("fwd_last",) else None
    grad_res = refs.pop(0) if mode in ("bwd", "bwd_last") else None
    fresh = refs.pop(0) if mode != "first" else None
    gain_part = refs.pop(0) if mode in ("bwd", "bwd_last") else None
    out = refs.pop(0) if has_gather else None
    if has_sum:
        landed, rs_send, rs_recv = refs.pop(0), refs.pop(0), refs.pop(0)
    if has_gather:
        own, z_send, z_recv, t_send, t_recv = refs

    me_c = lax.axis_index("ctx")
    me_t = lax.axis_index("tp")
    tp_peers = [lax.rem(me_t + d, n_tp) for d in range(1, n_tp)]
    ctx_peers = [lax.rem(me_c + d, n_ctx) for d in range(1, n_ctx)] if has_gather else []
    barrier = pltpu.get_barrier_semaphore()
    for peer in tp_peers:
        pl.semaphore_signal(barrier, inc=1, device_id={"tp": peer}, device_id_type=MESH)
    for peer in ctx_peers:
        pl.semaphore_signal(barrier, inc=1, device_id={"ctx": peer}, device_id_type=MESH)
    pl.semaphore_wait(barrier, len(tp_peers) + len(ctx_peers))

    if has_sum:
        sums = [
            remote(partial.at[peer], landed.at[d], rs_send.at[d], rs_recv.at[d], tp=peer)
            for d, peer in enumerate(tp_peers)
        ]
        for copy in sums:
            copy.start()
        total = partial[me_t].astype(F32)
        for d, copy in enumerate(sums):
            copy.wait_recv()
            total = total + landed[d].astype(F32)
        for copy in sums:
            copy.wait_send()

    field = stream[...]
    if mode == "first":
        sent = rms_forward(field, gain[...])[0].astype(BF16)
    elif mode in ("fwd", "fwd_last"):
        field = field + total
        fresh[...] = field
        if mode == "fwd":
            sent = rms_forward(field, gain[...])[0].astype(BF16)
    else:
        _, normed, inverse = rms_forward(field, gain[...])
        gain_part[...] = jnp.sum(total * normed, axis=0, keepdims=True)
        field = grad_res[...] + rms_backward(total, normed, inverse, gain[...])
        fresh[...] = field
        sent = field.astype(BF16)

    if has_gather:
        own[...] = sent
        copies = []
        for d, peer in enumerate(ctx_peers):
            copies.append(
                remote(own, out.at[me_c, me_t], z_send.at[d], z_recv.at[d], ctx=peer)
            )
        for d, peer in enumerate(tp_peers):
            copies.append(
                remote(own, out.at[me_c, me_t], t_send.at[0, d], t_recv.at[0, d], tp=peer)
            )
        for copy in copies:
            copy.start()
        out[me_c, me_t] = sent
        for d in range(n_ctx - 1):
            source = lax.rem(me_c + n_ctx - (d + 1), n_ctx)
            slot = out.at[source, me_t]
            remote(own, slot, z_send.at[d], z_recv.at[d], ctx=source).wait_recv()
            for k, peer in enumerate(tp_peers):
                copy = remote(slot, slot, t_send.at[d + 1, k], t_recv.at[d + 1, k], tp=peer)
                copy.start()
                copies.append(copy)
        for d in range(n_ctx):
            source = lax.rem(me_c + n_ctx - d, n_ctx)
            for k in range(n_tp - 1):
                origin = lax.rem(me_t + n_tp - (k + 1), n_tp)
                remote(
                    own, out.at[source, origin], t_send.at[d, k], t_recv.at[d, k], tp=origin
                ).wait_recv()
        for copy in copies:
            copy.wait_send()


IDS = {"first": 0, "fwd": 1, "fwd_last": 2, "bwd": 3, "bwd_last": 4}


def boundary(mode, stream, gain=None, partial=None, grad_res=None):
    n_ctx, n_tp = lax.axis_size("ctx"), lax.axis_size("tp")
    rows, width = stream.shape
    operands = []
    if partial is not None:
        operands.append(partial.reshape(n_tp, rows, width))
    operands.append(stream)
    if gain is not None:
        operands.append(gain.reshape(1, width))
    if grad_res is not None:
        operands.append(grad_res)
    shapes = []
    if mode != "first":
        shapes.append(jax.ShapeDtypeStruct((rows, width), F32))
    if grad_res is not None:
        shapes.append(jax.ShapeDtypeStruct((1, width), F32))
    scratch = []
    dma = pltpu.SemaphoreType.DMA
    if partial is not None:
        scratch += [pltpu.VMEM((n_tp - 1, rows, width), BF16), dma((n_tp - 1,)), dma((n_tp - 1,))]
    if mode in ("first", "fwd", "bwd"):
        shapes.append(jax.ShapeDtypeStruct((n_ctx, n_tp, rows, width), BF16))
        scratch += [
            pltpu.VMEM((rows, width), BF16),
            dma((n_ctx - 1,)),
            dma((n_ctx - 1,)),
            dma((n_ctx, n_tp - 1)),
            dma((n_ctx, n_tp - 1)),
        ]
    vmem = pl.BlockSpec(memory_space=pltpu.VMEM)
    outs = pl.pallas_call(
        functools.partial(boundary_kernel, mode, n_ctx, n_tp),
        out_shape=shapes,
        in_specs=[vmem] * len(operands),
        out_specs=[vmem] * len(shapes),
        scratch_shapes=scratch,
        name="boundary_" + mode,
        compiler_params=pltpu.CompilerParams(
            collective_id=IDS[mode], has_side_effects=True, vmem_limit_bytes=32 * 2**20
        ),
    )(*operands)
    outs = list(outs)
    if mode in ("first", "fwd", "bwd"):
        outs[-1] = outs[-1].reshape(n_ctx * n_tp * rows, width)
    return outs


def gains_kernel(sizes, x_ref, o_ref, cur, land_0, land_1, land_2, send, recv):
    lands = (land_0, land_1, land_2)
    axes = list(sizes)
    barrier = pltpu.get_barrier_semaphore()
    peers = {}
    count = 0
    for axis in axes:
        me = lax.axis_index(axis)
        peers[axis] = [lax.rem(me + d, sizes[axis]) for d in range(1, sizes[axis])]
        for peer in peers[axis]:
            pl.semaphore_signal(barrier, inc=1, device_id={axis: peer}, device_id_type=MESH)
            count += 1
    pl.semaphore_wait(barrier, count)
    total = x_ref[...]
    base = 0
    for step, axis in enumerate(axes):
        cur[step] = total
        copies = [
            remote(
                cur.at[step], lands[step].at[d], send.at[base + d], recv.at[base + d], **{axis: peer}
            )
            for d, peer in enumerate(peers[axis])
        ]
        for copy in copies:
            copy.start()
        me = lax.axis_index(axis)
        parts = []
        for d, copy in enumerate(copies):
            copy.wait_recv()
        acc = jnp.zeros_like(total)
        for position in range(sizes[axis]):
            offset = lax.rem(me + sizes[axis] - position, sizes[axis])
            slot = jnp.maximum(offset - 1, 0)
            acc = acc + jnp.where(offset == 0, total, lands[step][slot])
        total = acc
        for copy in copies:
            copy.wait_send()
        base += len(copies)
    o_ref[...] = total


def sum_gains(x):
    sizes = {axis: lax.axis_size(axis) for axis in ("dp", "ctx", "tp")}
    count = sum(n - 1 for n in sizes.values())
    vmem = pl.BlockSpec(memory_space=pltpu.VMEM)
    return pl.pallas_call(
        functools.partial(gains_kernel, sizes),
        out_shape=jax.ShapeDtypeStruct(x.shape, F32),
        in_specs=[vmem],
        out_specs=vmem,
        scratch_shapes=[pltpu.VMEM((3,) + x.shape, F32)]
        + [pltpu.VMEM((max(n - 1, 1),) + x.shape, F32) for n in sizes.values()]
        + [pltpu.SemaphoreType.DMA((count,)), pltpu.SemaphoreType.DMA((count,))],
        name="sum_gains",
        compiler_params=pltpu.CompilerParams(collective_id=5, has_side_effects=True),
    )(x)


NT = (((1,), (1,)), ((), ()))
NN = (((1,), (0,)), ((), ()))
TN = (((0,), (0,)), ((), ()))


def dot(a, b, dims):
    return lax.dot_general(a, b, dims, preferred_element_type=F32)


def turn(x):
    return pltpu.roll(x, x.shape[-1] // 2, axis=1)


def prepared(x, gain, cosine, sine):
    normed, plain, inverse = rms_forward(x, gain)
    return (normed * cosine + turn(normed) * sine).astype(BF16), plain, inverse


def soft_weights(scale, bq, q, k):
    rows = pl.program_id(2) * bq + lax.broadcasted_iota(jnp.int32, (bq, k.shape[0]), 0)
    cols = lax.broadcasted_iota(jnp.int32, (bq, k.shape[0]), 1)
    scores = jnp.where(cols <= rows, dot(q, k, NT) * scale, -jnp.inf)
    weights = jnp.exp(scores - jnp.max(scores, axis=-1, keepdims=True))
    return weights, jnp.sum(weights, axis=-1, keepdims=True)


def attend_kernel(
    scale, bq, q_ref, k_ref, v_ref, cq_ref, sq_ref, ck_ref, sk_ref, qg_ref, kg_ref, o_ref, k_rot
):
    @pl.when((pl.program_id(1) == 0) & (pl.program_id(2) == 0))
    def _():
        k_rot[...] = prepared(k_ref[...], kg_ref[...], ck_ref[...], sk_ref[...])[0]

    q = prepared(q_ref[...], qg_ref[...], cq_ref[...], sq_ref[...])[0]
    weights, total = soft_weights(scale, bq, q, k_rot[...])
    o_ref[...] = (dot(weights.astype(BF16), v_ref[...], NN) / total).astype(BF16)


def attend_back_kernel(
    scale,
    bq,
    q_ref,
    k_ref,
    v_ref,
    cq_ref,
    sq_ref,
    ck_ref,
    sk_ref,
    qg_ref,
    kg_ref,
    o_ref,
    do_ref,
    dq_ref,
    dk_ref,
    dv_ref,
    qp_ref,
    kp_ref,
    k_rot,
    dk_sum,
    dv_sum,
):
    head, member, block = pl.program_id(0), pl.program_id(1), pl.program_id(2)

    @pl.when((head == 0) & (member == 0) & (block == 0))
    def _():
        qp_ref[...] = jnp.zeros_like(qp_ref)
        kp_ref[...] = jnp.zeros_like(kp_ref)

    @pl.when((member == 0) & (block == 0))
    def _():
        k_rot[...] = prepared(k_ref[...], kg_ref[...], ck_ref[...], sk_ref[...])[0]
        dk_sum[...] = jnp.zeros_like(dk_sum)
        dv_sum[...] = jnp.zeros_like(dv_sum)

    q, plain, inverse = prepared(q_ref[...], qg_ref[...], cq_ref[...], sq_ref[...])
    k, do = k_rot[...], do_ref[...]
    weights, total = soft_weights(scale, bq, q, k)
    probs = weights / total
    delta = jnp.sum(do.astype(F32) * o_ref[...].astype(F32), axis=-1, keepdims=True)
    dscore = (probs * (dot(do, v_ref[...], NT) - delta)).astype(BF16)
    dk_sum[...] += dot(dscore, q, TN) * scale
    dv_sum[...] += dot(probs.astype(BF16), do, TN)
    grad = dot(dscore, k, NN) * scale
    grad = grad * cq_ref[...] - turn(grad) * sq_ref[...]
    qp_ref[...] += jnp.sum(grad * plain, axis=0, keepdims=True)
    dq_ref[...] = rms_backward(grad, plain, inverse, qg_ref[...]).astype(BF16)

    @pl.when((member == pl.num_programs(1) - 1) & (block == pl.num_programs(2) - 1))
    def _():
        _, k_plain, k_inverse = prepared(k_ref[...], kg_ref[...], ck_ref[...], sk_ref[...])
        grad_k = dk_sum[...]
        grad_k = grad_k * ck_ref[...] - turn(grad_k) * sk_ref[...]
        kp_ref[...] += jnp.sum(grad_k * k_plain, axis=0, keepdims=True)
        dk_ref[...] = rms_backward(grad_k, k_plain, k_inverse, kg_ref[...]).astype(BF16)
        dv_ref[...] = dv_sum[...].astype(BF16)


def attention(scale, group, query, keys, values, cosine, sine, query_gain, key_gain, *back):
    length, kv_width = keys.shape
    head_dim = cosine.shape[-1]
    kv_heads = kv_width // head_dim
    bq = min(length, 256)
    rows = pl.BlockSpec((bq, head_dim), lambda h, g, i: (i, h * group + g))
    keyed = pl.BlockSpec((length, head_dim), lambda h, g, i: (0, h))
    table_q = pl.BlockSpec((bq, head_dim), lambda h, g, i: (i, 0))
    table_k = pl.BlockSpec((length, head_dim), lambda h, g, i: (0, 0))
    flat = pl.BlockSpec((1, head_dim), lambda h, g, i: (0, 0))
    wide = jax.ShapeDtypeStruct((length, kv_width * group), BF16)
    narrow = jax.ShapeDtypeStruct((length, kv_width), BF16)
    part = jax.ShapeDtypeStruct((1, head_dim), F32)
    work = 2 * length * length * head_dim * kv_heads * group
    scratch = [pltpu.VMEM((length, head_dim), BF16)]
    if back:
        scratch += [pltpu.VMEM((length, head_dim), F32)] * 2
    return pl.pallas_call(
        functools.partial(attend_back_kernel if back else attend_kernel, scale, bq),
        grid=(kv_heads, group, length // bq),
        out_shape=(wide, narrow, narrow, part, part) if back else wide,
        in_specs=[rows, keyed, keyed, table_q, table_q, table_k, table_k, flat, flat]
        + [rows] * len(back),
        out_specs=(rows, keyed, keyed, flat, flat) if back else rows,
        scratch_shapes=scratch,
        name="attend_back" if back else "attend",
        cost_estimate=pl.CostEstimate(
            flops=work * (5 if back else 2), bytes_accessed=4 * length * 1024, transcendentals=0
        ),
        compiler_params=pltpu.CompilerParams(vmem_limit_bytes=40 * 2**20),
    )(
        query,
        keys,
        values,
        cosine,
        sine,
        cosine,
        sine,
        query_gain.reshape(1, -1),
        key_gain.reshape(1, -1),
        *back,
    )


def on_device(
    block_input,
    input_gain,
    query_weight,
    key_weight,
    value_weight,
    query_gain,
    key_gain,
    out_weight,
    post_gain,
    gate_weight,
    up_weight,
    down_weight,
    grad_output,
):
    local_rows, seq_local, width = block_input.shape
    assert seq_local == 1 and lax.axis_size("dp") == 2
    layers = input_gain.shape[0]
    head_dim = query_gain.shape[-1]
    heads = query_weight.shape[-1] // head_dim
    kv_heads = key_weight.shape[-1] // head_dim
    n_ctx, n_tp = lax.axis_size("ctx"), lax.axis_size("tp")
    block_rows = local_rows * n_tp
    length = block_rows * n_ctx
    scale = head_dim ** (-0.5)
    first_row = lax.axis_index("ctx") * block_rows
    cosine, sine = rope_tables(jnp.arange(length, dtype=F32), head_dim)
    piece = width // (2 * n_ctx)
    my_cols = (lax.axis_index("dp") * n_ctx + lax.axis_index("ctx")) * piece
    other_cols = ((1 - lax.axis_index("dp")) * n_ctx + lax.axis_index("ctx")) * piece
    swap = [(0, 1), (1, 0)]

    def mine(x):
        return lax.dynamic_slice_in_dim(x, first_row, block_rows, 0)

    def slices(x):
        parts = [lax.dynamic_slice_in_dim(x, at, piece, 1) for at in (my_cols, other_cols)]
        return jnp.concatenate(parts, axis=1)

    def settle(grad, axis):
        own, other = jnp.split(grad, 2, axis=axis)
        return own + lax.ppermute(other.astype(BF16), "dp", swap).astype(F32)

    def settle_rows(*products):
        other = [x[piece:].astype(BF16) for x in products]
        other = lax.ppermute(jnp.concatenate(other, axis=1), "dp", swap).astype(F32)
        out = []
        at = 0
        for x in products:
            out.append(x[:piece] + other[:, at : at + x.shape[1]])
            at += x.shape[1]
        return out

    hidden = block_input[:, 0]
    grad_hidden = grad_output[:, 0]
    grad_rows = lax.all_gather(grad_hidden.astype(BF16), ("ctx", "tp"), axis=0, tiled=True)
    (first_in,) = boundary("first", hidden, input_gain[0])
    kept = []
    for l in range(layers):
        query = dot(first_in, query_weight[l], NN)
        keys = dot(first_in, key_weight[l], NN)
        values = dot(first_in, value_weight[l], NN).astype(BF16)
        attend_args = (scale, heads // kv_heads, query, keys, values, cosine, sine)
        attend_args += (query_gain[l], key_gain[l])
        attended = attention(*attend_args)
        partial = dot(mine(attended), out_weight[l], NN).astype(BF16)
        mixed, second_in = boundary("fwd", hidden, post_gain[l], partial)
        gate = dot(second_in, gate_weight[l], NN)
        upward = dot(second_in, up_weight[l], NN)
        swish = (jax.nn.silu(gate) * upward).astype(BF16)
        partial = dot(mine(swish), down_weight[l], NN).astype(BF16)
        kept.append(
            (hidden, first_in, attend_args, attended, mixed, second_in, gate, upward, swish)
        )
        if l + 1 < layers:
            hidden, first_in = boundary("fwd", mixed, input_gain[l + 1], partial)
        else:
            hidden = mixed + lax.psum_scatter(
                partial, "tp", scatter_dimension=0, tiled=True
            ).astype(F32)

    grads = [None] * layers
    gains = [None] * layers
    for l in reversed(range(layers)):
        x_in, first_in, attend_args, attended, mixed, second_in, gate, upward, swish = kept[l]
        grad_swish = dot(grad_rows, down_weight[l], NT)
        sigma = jax.nn.sigmoid(gate)
        grad_gate = (grad_swish * upward * (sigma * (1.0 + gate * (1.0 - sigma)))).astype(BF16)
        grad_up = (grad_swish * (gate * sigma)).astype(BF16)
        partial = dot(mine(grad_gate), gate_weight[l], NT) + dot(mine(grad_up), up_weight[l], NT)
        grad_mixed, post_part, mixed_rows = boundary(
            "bwd", mixed, post_gain[l], partial.astype(BF16), grad_hidden
        )
        second_cols = slices(second_in)
        down_grad = settle(dot(swish, slices(grad_rows), TN), 1)
        gate_grad, up_grad = settle_rows(
            dot(second_cols, grad_gate, TN), dot(second_cols, grad_up, TN)
        )

        grad_heads = dot(mixed_rows, out_weight[l], NT).astype(BF16)
        out_grad = settle(dot(attended, slices(mixed_rows), TN), 1)
        query_bf, key_bf, value_bf, q_part, k_part = attention(*attend_args, attended, grad_heads)
        partial = (
            dot(mine(query_bf), query_weight[l], NT)
            + dot(mine(key_bf), key_weight[l], NT)
            + dot(mine(value_bf), value_weight[l], NT)
        ).astype(BF16)
        if l:
            grad_hidden, input_part, grad_rows = boundary(
                "bwd", x_in, input_gain[l], partial, grad_mixed
            )
        else:
            grad_hidden, input_part = boundary(
                "bwd_last", x_in, input_gain[l], partial, grad_mixed
            )
        first_cols = slices(first_in)
        query_grad, key_grad, value_grad = settle_rows(
            dot(first_cols, query_bf, TN),
            dot(first_cols, key_bf, TN),
            dot(first_cols, value_bf, TN),
        )
        grads[l] = (query_grad, key_grad, value_grad, out_grad, gate_grad, up_grad, down_grad)
        gains[l] = (input_part[0], q_part[0] / n_ctx, k_part[0] / n_ctx, post_part[0])
    stacked = [jnp.stack([part[m] for part in grads]) for m in range(7)]
    packed = jnp.concatenate([v for part in gains for v in part])
    sizes = [v.shape[0] for part in gains for v in part]
    padded = -(-packed.shape[0] // 1024) * 1024
    packed = jnp.pad(packed, (0, padded - packed.shape[0])).reshape(-1, 128)
    summed = sum_gains(packed).reshape(-1)
    pieces = []
    at = 0
    for size in sizes:
        pieces.append(summed[at : at + size])
        at += size
    gains = [jnp.stack([pieces[4 * l + m] for l in range(layers)]) for m in range(4)]
    return (
        hidden[:, None],
        grad_hidden[:, None],
        gains[0],
        stacked[0],
        stacked[1],
        stacked[2],
        gains[1],
        gains[2],
        stacked[3],
        gains[3],
        stacked[4],
        stacked[5],
        stacked[6],
    )


def rope_constants(length, head_dim):
    half = head_dim // 2
    frequency = np.float32(THETA) ** (-(np.float32(2.0) * np.arange(half, dtype=np.float32)) / np.float32(head_dim))
    angles = np.arange(length, dtype=np.float32)[:, None] * frequency.astype(np.float32)[None, :]
    cosine, sine = np.cos(angles), np.sin(angles)
    return (
        np.concatenate([cosine, cosine], axis=-1).astype(np.float32),
        np.concatenate([-sine, sine], axis=-1).astype(np.float32),
    )


def chunks(total, step=256):
    step = step if total % step == 0 else 128
    return [(at, step) for at in range(0, total, step)]


def fused_kernel(sz, *refs):
    (layers, n_ctx, n_tp, rows, width, heads, kv_heads, head_dim, ff) = sz
    block = rows * n_tp
    length = block * n_ctx
    group = heads // kv_heads
    q_w, k_w = heads * head_dim, kv_heads * head_dim
    piece = width // (2 * n_ctx)
    log2e = 1.4426950408889634
    scale = head_dim ** (-0.5)
    (x_ref, go_ref, ig_ref, pg_ref, qg_ref, kg_ref, cos_ref, sin_ref) = refs[:8]
    (wq_h, wk_h, wv_h, wo_h, wg_h, wu_h, wd_h) = refs[8:15]
    y_ref, gx_ref, gain_ref = refs[15:18]
    finals = refs[18:25]
    (wqkv, wo, wgu, wd, G, P, land, q_raw, k_raw, q_rot, k_rot, vals, att, swish, fa, fb, ggu, d_o, dqkv,
     dk_acc, dv_acc, mixed_s, xs_s, gm_s, gains, g_dp, g_ctx, g_tp,
     s_qkv, s_out, s_gu, s_dn, l_qkv, l_out, l_gu, l_dn,
     oq_ref, ok_ref, ov_ref, oo_ref, og_ref, ou_ref, od_ref, o_sem,
     w_sem, z_send, z_recv, t_send, t_recv, r_send, r_recv, d_send, d_recv, a_send, a_recv) = refs[25:]

    c, t, dp = lax.axis_index("ctx"), lax.axis_index("tp"), lax.axis_index("dp")
    tp_peers = [n_tp - 1 - t, t + 1 - 2 * lax.rem(t, 2), lax.rem(t + 2, n_tp)]
    ctx_peers = [lax.rem(c + d, n_ctx) for d in range(1, n_ctx)]
    other = 1 - dp
    pending = []

    loads = []

    def load(src, dst):
        copy = pltpu.make_async_copy(src, dst, w_sem.at[len(loads)])
        copy.start()
        loads.append(copy)

    for l in range(layers):
        load(wk_h.at[l], wqkv.at[l, :, pl.ds(q_w, k_w)])
        load(wv_h.at[l], wqkv.at[l, :, pl.ds(q_w + k_w, k_w)])
        load(wq_h.at[l], wqkv.at[l, :, pl.ds(0, q_w)])
        load(wo_h.at[l], wo.at[l])
        load(wg_h.at[l], wgu.at[l, :, pl.ds(0, ff)])
        load(wu_h.at[l], wgu.at[l, :, pl.ds(ff, ff)])
        load(wd_h.at[l], wd.at[l])

    barrier = pltpu.get_barrier_semaphore()
    for peer in tp_peers:
        pl.semaphore_signal(barrier, inc=1, device_id={"tp": peer}, device_id_type=MESH)
    for peer in ctx_peers:
        pl.semaphore_signal(barrier, inc=1, device_id={"ctx": peer}, device_id_type=MESH)
    pl.semaphore_signal(barrier, inc=1, device_id={"dp": other}, device_id_type=MESH)
    pl.semaphore_wait(barrier, n_tp + n_ctx - 1)

    def push(copy):
        copy.start()
        pending.append(copy)

    near = [1, n_ctx - 1] + list(range(2, n_ctx - 1))

    def source_of(d):
        return lax.rem(c + n_ctx - d, n_ctx)

    def spread(g, d):
        slot = G.at[g, source_of(d), t]
        for k, peer in enumerate(tp_peers):
            push(remote(slot, slot, t_send.at[g, d, k], t_recv.at[g, d, k], tp=peer))

    def complete(g, d):
        for k in range(n_tp - 1):
            origin = tp_peers[k]
            slot = G.at[g, source_of(d), origin]
            remote(slot, slot, t_send.at[g, d, k], t_recv.at[g, d, k], tp=origin).wait_recv()

    def start_gather(g, value, planes=False):
        own = G.at[g, c, t]
        G[g, c, t] = value
        mlp = layers <= g < 3 * layers
        if mlp:
            spread(g, 0)
        if not planes:
            for d in near:
                push(remote(own, own, z_send.at[g, d - 1], z_recv.at[g, d - 1], ctx=ctx_peers[d - 1]))
        if not mlp:
            spread(g, 0)

    def plane_send(g, *steps):
        own = G.at[g, c]
        for d in steps:
            push(remote(own, own, z_send.at[g, d - 1], z_recv.at[g, d - 1], ctx=ctx_peers[d - 1]))

    def plane_complete(g):
        for d in range(1, n_ctx):
            slot = G.at[g, source_of(d)]
            remote(slot, slot, z_send.at[g, d - 1], z_recv.at[g, d - 1], ctx=source_of(d)).wait_recv()

    def late_spread(g, *steps):
        for d in steps:
            source = source_of(d)
            slot = G.at[g, source, t]
            remote(slot, slot, z_send.at[g, d - 1], z_recv.at[g, d - 1], ctx=source).wait_recv()
            spread(g, d)

    def full_gather(g, work, early=None):
        if early is not None:
            early()
        late_spread(g, near[0], near[1])
        complete(g, 0)
        work(c)
        late_spread(g, *near[2:])
        for d in near:
            complete(g, d)
            work(source_of(d))

    def late_complete(g):
        for d in range(1, n_ctx):
            complete(g, d)

    wide = 512 if width % 512 == 0 else width

    def sum_part(r, k, at, peer):
        lanes = pl.ds(at, wide)
        src, dst = P.at[r, peer, :, lanes], land.at[r, k, :, lanes]
        return remote(src, dst, r_send.at[r, k, at // wide], r_recv.at[r, k, at // wide], tp=peer)

    def start_sum(r, value_of):
        for at in range(0, width, wide):
            P[r, :, :, at : at + wide] = value_of(at, at + wide).astype(BF16).reshape(n_tp, rows, wide)
            for k, peer in enumerate(tp_peers):
                push(sum_part(r, k, at, peer))

    def finish_sum(r):
        for at in range(0, width, wide):
            for k, peer in enumerate(tp_peers):
                sum_part(r, k, at, peer).wait_recv()
        total = P[r, t].astype(F32)
        for k in range(n_tp - 1):
            total = total + land[r, k].astype(F32)
        return total

    def others(body):
        def step(d, carry):
            body(d, lax.rem(c + n_ctx - d, n_ctx))
            return carry

        lax.fori_loop(1, n_ctx, step, 0)

    def tokens(g, s):
        return G[g, s].reshape(block, width)

    def qkv(l, s):
        x = tokens(l, s)
        cosine = cos_ref[pl.ds(pl.multiple_of(s * block, block), block), :]
        sine = sin_ref[pl.ds(pl.multiple_of(s * block, block), block), :]
        qg, kg = qg_ref[l : l + 1, :], kg_ref[l : l + 1, :]
        for at, step in chunks(q_w + 2 * k_w):
            y = dot(x, wqkv[l, :, at : at + step], NN)
            for sub in range(0, step, head_dim):
                yh = y[:, sub : sub + head_dim]
                h = (at + sub) // head_dim
                if h < heads:
                    q_raw[l, h, s] = yh
                    q_rot[l, h, s] = prepared(yh, qg, cosine, sine)[0]
                elif h < heads + kv_heads:
                    k_raw[l, h - heads, s] = yh
                    k_rot[l, h - heads, s] = prepared(yh, kg, cosine, sine)[0]
                else:
                    vals[l, h - heads - kv_heads, s] = yh.astype(BF16)

    def attend_block(l, i):
        at_row = i * block + lax.broadcasted_iota(jnp.int32, (block, length), 0)
        allowed = lax.broadcasted_iota(jnp.int32, (block, length), 1) <= at_row
        for h in range(heads):
            k = k_rot[l, h // group].reshape(length, head_dim)
            v = vals[l, h // group].reshape(length, head_dim)
            scores = dot(q_rot[l, h, i], k, NT) * (scale * log2e)
            weights = jnp.where(allowed, jnp.exp2(scores), 0.0)
            total = jnp.sum(weights, axis=-1, keepdims=True)
            out = dot(weights.astype(BF16), v, NN) / total
            att[l, i, :, h * head_dim : (h + 1) * head_dim] = out.astype(BF16)

    def out_partial(l):
        a = att[l, c]
        start_sum(l, lambda lo, hi: dot(a, wo[l, :, lo:hi], NN))

    def mlp_forward(l, s):
        x = tokens(layers + l, s)
        for at, step in chunks(ff):
            gate = dot(x, wgu[l, :, at : at + step], NN)
            up = dot(x, wgu[l, :, ff + at : ff + at + step], NN)
            sigma = jax.nn.sigmoid(gate)
            silu = gate * sigma
            swish[l, s, :, at : at + step] = (silu * up).astype(BF16)
            fa[l, s, :, at : at + step] = (up * (sigma * (1.0 + gate * (1.0 - sigma)))).astype(BF16)
            fb[l, s, :, at : at + step] = silu.astype(BF16)

    def down_partial(l):
        a = swish[l, c]
        start_sum(layers + l, lambda lo, hi: dot(a, wd[l, :, lo:hi], NN))

    def mlp_backward(l, s):
        x = tokens(2 * layers + l, s)
        for at, step in chunks(ff):
            grad = dot(x, wd[l, at : at + step, :], NT)
            ggu[l, s, :, at : at + step] = (grad * fa[l, s, :, at : at + step].astype(F32)).astype(BF16)
            ggu[l, s, :, ff + at : ff + at + step] = (
                grad * fb[l, s, :, at : at + step].astype(F32)
            ).astype(BF16)

    def mlp_back_partial(l):
        a = ggu[l, c]
        start_sum(2 * layers + l, lambda lo, hi: dot(a, wgu[l, lo:hi, :], NT))

    def heads_back(l, s):
        x = tokens(3 * layers + l, s)
        for at, step in chunks(q_w):
            d_o[s, :, at : at + step] = dot(x, wo[l, at : at + step, :], NT).astype(BF16)

    def attend_backward(l):
        dk_acc[...] = jnp.zeros_like(dk_acc)
        dv_acc[...] = jnp.zeros_like(dv_acc)
        half = length // 2
        per = n_ctx // 2
        causal = lax.broadcasted_iota(jnp.int32, (half, half), 1) <= lax.broadcasted_iota(
            jnp.int32, (half, half), 0
        )
        qg, kg = qg_ref[l : l + 1, :], kg_ref[l : l + 1, :]

        def one_head(h, part):
            lanes = pl.ds(pl.multiple_of(h * head_dim, head_dim), head_dim)
            kv = h // group
            for i in range(2):
                span = slice(i * per, (i + 1) * per)
                extent = (i + 1) * half
                q = q_rot[l, h, span].reshape(half, head_dim)
                do = d_o[span, :, lanes].reshape(half, head_dim)
                a = att[l, span, :, lanes].reshape(half, head_dim)
                k = k_rot[l, kv, : (i + 1) * per].reshape(extent, head_dim)
                v = vals[l, kv, : (i + 1) * per].reshape(extent, head_dim)
                weights = jnp.exp2(dot(q, k, NT) * (scale * log2e))
                last = jnp.where(causal, weights[:, i * half :], 0.0)
                weights = jnp.concatenate([weights[:, :half], last], axis=1) if i else last
                probs = weights / jnp.sum(weights, axis=-1, keepdims=True)
                delta = jnp.sum(do.astype(F32) * a.astype(F32), axis=-1, keepdims=True)
                dscore = (probs * (dot(do, v, NT) - delta)).astype(BF16)
                dk_acc[kv, :extent] += dot(dscore, q, TN)
                dv_acc[kv, :extent] += dot(probs.astype(BF16), do, TN)
                cosine = cos_ref[i * half : (i + 1) * half, :]
                sine = sin_ref[i * half : (i + 1) * half, :]
                grad = dot(dscore, k, NN) * scale
                grad = grad * cosine - turn(grad) * sine
                _, plain, inverse = rms_forward(q_raw[l, h, span].reshape(half, head_dim), qg)
                part = part + jnp.sum(grad * plain, axis=0, keepdims=True)
                grad = rms_backward(grad, plain, inverse, qg).astype(BF16)
                dqkv[span, :, lanes] = grad.reshape(per, block, head_dim)
            return part

        q_part = lax.fori_loop(0, heads, one_head, jnp.zeros((1, head_dim), F32))
        k_part = jnp.zeros((1, head_dim), F32)
        for kv in range(kv_heads):
            grad = dk_acc[kv] * scale
            grad = grad * cos_ref[...] - turn(grad) * sin_ref[...]
            _, plain, inverse = rms_forward(k_raw[l, kv].reshape(length, head_dim), kg)
            k_part = k_part + jnp.sum(grad * plain, axis=0, keepdims=True)
            grad = rms_backward(grad, plain, inverse, kg).astype(BF16)
            at = q_w + kv * head_dim
            dqkv[:, :, at : at + head_dim] = grad.reshape(n_ctx, block, head_dim)
            at += k_w
            dqkv[:, :, at : at + head_dim] = dv_acc[kv].astype(BF16).reshape(n_ctx, block, head_dim)
        at = 2 * layers
        gains[at : at + 1, 2 * l * head_dim : (2 * l + 1) * head_dim] = q_part / n_ctx
        gains[at : at + 1, (2 * l + 1) * head_dim : (2 * l + 2) * head_dim] = k_part / n_ctx

    def qkv_back_partial(l):
        a = dqkv[c]
        start_sum(3 * layers + l, lambda lo, hi: dot(a, wqkv[l, lo:hi, :], NT))

    my_cols = pl.ds(pl.multiple_of((dp * n_ctx + c) * piece, piece), piece)
    other_cols = pl.ds(pl.multiple_of((other * n_ctx + c) * piece, piece), piece)

    def columns(g):
        parts = [G[g, :, :, :, cols].reshape(length, piece) for cols in (my_cols, other_cols)]
        return jnp.concatenate(parts, axis=1)

    def exchange(i, src, dst):
        push(remote(src, dst, d_send.at[i], d_recv.at[i], dp=other))

    def grads_mlp(l):
        x = columns(layers + l)
        for at, step in chunks(2 * ff):
            g = dot(x, ggu[l, :, :, at : at + step].reshape(length, step), TN)
            ref, base = (og_ref, at) if at < ff else (ou_ref, at - ff)
            ref[l, :, base : base + step] = g[:piece]
            s_gu[l, :, at : at + step] = g[piece:].astype(BF16)
        exchange(4 * l, s_gu.at[l], l_gu.at[l])
        x = columns(2 * layers + l)
        for at, step in chunks(ff):
            g = dot(swish[l, :, :, at : at + step].reshape(length, step), x, TN)
            od_ref[l, at : at + step, :] = g[:, :piece]
            s_dn[l, at : at + step, :] = g[:, piece:].astype(BF16)
        exchange(4 * l + 1, s_dn.at[l], l_dn.at[l])

    def grads_out(l):
        x = columns(3 * layers + l)
        for at, step in chunks(q_w):
            g = dot(att[l, :, :, at : at + step].reshape(length, step), x, TN)
            oo_ref[l, at : at + step, :] = g[:, :piece]
            s_out[l, at : at + step, :] = g[:, piece:].astype(BF16)
        exchange(4 * l + 2, s_out.at[l], l_out.at[l])

    def grads_qkv(l):
        x = columns(l)
        for at, step in chunks(q_w + 2 * k_w):
            g = dot(x, dqkv[:, :, at : at + step].reshape(length, step), TN)
            if at < q_w:
                oq_ref[l, :, at : at + step] = g[:piece]
            elif at < q_w + k_w:
                ok_ref[l, :, at - q_w : at - q_w + step] = g[:piece]
            else:
                ov_ref[l, :, at - q_w - k_w : at - q_w - k_w + step] = g[:piece]
            s_qkv[l, :, at : at + step] = g[piece:].astype(BF16)
        exchange(4 * l + 3, s_qkv.at[l], l_qkv.at[l])

    def settle(l):
        def landed(i, dst):
            remote(dst, dst, d_send.at[i], d_recv.at[i], dp=other).wait_recv()

        landed(4 * l, l_gu.at[l])
        og_ref[l] += l_gu[l, :, :ff].astype(F32)
        ou_ref[l] += l_gu[l, :, ff:].astype(F32)
        landed(4 * l + 1, l_dn.at[l])
        od_ref[l] += l_dn[l].astype(F32)
        landed(4 * l + 2, l_out.at[l])
        oo_ref[l] += l_out[l].astype(F32)
        landed(4 * l + 3, l_qkv.at[l])
        oq_ref[l] += l_qkv[l, :, :q_w].astype(F32)
        ok_ref[l] += l_qkv[l, :, q_w : q_w + k_w].astype(F32)
        ov_ref[l] += l_qkv[l, :, q_w + k_w :].astype(F32)

    gains[...] = jnp.zeros_like(gains)

    leaving = []

    def deliver(l):
        staged = (oq_ref, ok_ref, ov_ref, oo_ref, og_ref, ou_ref, od_ref)
        for i, (src, dst) in enumerate(zip(staged, finals)):
            copy = pltpu.make_async_copy(src.at[l], dst.at[l], o_sem.at[i, l])
            copy.start()
            leaving.append(copy)

    stages = (("dp", dp, [other], g_dp, 0), ("ctx", c, ctx_peers, g_ctx, 1), ("tp", t, [lax.rem(t + k, n_tp) for k in range(1, n_tp)], g_tp, n_ctx))

    def gain_start(stage, value):
        axis, me, peers, buf, base = stages[stage]
        buf[me] = value
        for i, peer in enumerate(peers):
            own = buf.at[me]
            push(remote(own, own, a_send.at[base + i], a_recv.at[base + i], **{axis: peer}))

    def gain_finish(stage):
        axis, me, peers, buf, base = stages[stage]
        n = len(peers) + 1
        for i in range(n - 1):
            source = lax.rem(me + n - (i + 1), n)
            slot = buf.at[source]
            remote(slot, slot, a_send.at[base + i], a_recv.at[base + i], **{axis: source}).wait_recv()
        value = buf[0]
        for i in range(1, n):
            value = value + buf[i]
        return value

    top = layers - 1
    X1, X2, GR, MR = (lambda l: l), (lambda l: layers + l), (lambda l: 2 * layers + l), (lambda l: 3 * layers + l)

    x_in = x_ref[:, 0, :]
    xs_s[0] = x_in
    start_gather(X1(0), rms_forward(x_in, ig_ref[0:1, :])[0].astype(BF16))
    for l in range(layers):
        for i in range(3):
            loads[7 * l + i].wait()
        full_gather(X1(l), lambda s: qkv(l, s))
        if l == 0:
            start_gather(GR(top), go_ref[:, 0, :].astype(BF16), True)
        else:
            plane_send(GR(top), 2)
        attend_block(l, c)
        loads[7 * l + 3].wait()
        out_partial(l)
        attend_block(l, source_of(1))
        if l == 0:
            complete(GR(top), 0)
            plane_send(GR(top), 1, 3)
        attend_block(l, source_of(2))
        mixed = xs_s[l] + finish_sum(l)
        mixed_s[l] = mixed
        start_gather(X2(l), rms_forward(mixed, pg_ref[l : l + 1, :])[0].astype(BF16), l < top)
        for i in range(4, 7):
            loads[7 * l + i].wait()
        attend_block(l, source_of(3))
        complete(X2(l), 0)
        mlp_forward(l, c)
        if l < top:
            down_partial(l)
            x_next = mixed_s[l] + finish_sum(layers + l)
            xs_s[l + 1] = x_next
            start_gather(X1(l + 1), rms_forward(x_next, ig_ref[l + 1 : l + 2, :])[0].astype(BF16))

    for l in reversed(range(layers)):
        if l < top:
            complete(GR(l), 0)
        mlp_backward(l, c)
        mlp_back_partial(l)
        if l == top:
            down_partial(l)
            plane_complete(GR(top))
        else:
            others(lambda d, s: mlp_backward(l + 1, s))
        grad_res = go_ref[:, 0, :] if l == top else gm_s[1]
        _, normed, inverse = rms_forward(mixed_s[l], pg_ref[l : l + 1, :])
        total = finish_sum(2 * layers + l)
        gains[layers + l : layers + l + 1, :] = jnp.sum(total * normed, axis=0, keepdims=True)
        grad_mixed = grad_res + rms_backward(total, normed, inverse, pg_ref[l : l + 1, :])
        gm_s[0] = grad_mixed
        start_gather(MR(l), grad_mixed.astype(BF16))
        if l == top:
            y_ref[...] = mixed_s[l] + finish_sum(layers + l)

        def early():
            if l < top:
                grads_mlp(l + 1)
                plane_complete(X2(l))
                others(lambda d, s: mlp_forward(l, s))

        full_gather(MR(l), lambda s: heads_back(l, s), early)
        if l == top:
            late_spread(X2(l), 1, 3)
        else:
            late_spread(GR(l), 1, 2, 3)
        if l:
            plane_send(X2(l - 1), 1, 3)
        attend_backward(l)
        qkv_back_partial(l)
        if l == top:
            late_spread(X2(l), 2)
        if l == 0:
            plain = tokens(X1(l), c).astype(F32)
            back = P[3 * layers + l].reshape(block, width).astype(F32)
            gains[l : l + 1, :] = jnp.sum(back * plain, axis=0, keepdims=True) / ig_ref[l : l + 1, :]
            gain_start(0, gains[...])
        else:
            plane_send(X2(l - 1), 2)
        grads_out(l)
        if l == 0:
            gain_start(1, gain_finish(0))
        grads_qkv(l)
        if l:
            _, normed, inverse = rms_forward(xs_s[l], ig_ref[l : l + 1, :])
            total = finish_sum(3 * layers + l)
            gains[l : l + 1, :] = jnp.sum(total * normed, axis=0, keepdims=True)
            grad_x = gm_s[0] + rms_backward(total, normed, inverse, ig_ref[l : l + 1, :])
            gm_s[1] = grad_x
            start_gather(GR(l - 1), grad_x.astype(BF16))
            late_complete(X2(l))
            others(lambda d, s: mlp_forward(l, s))
        if l == 0:
            late_complete(GR(l))
            others(lambda d, s: mlp_backward(l, s))
            gain_start(2, gain_finish(1))
            grads_mlp(l)
            settle(l + 1)
            deliver(l + 1)
            _, normed, inverse = rms_forward(xs_s[l], ig_ref[l : l + 1, :])
            total = finish_sum(3 * layers + l)
            gx_ref[...] = gm_s[0] + rms_backward(total, normed, inverse, ig_ref[l : l + 1, :])
            settle(l)
            deliver(l)
            gain_ref[...] = gain_finish(2)

    for copy in leaving:
        copy.wait()
    for copy in pending:
        copy.wait_send()


def fused(sz, *operands):
    (layers, n_ctx, n_tp, rows, width, heads, kv_heads, head_dim, ff) = sz
    block = rows * n_tp
    length = block * n_ctx
    q_w, k_w = heads * head_dim, kv_heads * head_dim
    piece = width // (2 * n_ctx)
    vm = lambda *shape: pltpu.VMEM(shape, BF16)
    vf = lambda *shape: pltpu.VMEM(shape, F32)
    dma = pltpu.SemaphoreType.DMA
    sd = lambda *shape: jax.ShapeDtypeStruct(shape, F32)
    n_g = 4 * layers
    scratch = [
        vm(layers, width, q_w + 2 * k_w),
        vm(layers, q_w, width),
        vm(layers, width, 2 * ff),
        vm(layers, ff, width),
        vm(n_g, n_ctx, n_tp, rows, width),
        vm(n_g, n_tp, rows, width),
        vm(n_g, n_tp - 1, rows, width),
        vf(layers, heads, n_ctx, block, head_dim),
        vf(layers, kv_heads, n_ctx, block, head_dim),
        vm(layers, heads, n_ctx, block, head_dim),
        vm(layers, kv_heads, n_ctx, block, head_dim),
        vm(layers, kv_heads, n_ctx, block, head_dim),
        vm(layers, n_ctx, block, q_w),
        vm(layers, n_ctx, block, ff),
        vm(layers, n_ctx, block, ff),
        vm(layers, n_ctx, block, ff),
        vm(layers, n_ctx, block, 2 * ff),
        vm(n_ctx, block, q_w),
        vm(n_ctx, block, q_w + 2 * k_w),
        vf(kv_heads, length, head_dim),
        vf(kv_heads, length, head_dim),
        vf(layers, rows, width),
        vf(layers, rows, width),
        vf(2, rows, width),
        vf(8, width),
        vf(2, 8, width),
        vf(n_ctx, 8, width),
        vf(n_tp, 8, width),
    ]
    outs = [
        sd(layers, piece, q_w),
        sd(layers, piece, k_w),
        sd(layers, piece, k_w),
        sd(layers, q_w, piece),
        sd(layers, piece, ff),
        sd(layers, piece, ff),
        sd(layers, ff, piece),
    ]
    for _ in range(2):
        scratch += [
            vm(layers, piece, q_w + 2 * k_w),
            vm(layers, q_w, piece),
            vm(layers, piece, 2 * ff),
            vm(layers, ff, piece),
        ]
    scratch += [pltpu.VMEM(out.shape, F32) for out in outs]
    scratch += [
        dma((7, layers)),
        dma((7 * layers,)),
        dma((n_g, n_ctx - 1)),
        dma((n_g, n_ctx - 1)),
        dma((n_g, n_ctx, n_tp - 1)),
        dma((n_g, n_ctx, n_tp - 1)),
        dma((n_g, n_tp - 1, 2)),
        dma((n_g, n_tp - 1, 2)),
        dma((4 * layers,)),
        dma((4 * layers,)),
        dma((n_ctx + n_tp - 1,)),
        dma((n_ctx + n_tp - 1,)),
    ]
    vmem = pl.BlockSpec(memory_space=pltpu.VMEM)
    hbm = pl.BlockSpec(memory_space=pl.ANY)
    return pl.pallas_call(
        functools.partial(fused_kernel, sz),
        out_shape=[
            sd(rows, width),
            sd(rows, width),
            sd(8, width),
        ]
        + outs,
        in_specs=[vmem] * 8 + [hbm] * 7,
        out_specs=[vmem] * 3 + [hbm] * 7,
        scratch_shapes=scratch,
        name="two_layers",
        compiler_params=pltpu.CompilerParams(
            collective_id=6, has_side_effects=True, vmem_limit_bytes=60 * 2**20
        ),
    )(*operands)


def finish_kernel(layers, head_dim, *refs):
    y_in, gx_in, gain_in = refs[:3]
    grads_in = refs[3:10]
    y, gx, input_gain, query_gain, key_gain, post_gain = refs[10:16]
    grads_out = refs[16:23]
    held = refs[23:30]
    sems_in, sems_out = refs[30:]
    arrive, leave = [], []
    for l in reversed(range(layers)):
        for i, (src, mid, dst) in enumerate(zip(grads_in, held, grads_out)):
            arrive.append(pltpu.make_async_copy(src.at[l], mid.at[l], sems_in.at[i, l]))
            leave.append(pltpu.make_async_copy(mid.at[l], dst.at[l], sems_out.at[i, l]))
    for copy in arrive:
        copy.start()
    for first, second in zip(arrive, leave):
        first.wait()
        second.start()
    y[:, 0, :] = y_in[...]
    gx[:, 0, :] = gx_in[...]
    input_gain[...] = gain_in[:layers, :]
    post_gain[...] = gain_in[layers : 2 * layers, :]
    for l in range(layers):
        at = 2 * l * head_dim
        query_gain[l : l + 1, :] = gain_in[2 * layers : 2 * layers + 1, at : at + head_dim]
        key_gain[l : l + 1, :] = gain_in[2 * layers : 2 * layers + 1, at + head_dim : at + 2 * head_dim]
    for copy in leave:
        copy.wait()


def finish(layers, head_dim, y, gx, gains, *grads):
    rows, width = y.shape
    sd = lambda *shape: jax.ShapeDtypeStruct(shape, F32)
    vmem = pl.BlockSpec(memory_space=pltpu.VMEM)
    hbm = pl.BlockSpec(memory_space=pl.ANY)
    return pl.pallas_call(
        functools.partial(finish_kernel, layers, head_dim),
        out_shape=[
            sd(rows, 1, width),
            sd(rows, 1, width),
            sd(layers, width),
            sd(layers, head_dim),
            sd(layers, head_dim),
            sd(layers, width),
        ]
        + [sd(*grad.shape) for grad in grads],
        in_specs=[vmem] * 3 + [hbm] * len(grads),
        out_specs=[vmem] * 6 + [hbm] * len(grads),
        scratch_shapes=[pltpu.VMEM(grad.shape, F32) for grad in grads]
        + [pltpu.SemaphoreType.DMA((len(grads), layers))] * 2,
        name="finish",
    )(y, gx, gains, *grads)


def on_device_fused(
    block_input,
    input_gain,
    query_weight,
    key_weight,
    value_weight,
    query_gain,
    key_gain,
    out_weight,
    post_gain,
    gate_weight,
    up_weight,
    down_weight,
    grad_output,
):
    rows, _, width = block_input.shape
    layers = input_gain.shape[0]
    head_dim = query_gain.shape[-1]
    n_ctx, n_tp = lax.axis_size("ctx"), lax.axis_size("tp")
    sz = (
        layers,
        n_ctx,
        n_tp,
        rows,
        width,
        query_weight.shape[-1] // head_dim,
        key_weight.shape[-1] // head_dim,
        head_dim,
        gate_weight.shape[-1],
    )
    cosine, sine = rope_constants(rows * n_tp * n_ctx, head_dim)
    y, gx, gains, *grads = fused(
        sz,
        block_input,
        grad_output,
        input_gain,
        post_gain,
        query_gain,
        key_gain,
        cosine,
        sine,
        query_weight,
        key_weight,
        value_weight,
        out_weight,
        gate_weight,
        up_weight,
        down_weight,
    )
    y, gx, input_part, q_part, k_part, post_part, wq, wk, wv, wo, wg, wu, wd = finish(
        layers, head_dim, y, gx, gains, *grads
    )
    return (y, gx, input_part, wq, wk, wv, q_part, k_part, wo, post_part, wg, wu, wd)


def on_any_device(*arrays):
    rows, _, width = arrays[0].shape
    n_ctx, n_tp = lax.axis_size("ctx"), lax.axis_size("tp")
    small = n_tp == 4 and n_ctx == 4 and arrays[1].shape[0] == 2 and rows * n_tp * n_ctx <= 512 and (width // (2 * n_ctx)) % 128 == 0
    return (on_device_fused if small else on_device)(*arrays)


def solution(mesh):
    placed = (
        P(("ctx", "tp"), "dp", None),
        P(),
        P(None, None, "tp"),
        P(None, None, "tp"),
        P(None, None, "tp"),
        P(),
        P(),
        P(None, "tp", None),
        P(),
        P(None, None, "tp"),
        P(None, None, "tp"),
        P(None, "tp", None),
        P(("ctx", "tp"), "dp", None),
    )
    return jax.shard_map(
        on_any_device,
        mesh=mesh,
        in_specs=placed,
        out_specs=(
            P(("ctx", "tp"), "dp", None),
            P(("ctx", "tp"), "dp", None),
            P(),
            P(None, ("dp", "ctx"), "tp"),
            P(None, ("dp", "ctx"), "tp"),
            P(None, ("dp", "ctx"), "tp"),
            P(),
            P(),
            P(None, "tp", ("dp", "ctx")),
            P(),
            P(None, ("dp", "ctx"), "tp"),
            P(None, ("dp", "ctx"), "tp"),
            P(None, "tp", ("dp", "ctx")),
        ),
        check_vma=False,
    )
```
